128 devices in a mesh: row: 8 (over x, core), col: 16 (over y, z).
Axes of the slice: x: 4, y: 4, z: 4, core: 2. Of those that a mesh axis runs over, the one named last changes fastest.
Arguments:
- left_factor: bfloat16 [4, 2048, 24, 4096], P(None, 'row', None, 'col'), may hold values from -0.01953125 to 0.01953125
- prev_solution: bfloat16 [24, 4096, 512], P('row', 'col'), may hold values from -6 to 6
- cross: bfloat16 [4, 2048, 512], P(None, 'row'), may hold values from -6 to 6
- inverses: bfloat16 [2, 2, 2048, 1, 4096], P(None, None, 'row', None, 'col'), as said below
- coupling: bfloat16 [2, 2048, 1, 4096], P(None, 'row', None, 'col'), may hold values from -0.09375 to 0.09375
- prior_cov: float32 [512, 512], P('col'), may hold values from -6 to 6
Outputs:
- solved: bfloat16 [4, 2048, 512], P(None, 'row')
- pred_cov: float32 [512, 512], P('col')
The draws below stay inside these ranges and needn't reach their ends.
Inputs may be any that keep to these rules, and one draw needn't show every extreme that they name: Each block of inverses is lower triangular in natural order, with diagonal entries from 0.5 to 1.5.
All inputs are finite; a program needn't handle non-finite values.
Results may differ from the reference program's by a relative error of at most 0.0056.
Values may be sent and summed in bfloat16 or wider, within the bound.
No kernel may reach another device: no remote copies, remote signals or barrier semaphores. Data moves between devices by JAX's collectives and lax.ppermute only.
A program may use at most 64 MiB of HBM per device.

```python
import jax
import jax.numpy as jnp

TB = 256
S = 8192
P_SIZE = 98304
M = 512
PANEL = 4096
N_ROW = 8
N_COL = 16


def draw_inverses(key, part):
    key_off = jax.random.fold_in(key, 11)
    key_diag = jax.random.fold_in(key, 12)
    rows = jnp.arange(PANEL)[:, None]
    cols = jnp.arange(PANEL)[None, :]
    lower = (cols < rows).astype(jnp.float32)
    eye = (cols == rows).astype(jnp.float32)
    off_part = jax.random.normal(key_off, (2, PANEL, PANEL), jnp.float32) * (0.6 / PANEL ** 0.5)
    diag_part = jax.random.uniform(key_diag, (2, PANEL, 1), jnp.float32, 0.6, 1.4)
    whole = off_part * lower + diag_part * eye
    return whole.reshape(2, PANEL // (N_ROW * TB), N_ROW * TB, PANEL // (N_COL * TB), N_COL * TB).astype(jnp.bfloat16)


def block_scale(stream_key, extent, cuts, least, largest):
    factor_of, own = 1.0, jax.random.fold_in(stream_key, 6)
    for position, parts in cuts:
        draws = jnp.exp(jax.random.uniform(jax.random.fold_in(own, position), (parts,), jnp.float32, least / len(cuts), largest / len(cuts)))
        factor_of = factor_of * jnp.repeat(draws, extent[position] // parts).reshape([-1 if axis == position else 1 for axis in range(len(extent))])
    return factor_of


def centred(stream_key, extent, spread, limit, pieces=(), held_as=jnp.bfloat16):
    array = spread * jax.random.normal(stream_key, extent, jnp.float32)
    if pieces:
        array = array * block_scale(stream_key, extent, pieces, -0.22, 0.18)
    return jnp.clip(array, -limit, limit).astype(held_as)


def setup_inputs(seed: int = 0) -> dict:
    key_of = jax.random.split(jax.random.key(seed), 7)
    left_factor = centred(key_of[0], (S // (N_ROW * TB), N_ROW * TB, P_SIZE // (N_COL * TB), N_COL * TB), P_SIZE ** -0.5, 0.01953125, ((1, 8), (3, 16)))
    prev_solution = centred(key_of[1], (P_SIZE // (N_COL * TB), N_COL * TB, M), 1.0, 6.0, ((0, 8), (1, 16)))
    cross = centred(key_of[2], (S // (N_ROW * TB), N_ROW * TB, M), 1.0, 6.0, ((1, 8),))
    inverses = draw_inverses(jax.random.fold_in(key_of[6], 71), 0)
    coupling = centred(key_of[4], (PANEL // (N_ROW * TB), N_ROW * TB, PANEL // (N_COL * TB), N_COL * TB), PANEL ** -0.5, 0.09375, ((1, 8), (3, 16)))
    prior_cov = centred(key_of[5], (M, M), 1.0, 6.0, ((0, 16),), jnp.float32)
    return dict(left_factor=left_factor, prev_solution=prev_solution, cross=cross, inverses=inverses, coupling=coupling, prior_cov=prior_cov)


def reference(left_factor, prev_solution, cross, inverses, coupling, prior_cov):
    left_whole = left_factor.reshape(S, P_SIZE)
    prev_whole = prev_solution.reshape(P_SIZE, M)
    cross_whole = cross.reshape(S, M).astype(jnp.float32)
    first_inv = inverses[0].reshape(PANEL, PANEL)
    second_inv = inverses[1].reshape(PANEL, PANEL)
    coupled = coupling.reshape(PANEL, PANEL)
    pre = jnp.dot(left_whole, prev_whole, preferred_element_type=jnp.float32)
    first_rhs = (cross_whole[:PANEL] - pre[:PANEL]).astype(jnp.bfloat16)
    solved_first = jnp.dot(first_inv, first_rhs, preferred_element_type=jnp.float32).astype(jnp.bfloat16)
    linked = jnp.dot(coupled, solved_first, preferred_element_type=jnp.float32)
    second_rhs = (cross_whole[PANEL:] - pre[PANEL:] - linked).astype(jnp.bfloat16)
    solved_second = jnp.dot(second_inv, second_rhs, preferred_element_type=jnp.float32).astype(jnp.bfloat16)
    solved_all = jnp.concatenate([solved_first, solved_second], axis=0)
    outer = jnp.dot(solved_all.T, solved_all, preferred_element_type=jnp.float32)
    pred_cov = prior_cov - outer / S
    return solved_all.reshape(S // (N_ROW * TB), N_ROW * TB, M), pred_cov
```

```python
import jax
import jax.numpy as jnp
from jax import lax
from jax.experimental import pallas as pl
from jax.experimental.pallas import tpu as pltpu
from jax.sharding import PartitionSpec as P

S = 8192
BF = jnp.bfloat16
F32 = jnp.float32
VMEM = pltpu.VMEM
NT = (((1,), (1,)), ((), ()))


def x_shift(v, step):
    return lax.ppermute(v, "row", [(r, (r + 2 * step) % 8) for r in range(8)])


def other_core(v):
    return lax.ppermute(v, "row", [(r, r ^ 1) for r in range(8)])


def y_shift(v, step):
    return lax.ppermute(v, "col", [(c, (c // 4 + step) % 4 * 4 + c % 4) for c in range(16)])


def z_shift(v, step):
    return lax.ppermute(v, "col", [(c, c // 4 * 4 + (c + step) % 4) for c in range(16)])


def whole(array):
    rank = len(array.shape)
    return pl.BlockSpec(array.shape, lambda i, *_: (0,) * rank)


def cost(flops, moved):
    return pl.CostEstimate(flops=flops, bytes_accessed=moved, transcendentals=0)


def split_tiles_kernel(src, dst):
    dst[:, 0] = pltpu.einshape("tbu->btu", src[0])


def split_tiles(left):
    rounds, tile, count, width = left.shape
    rows = 64
    out = pl.pallas_call(
        split_tiles_kernel,
        grid=(rounds, tile // rows),
        in_specs=[pl.BlockSpec((1, rows, count, width), lambda a, t: (a, t, 0, 0))],
        out_specs=pl.BlockSpec((count, 1, rows, width), lambda a, t: (0, a, t, 0)),
        out_shape=jax.ShapeDtypeStruct((count, rounds, tile, width), BF),
        cost_estimate=cost(0, 2 * left.size * 2),
    )(left)
    return out.reshape(count, rounds * tile, width)


def accumulate(acc, left, held, step):
    rows = 128

    def part(m, _):
        here = pl.ds(pl.multiple_of(m * rows, rows), rows)
        total = jnp.dot(left[0, here, :], held[0], preferred_element_type=F32)
        for t in range(1, 3):
            total += jnp.dot(left[t, here, :], held[t], preferred_element_type=F32)

        @pl.when(step == 0)
        def _():
            acc[here, :] = total

        @pl.when(step > 0)
        def _():
            acc[here, :] += total

        return 0

    lax.fori_loop(0, 8, part, 0)


def take_pieces(step, pieces, held):
    half = held.shape[2] // 2
    for j in range(len(pieces) // 2):

        @pl.when(step == j)
        def _():
            held[:, :, :half] = pieces[2 * j][...]
            held[:, :, half:] = pieces[2 * j + 1][...]


def first_products_kernel(order, left, *refs):
    del order
    *pieces, acc, held = refs
    step = pl.program_id(0)
    take_pieces(step, pieces, held)
    accumulate(acc, left, held, step)


def last_products_kernel(order, left, before, *refs):
    del order
    *pieces, first, second, acc, held = refs
    step = pl.program_id(0)

    @pl.when(step == 0)
    def _():
        acc[...] = before[...]

    take_pieces(step, pieces, held)
    accumulate(acc, left, held, step + 1)

    @pl.when(step == pl.num_programs(0) - 1)
    def _():
        for out, base in ((first, 0), (second, 512)):
            for m in range(4):
                block = acc[base + m * 128 : base + (m + 1) * 128, :]
                out[:, m * 128 : (m + 1) * 128] = jnp.transpose(block).astype(BF)


def piece_specs(pieces):
    specs = []
    for array, place in pieces:
        specs.append(pl.BlockSpec((3, 256, 256), lambda i, *_, place=place: (0, 0, place)))
    return specs


def products(order, left, pieces, before=None):
    blocks = len(pieces) // 2
    _, rows, width = left.shape
    left_spec = pl.BlockSpec((3, rows, width), lambda i, order: (order[i], 0, 0))
    arrays = [array for array, _ in pieces]
    held = VMEM((3, 256, 512), BF)
    flops = blocks * 2 * rows * 768 * 512
    moved = blocks * 3 * 2 * (rows * 256 + 256 * 512) + rows * 512 * 4
    if before is None:
        out = jax.ShapeDtypeStruct((rows, 512), F32)
        return pl.pallas_call(
            first_products_kernel,
            grid_spec=pltpu.PrefetchScalarGridSpec(
                num_scalar_prefetch=1,
                grid=(blocks,),
                in_specs=[left_spec, *piece_specs(pieces)],
                out_specs=whole(out),
                scratch_shapes=[held],
            ),
            out_shape=out,
            cost_estimate=cost(flops, moved),
        )(order, left, *arrays)
    out = jax.ShapeDtypeStruct((512, 512), BF)
    return pl.pallas_call(
        last_products_kernel,
        grid_spec=pltpu.PrefetchScalarGridSpec(
            num_scalar_prefetch=1,
            grid=(blocks,),
            in_specs=[left_spec, whole(before), *piece_specs(pieces)],
            out_specs=[whole(out), whole(out)],
            scratch_shapes=[VMEM((rows, 512), F32), held],
        ),
        out_shape=[out, out],
        cost_estimate=cost(flops, moved),
    )(order, left, before, *arrays)


def ring(block, shift):
    half = block.shape[0] // 2
    before = shift(block, 1)
    after = shift(block, -1)
    far_low = shift(before[:half], 1)
    far_high = shift(after[half:], -1)
    return [block, before, after, far_low, far_high]


def both_ways(block, first_shift, then_shift):
    lines = block.shape[1]
    near = ring(block.reshape(3 * lines, -1), first_shift)
    near = jnp.concatenate([*near[:3], *near[3:]], axis=0)
    return ring(near.reshape(4, 3, lines, -1), then_shift)


RELATIVE = (0, -1, 1, 2)


def far_gather(block):
    low, high = block[:, :, :256], block[:, :, 256:]
    before_low = x_shift(low, 1)
    after_high = x_shift(high, -1)
    before_high = x_shift(high, 1)
    after_low = x_shift(low, -1)
    far_low = x_shift(before_low, 1)
    far_high = x_shift(after_high, -1)
    return (low, high), (before_low, before_high), (after_low, after_high), (far_low, far_high)


def stage_kernel(mode, order, tiles, own, one, two, three, base, *refs):
    *weights, out, held = refs
    for i, source in enumerate((own, one, two, three)):
        for k in range(2):
            line = order[2 * i + k]
            held[line] = source[k, :, :256]
            held[8 + line] = source[k, :, 256:]
    for a in range(2):
        flow = mode[a]
        total = jnp.zeros((32, 256), F32)
        place = 0
        for ref in weights[5 * a : 5 * a + 5]:
            for i in range(ref.shape[0]):
                tile = held[tiles[16 * flow + place]]
                total += lax.dot_general(tile, ref[i, 0], NT, preferred_element_type=F32)
                place += 1
        lanes = slice(256 * a, 256 * (a + 1))
        if base is None:
            out[:, lanes] = total.astype(BF)
        else:
            out[:, lanes] = (base[:, lanes] - total).astype(BF)


def apply_stage(order, tiles, values, flows, picks, base=None):
    pair = jnp.stack([values, other_core(values)])
    moved = [pair, x_shift(pair, 1), x_shift(pair, -1), x_shift(pair, 2)]
    weights, specs = [], []
    for flow, q in picks:
        for array in flows[flow]:
            weights.append(array)
            specs.append(
                pl.BlockSpec((array.shape[0], 1, 256, 256), lambda i, *_, q=q: (0, q, 0, 0))
            )
    mode = [flow for flow, _ in picks]
    bases = [] if base is None else [base]

    def kernel(order, tiles, own, one, two, three, *refs):
        if base is None:
            stage_kernel(mode, order, tiles, own, one, two, three, None, *refs)
        else:
            stage_kernel(mode, order, tiles, own, one, two, three, refs[0], *refs[1:])

    out = jax.ShapeDtypeStruct(values.shape, BF)
    return pl.pallas_call(
        kernel,
        grid_spec=pltpu.PrefetchScalarGridSpec(
            num_scalar_prefetch=2,
            grid=(1,),
            in_specs=[*map(whole, moved), *map(whole, bases), *specs],
            out_specs=whole(out),
            scratch_shapes=[VMEM((16, 32, 256), BF)],
        ),
        out_shape=out,
        cost_estimate=cost(2 * 32 * 4096 * 512, 2 * 4096 * 512),
    )(order, tiles, *moved, *bases, *weights)


def over_sites(partial):
    return lax.all_to_all(partial.reshape(16, 32, 512), "col", 0, 0, tiled=True)


def all_sites(values):
    sent = jnp.broadcast_to(values[None], (16, *values.shape))
    return lax.all_to_all(sent, "col", 0, 0, tiled=True).reshape(512, 512)


def row_sum(values):
    values = values + other_core(values)
    return values + x_shift(values, 1) + x_shift(values, -1) + x_shift(values, 2)


def outer_part(own, every):
    return lax.dot_general(own, every, NT, preferred_element_type=F32)


def in_rows(every):
    return jnp.transpose(every).reshape(2, 256, 512)


def body(left_factor, prev_solution, cross, inverses, coupling, prior_cov):
    row, col = lax.axis_index("row"), lax.axis_index("col")
    x, k = row // 2, row % 2
    y, z = col // 4, col % 4
    order = jnp.stack([(x + d) % 4 * 2 + (k + e) % 2 for d in RELATIVE for e in range(2)])
    tiles = jnp.stack(
        [(y + d) % 4 * 4 + (z + e) % 4 for e in RELATIVE for d in RELATIVE]
        + [(y + d) % 4 * 4 + (z + e) % 4 for d in RELATIVE for e in RELATIVE]
    )
    order, tiles = order.astype(jnp.int32), tiles.astype(jnp.int32)

    own, before, after, far = far_gather(prev_solution)
    sibling = other_core(prev_solution)
    factor_lines = [
        *inverses[0, :, :, 0, :],
        *coupling[:, :, 0, :],
        *inverses[1, :, :, 0, :],
    ]
    flows = (
        both_ways(jnp.stack(factor_lines[:3]), y_shift, z_shift),
        both_ways(jnp.stack(factor_lines[3:]), z_shift, y_shift),
    )
    left = split_tiles(left_factor)
    pieces = [(prev_solution, 0), (prev_solution, 1), (sibling, 0), (sibling, 1)]
    for pair in (before, after):
        pieces += [(v, 0) for v in pair] + [(other_core(v), 0) for v in pair]
    started = products(order[:6], left, pieces)
    pieces = [(v, 0) for v in far] + [(other_core(v), 0) for v in far]
    first, second = products(order[6:], left, pieces, started)

    sites = jnp.transpose(cross.reshape(1024, 512))
    sites = lax.dynamic_slice_in_dim(sites, 32 * col, 32, 0).astype(F32)
    first_sum = over_sites(first).astype(F32).sum(axis=0)
    second_sum = over_sites(second).astype(F32).sum(axis=0)
    first_rhs = (sites[:, :512] - first_sum).astype(BF)
    solved_first = apply_stage(order, tiles, first_rhs, flows, ((0, 0), (0, 1)))
    second_rhs = apply_stage(
        order, tiles, solved_first, flows, ((0, 2), (1, 0)), sites[:, 512:] - second_sum
    )
    every_first = all_sites(solved_first)
    solved_second = apply_stage(order, tiles, second_rhs, flows, ((1, 1), (1, 2)))
    every_second = all_sites(solved_second)
    outer = outer_part(solved_first, every_first) + outer_part(solved_second, every_second)
    pred_cov = prior_cov - row_sum(outer) / S
    return jnp.concatenate([in_rows(every_first), in_rows(every_second)]), pred_cov


def solution(mesh):
    placed = (
        P(None, "row", None, "col"),
        P("row", "col", None),
        P(None, "row", None),
        P(None, None, "row", None, "col"),
        P(None, "row", None, "col"),
        P("col", None),
    )
    return jax.shard_map(
        body,
        mesh=mesh,
        in_specs=placed,
        out_specs=(P(None, "row", None), P("col", None)),
        check_vma=False,
    )
```

```python
import jax
import jax.numpy as jnp
from jax import lax
from jax.experimental import pallas as pl
from jax.experimental.pallas import tpu as pltpu
from jax.sharding import PartitionSpec as P

S = 8192
BF = jnp.bfloat16
F32 = jnp.float32
VMEM = pltpu.VMEM
ROOMY = pltpu.CompilerParams(vmem_limit_bytes=20 << 20)
NT = (((1,), (1,)), ((), ()))


def x_shift(v, step):
    return lax.ppermute(v, "row", [(r, (r + 2 * step) % 8) for r in range(8)])


def other_core(v):
    return lax.ppermute(v, "row", [(r, r ^ 1) for r in range(8)])


def y_shift(v, step):
    return lax.ppermute(v, "col", [(c, (c // 4 + step) % 4 * 4 + c % 4) for c in range(16)])


def z_shift(v, step):
    return lax.ppermute(v, "col", [(c, c // 4 * 4 + (c + step) % 4) for c in range(16)])


def whole(array):
    rank = len(array.shape)
    return pl.BlockSpec(array.shape, lambda i, *_: (0,) * rank)


def cost(flops, moved):
    return pl.CostEstimate(flops=flops, bytes_accessed=moved, transcendentals=0)


def split_tiles_kernel(src, dst):
    dst[:, 0] = pltpu.einshape("tbu->btu", src[0])


def split_tiles(left):
    rounds, tile, count, width = left.shape
    rows = 256
    out = pl.pallas_call(
        split_tiles_kernel,
        grid=(rounds, tile // rows),
        in_specs=[pl.BlockSpec((1, rows, count, width), lambda a, t: (a, t, 0, 0))],
        out_specs=pl.BlockSpec((count, 1, rows, width), lambda a, t: (0, a, t, 0)),
        out_shape=jax.ShapeDtypeStruct((count, rounds, tile, width), BF),
        cost_estimate=cost(0, 2 * left.size * 2),
        compiler_params=ROOMY,
    )(left)
    return out.reshape(count, rounds * tile, width)


def accumulate(acc, left, held, step):
    for base in (0, 512):
        here = slice(base, base + 512)
        total = jnp.dot(left[0, here, :], held[0], preferred_element_type=F32)
        for t in range(1, 3):
            total += jnp.dot(left[t, here, :], held[t], preferred_element_type=F32)

        @pl.when(step == 0)
        def _():
            acc[here, :] = total

        @pl.when(step > 0)
        def _():
            acc[here, :] += total


def take_pieces(step, pieces, held):
    half = held.shape[1] // 2
    for j in range(len(pieces) // 2):

        @pl.when(step == j)
        def _():
            held[:, :half, :] = pieces[2 * j][...]
            held[:, half:, :] = pieces[2 * j + 1][...]


def first_products_kernel(order, left, *refs):
    del order
    *pieces, acc, held = refs
    step = pl.program_id(0)
    take_pieces(step, pieces, held)
    accumulate(acc, left, held, step)


def next_products_kernel(order, left, before, *refs):
    del order
    *pieces, acc, held = refs
    step = pl.program_id(0)

    @pl.when(step == 0)
    def _():
        acc[...] = before[...]

    take_pieces(step, pieces, held)
    accumulate(acc, left, held, step + 1)


def last_products_kernel(order, left, before, *refs):
    *pieces, first, second, acc, held = refs
    next_products_kernel(order, left, before, *pieces, acc, held)

    @pl.when(pl.program_id(0) == pl.num_programs(0) - 1)
    def _():
        for out, base in ((first, 0), (second, 512)):
            for m in range(4):
                block = acc[base + m * 128 : base + (m + 1) * 128, :]
                out[:, m * 128 : (m + 1) * 128] = jnp.transpose(block).astype(BF)


def piece_specs(pieces):
    specs = []
    for array, place in pieces:
        specs.append(pl.BlockSpec((3, 128, 512), lambda i, *_, place=place: (0, place, 0)))
    return specs


def products(order, left, pieces, before=None, last=False):
    blocks = len(pieces) // 2
    _, rows, width = left.shape
    left_spec = pl.BlockSpec((3, rows, width), lambda i, order: (order[i], 0, 0))
    arrays = [array for array, _ in pieces]
    scratch = [VMEM((3, 256, 512), BF)]
    flops = blocks * 2 * rows * 768 * 512
    moved = blocks * 3 * 2 * (rows * 256 + 256 * 512) + rows * 512 * 4
    starts = [] if before is None else [before]
    out = jax.ShapeDtypeStruct((rows, 512), F32)
    kernel = first_products_kernel if before is None else next_products_kernel
    if last:
        out = [jax.ShapeDtypeStruct((512, 512), BF)] * 2
        kernel = last_products_kernel
        scratch = [VMEM((rows, 512), F32), *scratch]
    return pl.pallas_call(
        kernel,
        grid_spec=pltpu.PrefetchScalarGridSpec(
            num_scalar_prefetch=1,
            grid=(blocks,),
            in_specs=[left_spec, *map(whole, starts), *piece_specs(pieces)],
            out_specs=jax.tree.map(whole, out),
            scratch_shapes=scratch,
        ),
        out_shape=out,
        cost_estimate=cost(flops, moved),
        compiler_params=ROOMY,
    )(order, left, *starts, *arrays)


def spread_panel(block):
    ways = (0, 1, -1, 2)
    near = jnp.stack([z_shift(block, d) if d else block for d in ways])
    return [y_shift(near, d) if d else near for d in ways]


RELATIVE = (0, -1, 1, 2)


def far_gather(block):
    low, high = block[:, :128, :], block[:, 128:, :]
    before_low = x_shift(low, 1)
    after_high = x_shift(high, -1)
    before_high = x_shift(high, 1)
    after_low = x_shift(low, -1)
    far_low = x_shift(before_low, 1)
    far_high = x_shift(after_high, -1)
    return (low, high), (before_low, before_high), (after_low, after_high), (far_low, far_high)


def place_values(order, sources, held):
    for i, source in enumerate(sources):
        for k in range(2):
            line = order[2 * i + k]
            held[line] = source[k, :, :256]
            held[8 + line] = source[k, :, 256:]


def block_product(tile, block):
    return lax.dot_general(tile, block, NT, preferred_element_type=F32)


def gathered_stage_kernel(subtract, order, own, one, two, three, *refs):
    *base, weights, out, held, total = refs
    step = pl.program_id(0)

    @pl.when(step == 0)
    def _():
        place_values(order, (own, one, two, three), held)
        total[...] = jnp.zeros_like(total)

    for a in range(2):
        rows = slice(256 * a, 256 * (a + 1))
        part = total[:, rows]
        for i in range(4):
            part += block_product(held[4 * step + i], weights[i, rows, :])
        total[:, rows] = part

    @pl.when(step == pl.num_programs(0) - 1)
    def _():
        result = total[...]
        if subtract:
            result = base[0][...] - result
        out[...] = result.astype(BF)


def spread_stage_kernel(order, tiles, own, one, two, three, *refs):
    *weights, out, held = refs
    place_values(order, (own, one, two, three), held)
    for a in range(2):
        rows = slice(256 * a, 256 * (a + 1))
        total = jnp.zeros((32, 256), F32)
        for j, ref in enumerate(weights):
            for i in range(4):
                total += block_product(held[tiles[4 * j + i]], ref[i, rows, :])
        out[:, rows] = total.astype(BF)


def over_cores(values):
    return jnp.stack([values, other_core(values)])


def over_chips(pair):
    return [pair, x_shift(pair, 1), x_shift(pair, -1), x_shift(pair, 2)]


STAGE_COST = cost(2 * 32 * 4096 * 512, 2 * 4096 * 512)
STAGE_OUT = jax.ShapeDtypeStruct((32, 512), BF)
LEAN = pltpu.CompilerParams(vmem_limit_bytes=12 << 20)
SCALARS = pl.BlockSpec(memory_space=pltpu.SMEM)
NEAR = pl.BlockSpec(memory_space=VMEM)


def gathered_stage(order, moved, panels, which, base=None):
    bases = [] if base is None else [base]
    return pl.pallas_call(
        lambda *refs: gathered_stage_kernel(base is not None, *refs),
        grid=(4,),
        in_specs=[
            SCALARS,
            *map(whole, moved),
            *map(whole, bases),
            pl.BlockSpec((4, None, 512, 256), lambda i: (i, which, 0, 0)),
        ],
        out_specs=whole(STAGE_OUT),
        scratch_shapes=[VMEM((16, 32, 256), BF), VMEM((32, 512), F32)],
        out_shape=STAGE_OUT,
        cost_estimate=STAGE_COST,
        compiler_params=LEAN,
    )(order, *moved, *bases, panels)


def spread_stage(order, tiles, moved, panels):
    return pl.pallas_call(
        spread_stage_kernel,
        in_specs=[SCALARS, SCALARS] + [NEAR] * 8,
        out_specs=NEAR,
        scratch_shapes=[VMEM((16, 32, 256), BF)],
        out_shape=STAGE_OUT,
        cost_estimate=STAGE_COST,
        compiler_params=LEAN,
    )(order, tiles, *moved, *panels)


def over_sites(partial):
    return lax.all_to_all(partial.reshape(16, 32, 512), "col", 0, 0, tiled=True)


def all_sites(values):
    sent = jnp.broadcast_to(values[None], (16, *values.shape))
    return lax.all_to_all(sent, "col", 0, 0, tiled=True).reshape(512, 512)


def row_sum(values):
    values = values + other_core(values)
    return values + x_shift(values, 1) + x_shift(values, -1) + x_shift(values, 2)


def outer_part(own, every):
    return lax.dot_general(own, every, NT, preferred_element_type=F32)


def in_rows(every):
    return jnp.transpose(every).reshape(2, 256, 512)


def body(left_factor, prev_solution, cross, inverses, coupling, prior_cov):
    row, col = lax.axis_index("row"), lax.axis_index("col")
    x, k = row // 2, row % 2
    y, z = col // 4, col % 4
    order = jnp.stack([(x + d) % 4 * 2 + (k + e) % 2 for d in RELATIVE for e in range(2)])
    tiles = jnp.stack([(y + d) % 4 * 4 + (z + e) % 4 for d in RELATIVE for e in RELATIVE])
    order, tiles = order.astype(jnp.int32), tiles.astype(jnp.int32)

    own, before, after, far = far_gather(prev_solution)
    sibling = other_core(prev_solution)
    early = jnp.stack([inverses[0].reshape(512, 256), coupling.reshape(512, 256)])
    panels = lax.all_gather(early, "col")
    late_panels = spread_panel(inverses[1].reshape(512, 256))
    left = split_tiles(left_factor)
    pieces = [(prev_solution, 0), (prev_solution, 1), (sibling, 0), (sibling, 1)]
    started = products(order[:2], left, pieces)
    pieces = []
    for pair in (before, after):
        pieces += [(v, 0) for v in pair] + [(other_core(v), 0) for v in pair]
    started = products(order[2:6], left, pieces, started)
    pieces = [(v, 0) for v in far] + [(other_core(v), 0) for v in far]
    first, second = products(order[6:], left, pieces, started, last=True)

    sites = jnp.transpose(cross.reshape(1024, 512))
    sites = lax.dynamic_slice_in_dim(sites, 32 * col, 32, 0).astype(F32)
    first_sum = over_sites(first).astype(F32).sum(axis=0)
    second_sum = over_sites(second).astype(F32).sum(axis=0)
    first_rhs = (sites[:, :512] - first_sum).astype(BF)
    solved_first = gathered_stage(order, over_chips(over_cores(first_rhs)), panels, 0)
    pair = over_cores(solved_first)
    sent, pair = lax.optimization_barrier((solved_first, pair))
    every_first = all_sites(sent)
    base = sites[:, 512:] - second_sum
    second_rhs = gathered_stage(order, over_chips(pair), panels, 1, base)
    second_rhs, every_first = lax.optimization_barrier((second_rhs, every_first))
    moved = over_chips(over_cores(second_rhs))
    solved_second = spread_stage(order, tiles, moved, late_panels)
    every_second = all_sites(solved_second)
    outer = outer_part(solved_first, every_first) + outer_part(solved_second, every_second)
    pred_cov = prior_cov - row_sum(outer) / S
    return jnp.concatenate([in_rows(every_first), in_rows(every_second)]), pred_cov


def solution(mesh):
    placed = (
        P(None, "row", None, "col"),
        P("row", "col", None),
        P(None, "row", None),
        P(None, None, "row", None, "col"),
        P(None, "row", None, "col"),
        P("col", None),
    )
    return jax.shard_map(
        body,
        mesh=mesh,
        in_specs=placed,
        out_specs=(P(None, "row", None), P("col", None)),
        check_vma=False,
    )
```

```python
import jax
import jax.numpy as jnp
from jax import lax
from jax.experimental import pallas as pl
from jax.experimental.pallas import tpu as pltpu
from jax.sharding import PartitionSpec as P

S = 8192
BF = jnp.bfloat16
F32 = jnp.float32
VMEM = pltpu.VMEM
ROOMY = pltpu.CompilerParams(vmem_limit_bytes=20 << 20)
NT = (((1,), (1,)), ((), ()))


def x_shift(v, step):
    return lax.ppermute(v, "row", [(r, (r + 2 * step) % 8) for r in range(8)])


def other_core(v):
    return lax.ppermute(v, "row", [(r, r ^ 1) for r in range(8)])


def y_shift(v, step):
    return lax.ppermute(v, "col", [(c, (c // 4 + step) % 4 * 4 + c % 4) for c in range(16)])


def z_shift(v, step):
    return lax.ppermute(v, "col", [(c, c // 4 * 4 + (c + step) % 4) for c in range(16)])


def whole(array):
    rank = len(array.shape)
    return pl.BlockSpec(array.shape, lambda i, *_: (0,) * rank)


def cost(flops, moved):
    return pl.CostEstimate(flops=flops, bytes_accessed=moved, transcendentals=0)


def split_tiles_kernel(src, dst):
    dst[:, 0] = pltpu.einshape("tbu->btu", src[0])


def split_tiles(left):
    rounds, tile, count, width = left.shape
    rows = 256
    out = pl.pallas_call(
        split_tiles_kernel,
        grid=(rounds, tile // rows),
        in_specs=[pl.BlockSpec((1, rows, count, width), lambda a, t: (a, t, 0, 0))],
        out_specs=pl.BlockSpec((count, 1, rows, width), lambda a, t: (0, a, t, 0)),
        out_shape=pltpu.HBM((count, rounds, tile, width), BF),
        cost_estimate=cost(0, 2 * left.size * 2),
        compiler_params=ROOMY,
    )(left)
    return out.reshape(count, rounds * tile, width)


def accumulate(acc, left, held, step):
    for base in (0, 512):
        here = slice(base, base + 512)
        total = jnp.dot(left[0, here, :], held[0], preferred_element_type=F32)
        for t in range(1, 3):
            total += jnp.dot(left[t, here, :], held[t], preferred_element_type=F32)

        @pl.when(step == 0)
        def _():
            acc[here, :] = total

        @pl.when(step > 0)
        def _():
            acc[here, :] += total


def take_pieces(step, pieces, held):
    half = held.shape[1] // 2
    for j in range(len(pieces) // 2):

        @pl.when(step == j)
        def _():
            held[:, :half, :] = pieces[2 * j][...]
            held[:, half:, :] = pieces[2 * j + 1][...]


def first_products_kernel(order, left, *refs):
    del order
    *pieces, acc, held = refs
    step = pl.program_id(0)
    take_pieces(step, pieces, held)
    accumulate(acc, left, held, step)


def next_products_kernel(order, left, before, *refs):
    del order
    *pieces, acc, held = refs
    step = pl.program_id(0)

    @pl.when(step == 0)
    def _():
        acc[...] = before[...]

    take_pieces(step, pieces, held)
    accumulate(acc, left, held, step + 1)


def last_products_kernel(order, left, before, *refs):
    *pieces, first, second, acc, held = refs
    next_products_kernel(order, left, before, *pieces, acc, held)

    @pl.when(pl.program_id(0) == pl.num_programs(0) - 1)
    def _():
        for out, base in ((first, 0), (second, 512)):
            for m in range(4):
                block = acc[base + m * 128 : base + (m + 1) * 128, :]
                out[:, m * 128 : (m + 1) * 128] = jnp.transpose(block).astype(BF)


def piece_specs(pieces):
    specs = []
    for array, place in pieces:
        specs.append(pl.BlockSpec((3, 128, 512), lambda i, *_, place=place: (0, place, 0)))
    return specs


def products(order, left, pieces, before=None, last=False):
    blocks = len(pieces) // 2
    _, rows, width = left.shape
    left_spec = pl.BlockSpec((3, rows, width), lambda i, order: (order[i], 0, 0))
    left = pltpu.with_memory_space_constraint(left, pltpu.HBM)
    arrays = [array for array, _ in pieces]
    scratch = [VMEM((3, 256, 512), BF)]
    flops = blocks * 2 * rows * 768 * 512
    moved = blocks * 3 * 2 * (rows * 256 + 256 * 512) + rows * 512 * 4
    starts = [] if before is None else [before]
    out = jax.ShapeDtypeStruct((rows, 512), F32)
    kernel = first_products_kernel if before is None else next_products_kernel
    if last:
        out = [jax.ShapeDtypeStruct((512, 512), BF)] * 2
        kernel = last_products_kernel
        scratch = [VMEM((rows, 512), F32), *scratch]
    return pl.pallas_call(
        kernel,
        grid_spec=pltpu.PrefetchScalarGridSpec(
            num_scalar_prefetch=1,
            grid=(blocks,),
            in_specs=[left_spec, *map(whole, starts), *piece_specs(pieces)],
            out_specs=jax.tree.map(whole, out),
            scratch_shapes=scratch,
        ),
        out_shape=out,
        cost_estimate=cost(flops, moved),
        compiler_params=ROOMY,
    )(order, left, *starts, *arrays)


def four_ways(block, shift):
    return [shift(block, -d) if d else block for d in RELATIVE]


RELATIVE = (0, -1, 1, 2)


def place_values(order, sources, held):
    for i, source in enumerate(sources):
        for k in range(2):
            line = order[2 * i + k]
            held[line] = source[k, :, :256]
            held[8 + line] = source[k, :, 256:]


def block_product(tile, block):
    return lax.dot_general(tile, block, NT, preferred_element_type=F32)


def gathered_stage_kernel(subtract, order, own, one, two, three, *refs):
    *base, weights, out, held, total = refs
    step = pl.program_id(0)

    @pl.when(step == 0)
    def _():
        place_values(order, (own, one, two, three), held)
        total[...] = jnp.zeros_like(total)

    for a in range(2):
        rows = slice(256 * a, 256 * (a + 1))
        part = total[:, rows]
        for i in range(4):
            part += block_product(held[4 * step + i], weights[i, rows, :])
        total[:, rows] = part

    @pl.when(step == pl.num_programs(0) - 1)
    def _():
        result = total[...]
        if subtract:
            result = base[0][...] - result
        out[...] = result.astype(BF)


def spread_stage_kernel(order, tiles, own, one, two, three, *refs):
    *weights, out, held = refs
    place_values(order, (own, one, two, three), held)
    for a in range(2):
        rows = slice(256 * a, 256 * (a + 1))
        total = jnp.zeros((32, 256), F32)
        for j, ref in enumerate(weights):
            for i in range(4):
                total += block_product(held[tiles[4 * j + i]], ref[i, rows, :])
        out[:, rows] = total.astype(BF)


def over_cores(values):
    return jnp.stack([values, other_core(values)])


def over_chips(pair):
    return [pair, x_shift(pair, 1), x_shift(pair, -1), x_shift(pair, 2)]


STAGE_COST = cost(2 * 32 * 4096 * 512, 2 * 4096 * 512)
STAGE_OUT = jax.ShapeDtypeStruct((32, 512), BF)
LEAN = pltpu.CompilerParams(vmem_limit_bytes=12 << 20)
SCALARS = pl.BlockSpec(memory_space=pltpu.SMEM)
NEAR = pl.BlockSpec(memory_space=VMEM)


def gathered_stage(order, moved, panels, which, base=None):
    bases = [] if base is None else [base]
    return pl.pallas_call(
        lambda *refs: gathered_stage_kernel(base is not None, *refs),
        grid=(4,),
        in_specs=[
            SCALARS,
            *map(whole, moved),
            *map(whole, bases),
            pl.BlockSpec((4, None, 512, 256), lambda i: (i, which, 0, 0)),
        ],
        out_specs=whole(STAGE_OUT),
        scratch_shapes=[VMEM((16, 32, 256), BF), VMEM((32, 512), F32)],
        out_shape=STAGE_OUT,
        cost_estimate=STAGE_COST,
        compiler_params=LEAN,
    )(order, *moved, *bases, panels)


def spread_stage(order, tiles, moved, panels):
    return pl.pallas_call(
        spread_stage_kernel,
        in_specs=[SCALARS, SCALARS] + [NEAR] * 8,
        out_specs=NEAR,
        scratch_shapes=[VMEM((16, 32, 256), BF)],
        out_shape=STAGE_OUT,
        cost_estimate=STAGE_COST,
        compiler_params=LEAN,
    )(order, tiles, *moved, *panels)


def over_sites(partial):
    return lax.all_to_all(partial.reshape(16, 32, 512), "col", 0, 0, tiled=True)


def all_sites(values):
    sent = jnp.broadcast_to(values[None], (16, *values.shape))
    return lax.all_to_all(sent, "col", 0, 0, tiled=True).reshape(512, 512)


def row_sum(values):
    values = values + other_core(values)
    return values + x_shift(values, 1) + x_shift(values, -1) + x_shift(values, 2)


def outer_part(own, every):
    return lax.dot_general(own, every, NT, preferred_element_type=F32)


def in_rows(every):
    return jnp.transpose(every).reshape(2, 256, 512)


def body(left_factor, prev_solution, cross, inverses, coupling, prior_cov):
    row, col = lax.axis_index("row"), lax.axis_index("col")
    x, k = row // 2, row % 2
    y, z = col // 4, col % 4
    order = jnp.stack([(x + d) % 4 * 2 + (k + e) % 2 for d in RELATIVE for e in range(2)])
    tiles = jnp.stack([(y + d) % 4 * 4 + (z + e) % 4 for d in RELATIVE for e in RELATIVE])
    order, tiles = order.astype(jnp.int32), tiles.astype(jnp.int32)

    early = jnp.stack([inverses[0].reshape(512, 256), coupling.reshape(512, 256)])
    panels = lax.all_gather(early, "col")
    panels = pltpu.with_memory_space_constraint(panels, pltpu.HBM)
    sibling = other_core(prev_solution)
    low, high = prev_solution[:, :128, :], prev_solution[:, 128:, :]
    before_low, after_high = x_shift(low, 1), x_shift(high, -1)
    before_high, after_low = x_shift(high, 1), x_shift(low, -1)
    left = split_tiles(pltpu.with_memory_space_constraint(left_factor, pltpu.HBM))
    late = inverses[1].reshape(512, 256)
    before_low, after_high, left, late = lax.optimization_barrier(
        (before_low, after_high, left, late)
    )
    far_low, far_high = x_shift(before_low, 1), x_shift(after_high, -1)
    near = jnp.stack(four_ways(late, z_shift))
    pieces = [(prev_solution, 0), (prev_solution, 1), (sibling, 0), (sibling, 1)]
    started = products(order[:2], left, pieces)
    before_high, after_low, started = lax.optimization_barrier((before_high, after_low, started))
    started, near = lax.optimization_barrier((started, near))
    late_panels = four_ways(near, y_shift)
    pieces = []
    for pair in ((before_low, before_high), (after_low, after_high)):
        pieces += [(v, 0) for v in pair] + [(other_core(v), 0) for v in pair]
    started = products(order[2:6], left, pieces, started)
    far = (far_low, far_high)
    pieces = [(v, 0) for v in far] + [(other_core(v), 0) for v in far]
    first, second = products(order[6:], left, pieces, started, last=True)

    sites = jnp.transpose(cross.reshape(1024, 512))
    sites = lax.dynamic_slice_in_dim(sites, 32 * col, 32, 0).astype(F32)
    first_sum = over_sites(first).astype(F32).sum(axis=0)
    second_sum = over_sites(second).astype(F32).sum(axis=0)
    first_rhs = (sites[:, :512] - first_sum).astype(BF)
    solved_first = gathered_stage(order, over_chips(over_cores(first_rhs)), panels, 0)
    pair = over_cores(solved_first)
    sent, pair = lax.optimization_barrier((solved_first, pair))
    every_first = all_sites(sent)
    base = sites[:, 512:] - second_sum
    second_rhs = gathered_stage(order, over_chips(pair), panels, 1, base)
    moved = over_chips(over_cores(second_rhs))
    solved_second = spread_stage(order, tiles, moved, late_panels)
    solved_second, every_first = lax.optimization_barrier((solved_second, every_first))
    every_second = all_sites(solved_second)
    outer = outer_part(solved_first, every_first) + outer_part(solved_second, every_second)
    pred_cov = prior_cov - row_sum(outer) / S
    return jnp.concatenate([in_rows(every_first), in_rows(every_second)]), pred_cov


def solution(mesh):
    placed = (
        P(None, "row", None, "col"),
        P("row", "col", None),
        P(None, "row", None),
        P(None, None, "row", None, "col"),
        P(None, "row", None, "col"),
        P("col", None),
    )
    return jax.shard_map(
        body,
        mesh=mesh,
        in_specs=placed,
        out_specs=(P(None, "row", None), P("col", None)),
        check_vma=False,
    )
```

```python
import jax
import jax.numpy as jnp
from jax import lax
from jax.experimental import pallas as pl
from jax.experimental.pallas import tpu as pltpu
from jax.sharding import PartitionSpec as P

S = 8192
BF = jnp.bfloat16
F32 = jnp.float32
VMEM = pltpu.VMEM
ROOMY = pltpu.CompilerParams(vmem_limit_bytes=20 << 20)
NT = (((1,), (1,)), ((), ()))


def x_shift(v, step):
    return lax.ppermute(v, "row", [(r, (r + 2 * step) % 8) for r in range(8)])


def other_core(v):
    return lax.ppermute(v, "row", [(r, r ^ 1) for r in range(8)])


def whole(array):
    rank = len(array.shape)
    return pl.BlockSpec(array.shape, lambda i, *_: (0,) * rank)


def cost(flops, moved):
    return pl.CostEstimate(flops=flops, bytes_accessed=moved, transcendentals=0)


def in_hbm(array):
    return pltpu.with_memory_space_constraint(array, pltpu.HBM)


def prepare_kernel(values, first, second, linking, low, high, lines):
    low[...] = values[:, :128, :]
    high[...] = values[:, 128:, :]
    lines[0] = first[...]
    lines[1] = linking[...]
    lines[2] = second[...]


def prepare(values, inverses, coupling):
    inverses = in_hbm(inverses.reshape(2, 512, 256))
    coupling = in_hbm(coupling.reshape(512, 256))
    half = jax.ShapeDtypeStruct((3, 128, 512), BF)
    out = [half, half, pltpu.HBM((3, 512, 256), BF)]
    return pl.pallas_call(
        prepare_kernel,
        grid=(1,),
        in_specs=[
            whole(values),
            pl.BlockSpec((None, 512, 256), lambda i: (0, 0, 0)),
            pl.BlockSpec((None, 512, 256), lambda i: (1, 0, 0)),
            whole(coupling),
        ],
        out_specs=list(map(whole, out)),
        out_shape=out,
        compiler_params=ROOMY,
    )(in_hbm(values), inverses, inverses, coupling)


def split_tiles_kernel(src, dst):
    dst[:, 0] = pltpu.einshape("tbu->btu", src[0])


def split_tiles(left):
    rounds, tile, count, width = left.shape
    rows = 256
    out = pl.pallas_call(
        split_tiles_kernel,
        grid=(rounds, tile // rows),
        in_specs=[pl.BlockSpec((1, rows, count, width), lambda a, t: (a, t, 0, 0))],
        out_specs=pl.BlockSpec((count, 1, rows, width), lambda a, t: (0, a, t, 0)),
        out_shape=pltpu.HBM((count, rounds, tile, width), BF),
        cost_estimate=cost(0, 2 * left.size * 2),
        compiler_params=ROOMY,
    )(left)
    return out.reshape(count, rounds * tile, width)


def accumulate(acc, left, held, step):
    for base in (0, 512):
        here = slice(base, base + 512)
        total = jnp.dot(left[0, here, :], held[0], preferred_element_type=F32)
        for t in range(1, 3):
            total += jnp.dot(left[t, here, :], held[t], preferred_element_type=F32)

        @pl.when(step == 0)
        def _():
            acc[here, :] = total

        @pl.when(step > 0)
        def _():
            acc[here, :] += total


def take_pieces(step, pieces, held):
    half = held.shape[1] // 2
    for j in range(len(pieces) // 2):

        @pl.when(step == j)
        def _():
            held[:, :half, :] = pieces[2 * j][...]
            held[:, half:, :] = pieces[2 * j + 1][...]


def first_products_kernel(order, left, *refs):
    del order
    *pieces, acc, held = refs
    step = pl.program_id(0)
    take_pieces(step, pieces, held)
    accumulate(acc, left, held, step)


def next_products_kernel(order, left, before, *refs):
    del order
    *pieces, acc, held = refs
    step = pl.program_id(0)

    @pl.when(step == 0)
    def _():
        acc[...] = before[...]

    take_pieces(step, pieces, held)
    accumulate(acc, left, held, step + 1)


def last_products_kernel(order, left, before, *refs):
    *pieces, first, second, acc, held = refs
    next_products_kernel(order, left, before, *pieces, acc, held)

    @pl.when(pl.program_id(0) == pl.num_programs(0) - 1)
    def _():
        for out, base in ((first, 0), (second, 512)):
            for m in range(4):
                block = acc[base + m * 128 : base + (m + 1) * 128, :]
                out[:, m * 128 : (m + 1) * 128] = jnp.transpose(block).astype(BF)


def piece_specs(pieces):
    specs = []
    for array, place in pieces:
        specs.append(pl.BlockSpec((3, 128, 512), lambda i, *_, place=place: (0, place, 0)))
    return specs


def products(order, left, pieces, before=None, last=False):
    blocks = len(pieces) // 2
    _, rows, width = left.shape
    left_spec = pl.BlockSpec((3, rows, width), lambda i, order: (order[i], 0, 0))
    left = pltpu.with_memory_space_constraint(left, pltpu.HBM)
    arrays = [array for array, _ in pieces]
    scratch = [VMEM((3, 256, 512), BF)]
    flops = blocks * 2 * rows * 768 * 512
    moved = blocks * 3 * 2 * (rows * 256 + 256 * 512) + rows * 512 * 4
    starts = [] if before is None else [before]
    out = jax.ShapeDtypeStruct((rows, 512), F32)
    kernel = first_products_kernel if before is None else next_products_kernel
    if last:
        out = [jax.ShapeDtypeStruct((512, 512), BF)] * 2
        kernel = last_products_kernel
        scratch = [VMEM((rows, 512), F32), *scratch]
    return pl.pallas_call(
        kernel,
        grid_spec=pltpu.PrefetchScalarGridSpec(
            num_scalar_prefetch=1,
            grid=(blocks,),
            in_specs=[left_spec, *map(whole, starts), *piece_specs(pieces)],
            out_specs=jax.tree.map(whole, out),
            scratch_shapes=scratch,
        ),
        out_shape=out,
        cost_estimate=cost(flops, moved),
        compiler_params=ROOMY,
    )(order, left, *starts, *arrays)


RELATIVE = (0, -1, 1, 2)


def place_values(order, sources, held):
    for i, source in enumerate(sources):
        for k in range(2):
            line = order[2 * i + k]
            held[line] = source[k, :, :256]
            held[8 + line] = source[k, :, 256:]


def block_product(tile, block):
    return lax.dot_general(tile, block, NT, preferred_element_type=F32)


def gathered_stage_kernel(subtract, order, own, one, two, three, *refs):
    *base, weights, out, held, total = refs
    step = pl.program_id(0)

    @pl.when(step == 0)
    def _():
        place_values(order, (own, one, two, three), held)
        total[...] = jnp.zeros_like(total)

    for a in range(2):
        rows = slice(256 * a, 256 * (a + 1))
        part = total[:, rows]
        for i in range(4):
            part += block_product(held[4 * step + i], weights[i, rows, :])
        total[:, rows] = part

    @pl.when(step == pl.num_programs(0) - 1)
    def _():
        result = total[...]
        if subtract:
            result = base[0][...] - result
        out[...] = result.astype(BF)


def over_cores(values):
    return jnp.stack([values, other_core(values)])


def over_chips(pair):
    return [pair, x_shift(pair, 1), x_shift(pair, -1), x_shift(pair, 2)]


STAGE_COST = cost(2 * 32 * 4096 * 512, 2 * 4096 * 512)
STAGE_OUT = jax.ShapeDtypeStruct((32, 512), BF)
LEAN = pltpu.CompilerParams(vmem_limit_bytes=12 << 20)
SCALARS = pl.BlockSpec(memory_space=pltpu.SMEM)


def gathered_stage(order, moved, panels, which, base=None):
    bases = [] if base is None else [base]
    return pl.pallas_call(
        lambda *refs: gathered_stage_kernel(base is not None, *refs),
        grid=(4,),
        in_specs=[
            SCALARS,
            *map(whole, moved),
            *map(whole, bases),
            pl.BlockSpec((4, None, 512, 256), lambda i: (i, which, 0, 0)),
        ],
        out_specs=whole(STAGE_OUT),
        scratch_shapes=[VMEM((16, 32, 256), BF), VMEM((32, 512), F32)],
        out_shape=STAGE_OUT,
        cost_estimate=STAGE_COST,
        compiler_params=LEAN,
    )(order, *moved, *bases, panels)


def over_sites(partial):
    return lax.all_to_all(partial.reshape(16, 32, 512), "col", 0, 0, tiled=True)


def all_sites(values):
    sent = jnp.broadcast_to(values[None], (16, *values.shape))
    return lax.all_to_all(sent, "col", 0, 0, tiled=True).reshape(512, 512)


def row_sum(values):
    values = values + other_core(values)
    return values + x_shift(values, 1) + x_shift(values, -1) + x_shift(values, 2)


def outer_part(own, every):
    return lax.dot_general(own, every, NT, preferred_element_type=F32)


def in_rows(every):
    return jnp.transpose(every).reshape(2, 256, 512)


def body(left_factor, prev_solution, cross, inverses, coupling, prior_cov):
    row, col = lax.axis_index("row"), lax.axis_index("col")
    x, k = row // 2, row % 2
    order = jnp.stack([(x + d) % 4 * 2 + (k + e) % 2 for d in RELATIVE for e in range(2)])
    order = order.astype(jnp.int32)

    low, high, lines = prepare(prev_solution, inverses, coupling)
    panels = in_hbm(lax.all_gather(lines, "col"))
    before_low, after_high = x_shift(low, 1), x_shift(high, -1)
    before_high, after_low = x_shift(high, 1), x_shift(low, -1)
    sibling = other_core(prev_solution)
    left = split_tiles(in_hbm(left_factor))
    before_low, after_high, left = lax.optimization_barrier((before_low, after_high, left))
    far_low, far_high = x_shift(before_low, 1), x_shift(after_high, -1)
    pieces = [(prev_solution, 0), (prev_solution, 1), (sibling, 0), (sibling, 1)]
    started = products(order[:2], left, pieces)
    before_high, after_low, _ = lax.optimization_barrier(
        (before_high, after_low, started[:8, :128])
    )
    pieces = []
    for pair in ((before_low, before_high), (after_low, after_high)):
        pieces += [(v, 0) for v in pair] + [(other_core(v), 0) for v in pair]
    started = products(order[2:6], left, pieces, started)
    far_low, far_high, _ = lax.optimization_barrier((far_low, far_high, started[:8, :128]))
    far = (far_low, far_high)
    pieces = [(v, 0) for v in far] + [(other_core(v), 0) for v in far]
    first, second = products(order[6:], left, pieces, started, last=True)

    sites = jnp.transpose(cross.reshape(1024, 512))
    sites = lax.dynamic_slice_in_dim(sites, 32 * col, 32, 0).astype(F32)
    first_sum = over_sites(first).astype(F32).sum(axis=0)
    first_rhs = (sites[:, :512] - first_sum).astype(BF)
    first_rhs, second = lax.optimization_barrier((first_rhs, second))
    second_sum = over_sites(second).astype(F32).sum(axis=0)
    solved_first = gathered_stage(order, over_chips(over_cores(first_rhs)), panels, 0)
    pair = over_cores(solved_first)
    moved = over_chips(pair)
    sent, moved[1] = lax.optimization_barrier((solved_first, moved[1]))
    every_first = all_sites(sent)
    base = sites[:, 512:] - second_sum
    second_rhs = gathered_stage(order, moved, panels, 1, base)
    moved = over_chips(over_cores(second_rhs))
    solved_second = gathered_stage(order, moved, panels, 2)
    solved_second, every_first = lax.optimization_barrier((solved_second, every_first))
    every_second = all_sites(solved_second)
    outer = outer_part(solved_first, every_first) + outer_part(solved_second, every_second)
    pred_cov = prior_cov - row_sum(outer) / S
    return jnp.concatenate([in_rows(every_first), in_rows(every_second)]), pred_cov


def solution(mesh):
    placed = (
        P(None, "row", None, "col"),
        P("row", "col", None),
        P(None, "row", None),
        P(None, None, "row", None, "col"),
        P(None, "row", None, "col"),
        P("col", None),
    )
    return jax.shard_map(
        body,
        mesh=mesh,
        in_specs=placed,
        out_specs=(P(None, "row", None), P("col", None)),
        check_vma=False,
    )
```

```python
import jax
import jax.numpy as jnp
from jax import lax
from jax.experimental import pallas as pl
from jax.experimental.pallas import tpu as pltpu
from jax.sharding import PartitionSpec as P

S = 8192
BF = jnp.bfloat16
F32 = jnp.float32
VMEM = pltpu.VMEM
ROOMY = pltpu.CompilerParams(vmem_limit_bytes=20 << 20)


def x_shift(v, step):
    return lax.ppermute(v, "row", [(r, (r + 2 * step) % 8) for r in range(8)])


def other_core(v):
    return lax.ppermute(v, "row", [(r, r ^ 1) for r in range(8)])


def z_exchange(v):
    groups = [[4 * y + z for z in range(4)] for y in range(4)]
    return lax.all_to_all(v, "col", 0, 0, axis_index_groups=groups, tiled=True)


def y_gather(v):
    groups = [[4 * y + z for y in range(4)] for z in range(4)]
    return lax.all_gather(v, "col", axis=0, axis_index_groups=groups, tiled=True)


def whole(array):
    rank = len(array.shape)
    return pl.BlockSpec(array.shape, lambda i, *_: (0,) * rank)


def cost(flops, moved):
    return pl.CostEstimate(flops=flops, bytes_accessed=moved, transcendentals=0)


def in_hbm(array):
    return pltpu.with_memory_space_constraint(array, pltpu.HBM)


def prepare_kernel(values, first, second, linking, low, high, lines):
    low[...] = values[:, :128, :]
    high[...] = values[:, 128:, :]
    for m, source in enumerate((first, linking, second)):
        turned = jnp.transpose(source[...].astype(F32)).astype(BF)
        for q in range(4):
            lines[q, m] = turned[64 * q : 64 * (q + 1), :]


def prepare(values, inverses, coupling):
    inverses = in_hbm(inverses.reshape(2, 512, 256))
    coupling = in_hbm(coupling.reshape(512, 256))
    half = jax.ShapeDtypeStruct((3, 128, 512), BF)
    out = [half, half, jax.ShapeDtypeStruct((4, 3, 64, 512), BF)]
    return pl.pallas_call(
        prepare_kernel,
        grid=(1,),
        in_specs=[
            whole(values),
            pl.BlockSpec((None, 512, 256), lambda i: (0, 0, 0)),
            pl.BlockSpec((None, 512, 256), lambda i: (1, 0, 0)),
            whole(coupling),
        ],
        out_specs=list(map(whole, out)),
        out_shape=out,
        compiler_params=ROOMY,
    )(in_hbm(values), inverses, inverses, coupling)


def split_tiles_kernel(src, dst):
    dst[:, 0] = pltpu.einshape("tbu->btu", src[0])


def split_tiles(left):
    rounds, tile, count, width = left.shape
    rows = 256
    out = pl.pallas_call(
        split_tiles_kernel,
        grid=(rounds, tile // rows),
        in_specs=[pl.BlockSpec((1, rows, count, width), lambda a, t: (a, t, 0, 0))],
        out_specs=pl.BlockSpec((count, 1, rows, width), lambda a, t: (0, a, t, 0)),
        out_shape=pltpu.HBM((count, rounds, tile, width), BF),
        cost_estimate=cost(0, 2 * left.size * 2),
        compiler_params=ROOMY,
    )(left)
    return out.reshape(count, rounds * tile, width)


def accumulate(acc, left, held, step):
    for base in (0, 512):
        here = slice(base, base + 512)
        total = jnp.dot(left[0, here, :], held[0], preferred_element_type=F32)
        for t in range(1, 3):
            total += jnp.dot(left[t, here, :], held[t], preferred_element_type=F32)

        @pl.when(step == 0)
        def _():
            acc[here, :] = total

        @pl.when(step > 0)
        def _():
            acc[here, :] += total


def take_pieces(step, pieces, held):
    half = held.shape[1] // 2
    for j in range(len(pieces) // 2):

        @pl.when(step == j)
        def _():
            held[:, :half, :] = pieces[2 * j][...]
            held[:, half:, :] = pieces[2 * j + 1][...]


def first_products_kernel(order, left, *refs):
    del order
    *pieces, acc, held = refs
    step = pl.program_id(0)
    take_pieces(step, pieces, held)
    accumulate(acc, left, held, step)


def next_products_kernel(order, left, before, token, *refs):
    del order, token
    *pieces, acc, held = refs
    step = pl.program_id(0)

    @pl.when(step == 0)
    def _():
        acc[...] = before[...]

    take_pieces(step, pieces, held)
    accumulate(acc, left, held, step + 1)


def last_products_kernel(order, left, before, token, *refs):
    *pieces, first, second, acc, held = refs
    next_products_kernel(order, left, before, token, *pieces, acc, held)

    @pl.when(pl.program_id(0) == pl.num_programs(0) - 1)
    def _():
        for out, base in ((first, 0), (second, 512)):
            for y in range(4):
                for z in range(4):
                    for a in range(2):
                        top = base + 256 * a + 64 * z
                        block = acc[top : top + 64, 128 * y : 128 * (y + 1)]
                        out[4 * y + z, 64 * a : 64 * (a + 1), :] = block.astype(BF)


def piece_specs(pieces):
    specs = []
    for array, place in pieces:
        specs.append(pl.BlockSpec((3, 128, 512), lambda i, *_, place=place: (0, place, 0)))
    return specs


def products(order, left, pieces, before=None, token=None, last=False):
    blocks = len(pieces) // 2
    _, rows, width = left.shape
    left_spec = pl.BlockSpec((3, rows, width), lambda i, order: (order[i], 0, 0))
    left = pltpu.with_memory_space_constraint(left, pltpu.HBM)
    arrays = [array for array, _ in pieces]
    scratch = [VMEM((3, 256, 512), BF)]
    flops = blocks * 2 * rows * 768 * 512
    moved = blocks * 3 * 2 * (rows * 256 + 256 * 512) + rows * 512 * 4
    starts = [] if before is None else [before, token]
    out = jax.ShapeDtypeStruct((rows, 512), F32)
    kernel = first_products_kernel if before is None else next_products_kernel
    if last:
        out = [jax.ShapeDtypeStruct((16, 128, 128), BF)] * 2
        kernel = last_products_kernel
        scratch = [VMEM((rows, 512), F32), *scratch]
    return pl.pallas_call(
        kernel,
        grid_spec=pltpu.PrefetchScalarGridSpec(
            num_scalar_prefetch=1,
            grid=(blocks,),
            in_specs=[left_spec, *map(whole, starts), *piece_specs(pieces)],
            out_specs=jax.tree.map(whole, out),
            scratch_shapes=scratch,
        ),
        out_shape=out,
        cost_estimate=cost(flops, moved),
        compiler_params=ROOMY,
    )(order, left, *starts, *arrays)


RELATIVE = (0, -1, 1, 2)


def stage_kernel(order, own, one, two, three, weights, out, held):
    for i, source in enumerate((own, one, two, three)):
        for k in range(2):
            line = order[2 * i + k]
            held[line] = source[k, :64, :]
            held[8 + line] = source[k, 64:, :]
    values = held[...].reshape(1024, 128).astype(F32)
    values = jnp.transpose(values).astype(BF)
    factor = weights[...].reshape(1024, 512)
    total = jnp.dot(values, factor, preferred_element_type=F32)
    total = jnp.transpose(total).astype(BF)
    for q in range(4):
        for a in range(2):
            top = 256 * a + 64 * q
            out[q, 64 * a : 64 * (a + 1), :] = total[top : top + 64, :]


def over_cores(values):
    return jnp.stack([values, other_core(values)])


def over_chips(pair):
    return [pair, x_shift(pair, 1), x_shift(pair, -1), x_shift(pair, 2)]


SCALARS = pl.BlockSpec(memory_space=pltpu.SMEM)


def stage(order, values, panels, which):
    moved = over_chips(over_cores(values))
    out = jax.ShapeDtypeStruct((4, 128, 128), BF)
    partial = pl.pallas_call(
        stage_kernel,
        grid=(1,),
        in_specs=[
            SCALARS,
            *map(whole, moved),
            pl.BlockSpec((16, None, 64, 512), lambda i: (0, which, 0, 0)),
        ],
        out_specs=whole(out),
        scratch_shapes=[VMEM((16, 64, 128), BF)],
        out_shape=out,
        cost_estimate=cost(2 * 128 * 1024 * 512, 2 * 1024 * 512),
        compiler_params=ROOMY,
    )(order, *moved, panels)
    return z_exchange(partial).astype(F32).sum(axis=0)


def over_sites(partial):
    return lax.all_to_all(partial, "col", 0, 0, tiled=True).astype(F32).sum(axis=0)


def all_sites(values):
    sent = jnp.broadcast_to(values[None], (16, 128, 128))
    every = lax.all_to_all(sent, "col", 0, 0, tiled=True).reshape(4, 4, 2, 64, 128)
    return jnp.transpose(every, (2, 1, 3, 0, 4)).reshape(2, 256, 512)


def row_sum(values):
    values = values + other_core(values)
    return values + x_shift(values, 1) + x_shift(values, -1) + x_shift(values, 2)


def outer_part(every, col):
    own = lax.dynamic_slice_in_dim(every, 32 * col, 32, 2)
    return jnp.einsum("atm,atn->mn", own, every, preferred_element_type=F32)


def body(left_factor, prev_solution, cross, inverses, coupling, prior_cov):
    row, col = lax.axis_index("row"), lax.axis_index("col")
    x, k = row // 2, row % 2
    y, z = col // 4, col % 4
    order = jnp.stack([(x + d) % 4 * 2 + (k + e) % 2 for d in RELATIVE for e in range(2)])
    order = order.astype(jnp.int32)

    low, high, lines = prepare(prev_solution, inverses, coupling)
    before_low, after_high = x_shift(low, 1), x_shift(high, -1)
    before_high, after_low = x_shift(high, 1), x_shift(low, -1)
    sibling = in_hbm(other_core(prev_solution))
    left = split_tiles(in_hbm(left_factor))
    before_low, after_high, left, lines = lax.optimization_barrier(
        (before_low, after_high, left, lines)
    )
    panels = in_hbm(y_gather(z_exchange(lines)))
    far_low, far_high = x_shift(before_low, 1), x_shift(after_high, -1)
    pieces = [(prev_solution, 0), (prev_solution, 1), (sibling, 0), (sibling, 1)]
    started = products(order[:2], left, pieces)
    before_high, after_low, token = lax.optimization_barrier(
        (before_high, after_low, started[:8, :128])
    )
    pieces = []
    for pair in ((before_low, before_high), (after_low, after_high)):
        pieces += [(v, 0) for v in pair] + [(other_core(v), 0) for v in pair]
    started = products(order[2:6], left, pieces, started, token)
    far_low, far_high, token = lax.optimization_barrier(
        (far_low, far_high, started[:8, :128])
    )
    far = (far_low, far_high)
    pieces = [(v, 0) for v in far] + [(other_core(v), 0) for v in far]
    first, second = products(order[6:], left, pieces, started, token, last=True)

    known = lax.dynamic_slice(cross, (0, 64 * z, 128 * y), (4, 64, 128))
    known = known.astype(F32).reshape(2, 128, 128)
    first_rhs = (known[0] - over_sites(first)).astype(BF)
    first_rhs, second = lax.optimization_barrier((first_rhs, second))
    rest = known[1] - over_sites(second)
    solved_first = stage(order, first_rhs, panels, 0).astype(BF)
    every_first = all_sites(solved_first)
    second_rhs = (rest - stage(order, solved_first, panels, 1)).astype(BF)
    second_rhs, every_first = lax.optimization_barrier((second_rhs, every_first))
    solved_second = stage(order, second_rhs, panels, 2).astype(BF)
    every_second = all_sites(solved_second)
    outer = outer_part(every_first, col) + outer_part(every_second, col)
    pred_cov = prior_cov - row_sum(outer) / S
    return jnp.concatenate([every_first, every_second]), pred_cov


def solution(mesh):
    placed = (
        P(None, "row", None, "col"),
        P("row", "col", None),
        P(None, "row", None),
        P(None, None, "row", None, "col"),
        P(None, "row", None, "col"),
        P("col", None),
    )
    return jax.shard_map(
        body,
        mesh=mesh,
        in_specs=placed,
        out_specs=(P(None, "row", None), P("col", None)),
        check_vma=False,
    )
```

```python
import jax
import jax.numpy as jnp
from jax import lax
from jax.experimental import pallas as pl
from jax.experimental.pallas import tpu as pltpu
from jax.sharding import PartitionSpec as P

S = 8192
BF = jnp.bfloat16
F32 = jnp.float32
VMEM = pltpu.VMEM
ROOMY = pltpu.CompilerParams(vmem_limit_bytes=20 << 20)
NT = (((1,), (1,)), ((), ()))


def x_shift(v, step):
    return lax.ppermute(v, "row", [(r, (r + 2 * step) % 8) for r in range(8)])


def other_core(v):
    return lax.ppermute(v, "row", [(r, r ^ 1) for r in range(8)])


def y_shift(v, step):
    return lax.ppermute(v, "col", [(c, (c // 4 + step) % 4 * 4 + c % 4) for c in range(16)])


def z_shift(v, step):
    return lax.ppermute(v, "col", [(c, c // 4 * 4 + (c + step) % 4) for c in range(16)])


def whole(array):
    rank = len(array.shape)
    return pl.BlockSpec(array.shape, lambda i, *_: (0,) * rank)


def cost(flops, moved):
    return pl.CostEstimate(flops=flops, bytes_accessed=moved, transcendentals=0)


def in_hbm(array):
    return pltpu.with_memory_space_constraint(array, pltpu.HBM)


def prepare_kernel(values, first, second, linking, low, high, early, late):
    low[...] = values[:, :128, :]
    high[...] = values[:, 128:, :]
    early[0] = first[...]
    early[1] = linking[...]
    late[...] = second[...]


def prepare(values, inverses, coupling):
    inverses = in_hbm(inverses.reshape(2, 512, 256))
    coupling = in_hbm(coupling.reshape(512, 256))
    half = jax.ShapeDtypeStruct((3, 128, 512), BF)
    late = jax.ShapeDtypeStruct((512, 256), BF)
    out = [half, half, pltpu.HBM((2, 512, 256), BF), late]
    return pl.pallas_call(
        prepare_kernel,
        grid=(1,),
        in_specs=[
            whole(values),
            pl.BlockSpec((None, 512, 256), lambda i: (0, 0, 0)),
            pl.BlockSpec((None, 512, 256), lambda i: (1, 0, 0)),
            whole(coupling),
        ],
        out_specs=list(map(whole, out)),
        out_shape=out,
        compiler_params=ROOMY,
    )(in_hbm(values), inverses, inverses, coupling)


def split_tiles_kernel(src, dst):
    dst[:, 0] = pltpu.einshape("tbu->btu", src[0])


def split_tiles(left):
    rounds, tile, count, width = left.shape
    rows = 256
    out = pl.pallas_call(
        split_tiles_kernel,
        grid=(rounds, tile // rows),
        in_specs=[pl.BlockSpec((1, rows, count, width), lambda a, t: (a, t, 0, 0))],
        out_specs=pl.BlockSpec((count, 1, rows, width), lambda a, t: (0, a, t, 0)),
        out_shape=pltpu.HBM((count, rounds, tile, width), BF),
        cost_estimate=cost(0, 2 * left.size * 2),
        compiler_params=ROOMY,
    )(left)
    return out.reshape(count, rounds * tile, width)


def accumulate(acc, left, held, step):
    for base in (0, 512):
        here = slice(base, base + 512)
        total = jnp.dot(left[0, here, :], held[0], preferred_element_type=F32)
        for t in range(1, 3):
            total += jnp.dot(left[t, here, :], held[t], preferred_element_type=F32)

        @pl.when(step == 0)
        def _():
            acc[here, :] = total

        @pl.when(step > 0)
        def _():
            acc[here, :] += total


def take_pieces(step, pieces, held):
    half = held.shape[1] // 2
    for j in range(len(pieces) // 2):

        @pl.when(step == j)
        def _():
            held[:, :half, :] = pieces[2 * j][...]
            held[:, half:, :] = pieces[2 * j + 1][...]


def first_products_kernel(order, left, *refs):
    del order
    *pieces, acc, held = refs
    step = pl.program_id(0)
    take_pieces(step, pieces, held)
    accumulate(acc, left, held, step)


def next_products_kernel(order, left, before, token, *refs):
    del order, token
    *pieces, acc, held = refs
    step = pl.program_id(0)

    @pl.when(step == 0)
    def _():
        acc[...] = before[...]

    take_pieces(step, pieces, held)
    accumulate(acc, left, held, step + 1)


def last_products_kernel(order, left, before, token, *refs):
    *pieces, first, second, acc, held = refs
    next_products_kernel(order, left, before, token, *pieces, acc, held)

    @pl.when(pl.program_id(0) == pl.num_programs(0) - 1)
    def _():
        for out, base in ((first, 0), (second, 512)):
            for m in range(4):
                block = acc[base + m * 128 : base + (m + 1) * 128, :]
                out[:, m * 128 : (m + 1) * 128] = jnp.transpose(block).astype(BF)


def piece_specs(pieces):
    specs = []
    for array, place in pieces:
        specs.append(pl.BlockSpec((3, 128, 512), lambda i, *_, place=place: (0, place, 0)))
    return specs


def products(order, left, pieces, before=None, token=None, last=False):
    blocks = len(pieces) // 2
    _, rows, width = left.shape
    left_spec = pl.BlockSpec((3, rows, width), lambda i, order: (order[i], 0, 0))
    left = pltpu.with_memory_space_constraint(left, pltpu.HBM)
    arrays = [array for array, _ in pieces]
    scratch = [VMEM((3, 256, 512), BF)]
    flops = blocks * 2 * rows * 768 * 512
    moved = blocks * 3 * 2 * (rows * 256 + 256 * 512) + rows * 512 * 4
    starts = [] if before is None else [before, token]
    out = jax.ShapeDtypeStruct((rows, 512), F32)
    kernel = first_products_kernel if before is None else next_products_kernel
    if last:
        out = [jax.ShapeDtypeStruct((512, 512), BF)] * 2
        kernel = last_products_kernel
        scratch = [VMEM((rows, 512), F32), *scratch]
    return pl.pallas_call(
        kernel,
        grid_spec=pltpu.PrefetchScalarGridSpec(
            num_scalar_prefetch=1,
            grid=(blocks,),
            in_specs=[left_spec, *map(whole, starts), *piece_specs(pieces)],
            out_specs=jax.tree.map(whole, out),
            scratch_shapes=scratch,
        ),
        out_shape=out,
        cost_estimate=cost(flops, moved),
        compiler_params=ROOMY,
    )(order, left, *starts, *arrays)


def four_ways(block, shift):
    return [shift(block, -d) if d else block for d in RELATIVE]


RELATIVE = (0, -1, 1, 2)


def place_values(order, sources, held):
    for i, source in enumerate(sources):
        for k in range(2):
            line = order[2 * i + k]
            held[line] = source[k, :, :256]
            held[8 + line] = source[k, :, 256:]


def block_product(tile, block):
    return lax.dot_general(tile, block, NT, preferred_element_type=F32)


def gathered_stage_kernel(subtract, order, own, one, two, three, *refs):
    *base, weights, out, held, total = refs
    step = pl.program_id(0)

    @pl.when(step == 0)
    def _():
        place_values(order, (own, one, two, three), held)
        total[...] = jnp.zeros_like(total)

    for a in range(2):
        rows = slice(256 * a, 256 * (a + 1))
        part = total[:, rows]
        for i in range(4):
            part += block_product(held[4 * step + i], weights[i, rows, :])
        total[:, rows] = part

    @pl.when(step == pl.num_programs(0) - 1)
    def _():
        result = total[...]
        if subtract:
            result = base[0][...] - result
        out[...] = result.astype(BF)


def spread_stage_kernel(order, tiles, own, one, two, three, *refs):
    *weights, out, held = refs
    place_values(order, (own, one, two, three), held)
    for a in range(2):
        rows = slice(256 * a, 256 * (a + 1))
        total = jnp.zeros((32, 256), F32)
        for j, ref in enumerate(weights):
            for i in range(4):
                total += block_product(held[tiles[4 * j + i]], ref[i, rows, :])
        out[:, rows] = total.astype(BF)


def over_cores(values):
    return jnp.stack([values, other_core(values)])


def over_chips(pair):
    return [pair, x_shift(pair, 1), x_shift(pair, -1), x_shift(pair, 2)]


STAGE_COST = cost(2 * 32 * 4096 * 512, 2 * 4096 * 512)
STAGE_OUT = jax.ShapeDtypeStruct((32, 512), BF)
LEAN = pltpu.CompilerParams(vmem_limit_bytes=12 << 20)
SCALARS = pl.BlockSpec(memory_space=pltpu.SMEM)
NEAR = pl.BlockSpec(memory_space=VMEM)


def gathered_stage(order, moved, panels, which, base=None):
    bases = [] if base is None else [base]
    return pl.pallas_call(
        lambda *refs: gathered_stage_kernel(base is not None, *refs),
        grid=(4,),
        in_specs=[
            SCALARS,
            *map(whole, moved),
            *map(whole, bases),
            pl.BlockSpec((4, None, 512, 256), lambda i: (i, which, 0, 0)),
        ],
        out_specs=whole(STAGE_OUT),
        scratch_shapes=[VMEM((16, 32, 256), BF), VMEM((32, 512), F32)],
        out_shape=STAGE_OUT,
        cost_estimate=STAGE_COST,
        compiler_params=LEAN,
    )(order, *moved, *bases, panels)


def spread_stage(order, tiles, moved, panels):
    return pl.pallas_call(
        spread_stage_kernel,
        in_specs=[SCALARS, SCALARS] + [NEAR] * 8,
        out_specs=NEAR,
        scratch_shapes=[VMEM((16, 32, 256), BF)],
        out_shape=STAGE_OUT,
        cost_estimate=STAGE_COST,
        compiler_params=LEAN,
    )(order, tiles, *moved, *panels)


def over_sites(partial):
    return lax.all_to_all(partial.reshape(16, 32, 512), "col", 0, 0, tiled=True)


def all_sites(values):
    sent = jnp.broadcast_to(values[None], (16, *values.shape))
    return lax.all_to_all(sent, "col", 0, 0, tiled=True).reshape(512, 512)


def row_sum(values):
    values = values + other_core(values)
    return values + x_shift(values, 1) + x_shift(values, -1) + x_shift(values, 2)


def outer_part(own, every):
    return lax.dot_general(own, every, NT, preferred_element_type=F32)


def in_rows(every):
    return jnp.transpose(every).reshape(2, 256, 512)


def body(left_factor, prev_solution, cross, inverses, coupling, prior_cov):
    row, col = lax.axis_index("row"), lax.axis_index("col")
    x, k = row // 2, row % 2
    order = jnp.stack([(x + d) % 4 * 2 + (k + e) % 2 for d in RELATIVE for e in range(2)])
    y, z = col // 4, col % 4
    tiles = jnp.stack([(y + d) % 4 * 4 + (z + e) % 4 for d in RELATIVE for e in RELATIVE])
    order, tiles = order.astype(jnp.int32), tiles.astype(jnp.int32)

    low, high, early, late = prepare(prev_solution, inverses, coupling)
    panels = in_hbm(lax.all_gather(early, "col"))
    before_low, after_high = x_shift(low, 1), x_shift(high, -1)
    before_high, after_low = x_shift(high, 1), x_shift(low, -1)
    sibling = in_hbm(other_core(prev_solution))
    left = split_tiles(in_hbm(left_factor))
    before_low, after_high, left = lax.optimization_barrier((before_low, after_high, left))
    far_low, far_high = x_shift(before_low, 1), x_shift(after_high, -1)
    pieces = [(prev_solution, 0), (prev_solution, 1), (sibling, 0), (sibling, 1)]
    started = products(order[:2], left, pieces)
    before_high, after_low, token = lax.optimization_barrier(
        (before_high, after_low, started[:8, :128])
    )
    pieces = []
    for pair in ((before_low, before_high), (after_low, after_high)):
        pieces += [(v, 0) for v in pair] + [(other_core(v), 0) for v in pair]
    started = products(order[2:6], left, pieces, started, token)
    far_low, far_high, token = lax.optimization_barrier(
        (far_low, far_high, started[:8, :128])
    )
    far = (far_low, far_high)
    pieces = [(v, 0) for v in far] + [(other_core(v), 0) for v in far]
    first, second = products(order[6:], left, pieces, started, token, last=True)
    first, second, late = lax.optimization_barrier((first, second, late))
    near = jnp.stack(four_ways(late, z_shift))

    sites = jnp.transpose(cross.reshape(1024, 512))
    sites = lax.dynamic_slice_in_dim(sites, 32 * col, 32, 0).astype(F32)
    first_sum = over_sites(first).astype(F32).sum(axis=0)
    first_rhs = (sites[:, :512] - first_sum).astype(BF)
    first_rhs, near = lax.optimization_barrier((first_rhs, near))
    late_panels = four_ways(near, y_shift)
    *moved, second = lax.optimization_barrier((*over_chips(over_cores(first_rhs)), second))
    solved_first = gathered_stage(order, moved, panels, 0)
    base = sites[:, 512:] - over_sites(second).astype(F32).sum(axis=0)
    moved = over_chips(over_cores(solved_first))
    *moved, sent = lax.optimization_barrier((*moved, solved_first))
    every_first = all_sites(sent)
    second_rhs = gathered_stage(order, moved, panels, 1, base)
    moved = over_chips(over_cores(second_rhs))
    solved_second = spread_stage(order, tiles, moved, late_panels)
    solved_second, every_first = lax.optimization_barrier((solved_second, every_first))
    every_second = all_sites(solved_second)
    outer = outer_part(solved_first, every_first) + outer_part(solved_second, every_second)
    pred_cov = prior_cov - row_sum(outer) / S
    return jnp.concatenate([in_rows(every_first), in_rows(every_second)]), pred_cov


def solution(mesh):
    placed = (
        P(None, "row", None, "col"),
        P("row", "col", None),
        P(None, "row", None),
        P(None, None, "row", None, "col"),
        P(None, "row", None, "col"),
        P("col", None),
    )
    return jax.shard_map(
        body,
        mesh=mesh,
        in_specs=placed,
        out_specs=(P(None, "row", None), P("col", None)),
        check_vma=False,
    )
```

```python
import jax
import jax.numpy as jnp
from jax import lax
from jax.experimental import pallas as pl
from jax.experimental.pallas import tpu as pltpu
from jax.sharding import PartitionSpec as P

S = 8192
BF = jnp.bfloat16
F32 = jnp.float32
VMEM = pltpu.VMEM
ROOMY = pltpu.CompilerParams(vmem_limit_bytes=20 << 20)


def x_shift(v, step):
    return lax.ppermute(v, "row", [(r, (r + 2 * step) % 8) for r in range(8)])


def other_core(v):
    return lax.ppermute(v, "row", [(r, r ^ 1) for r in range(8)])


def z_exchange(v):
    groups = [[4 * y + z for z in range(4)] for y in range(4)]
    return lax.all_to_all(v, "col", 0, 0, axis_index_groups=groups, tiled=True)


def y_gather(v):
    groups = [[4 * y + z for y in range(4)] for z in range(4)]
    return lax.all_gather(v, "col", axis=0, axis_index_groups=groups, tiled=True)


def whole(array):
    rank = len(array.shape)
    return pl.BlockSpec(array.shape, lambda i, *_: (0,) * rank)


def cost(flops, moved):
    return pl.CostEstimate(flops=flops, bytes_accessed=moved, transcendentals=0)


def in_hbm(array):
    return pltpu.with_memory_space_constraint(array, pltpu.HBM)


def prepare_kernel(values, first, second, linking, low, high, lines):
    low[...] = values[:, :128, :]
    high[...] = values[:, 128:, :]
    for m, source in enumerate((first, linking, second)):
        turned = jnp.transpose(source[...].astype(F32)).astype(BF)
        for q in range(4):
            lines[q, m] = turned[64 * q : 64 * (q + 1), :]


def prepare(values, inverses, coupling):
    inverses = in_hbm(inverses.reshape(2, 512, 256))
    coupling = in_hbm(coupling.reshape(512, 256))
    half = jax.ShapeDtypeStruct((3, 128, 512), BF)
    out = [half, half, jax.ShapeDtypeStruct((4, 3, 64, 512), BF)]
    return pl.pallas_call(
        prepare_kernel,
        grid=(1,),
        in_specs=[
            whole(values),
            pl.BlockSpec((None, 512, 256), lambda i: (0, 0, 0)),
            pl.BlockSpec((None, 512, 256), lambda i: (1, 0, 0)),
            whole(coupling),
        ],
        out_specs=list(map(whole, out)),
        out_shape=out,
        compiler_params=ROOMY,
    )(in_hbm(values), inverses, inverses, coupling)


def split_tiles_kernel(src, dst):
    dst[:, 0] = pltpu.einshape("tbu->btu", src[0])


def split_tiles(left):
    rounds, tile, count, width = left.shape
    rows = 256
    out = pl.pallas_call(
        split_tiles_kernel,
        grid=(rounds, tile // rows),
        in_specs=[pl.BlockSpec((1, rows, count, width), lambda a, t: (a, t, 0, 0))],
        out_specs=pl.BlockSpec((count, 1, rows, width), lambda a, t: (0, a, t, 0)),
        out_shape=pltpu.HBM((count, rounds, tile, width), BF),
        cost_estimate=cost(0, 2 * left.size * 2),
        compiler_params=ROOMY,
    )(left)
    return out.reshape(count, rounds * tile, width)


def accumulate(acc, left, held, step):
    for base in (0, 512):
        here = slice(base, base + 512)
        total = jnp.dot(left[0, here, :], held[0], preferred_element_type=F32)
        for t in range(1, 3):
            total += jnp.dot(left[t, here, :], held[t], preferred_element_type=F32)

        @pl.when(step == 0)
        def _():
            acc[here, :] = total

        @pl.when(step > 0)
        def _():
            acc[here, :] += total


def take_pieces(step, pieces, held):
    half = held.shape[1] // 2
    for j in range(len(pieces) // 2):

        @pl.when(step == j)
        def _():
            held[:, :half, :] = pieces[2 * j][...]
            held[:, half:, :] = pieces[2 * j + 1][...]


def first_products_kernel(order, left, *refs):
    del order
    *pieces, acc, held = refs
    step = pl.program_id(0)
    take_pieces(step, pieces, held)
    accumulate(acc, left, held, step)


def next_products_kernel(order, left, before, token, *refs):
    del order, token
    *pieces, acc, held = refs
    step = pl.program_id(0)

    @pl.when(step == 0)
    def _():
        acc[...] = before[...]

    take_pieces(step, pieces, held)
    accumulate(acc, left, held, step + 1)


def last_products_kernel(order, left, before, token, *refs):
    *pieces, first, second, acc, held = refs
    next_products_kernel(order, left, before, token, *pieces, acc, held)

    @pl.when(pl.program_id(0) == pl.num_programs(0) - 1)
    def _():
        for out, base in ((first, 0), (second, 512)):
            for y in range(4):
                for z in range(4):
                    for a in range(2):
                        top = base + 256 * a + 64 * z
                        block = acc[top : top + 64, 128 * y : 128 * (y + 1)]
                        out[4 * y + z, 64 * a : 64 * (a + 1), :] = block.astype(BF)


def piece_specs(pieces):
    specs = []
    for array, place in pieces:
        specs.append(pl.BlockSpec((3, 128, 512), lambda i, *_, place=place: (0, place, 0)))
    return specs


def products(order, left, pieces, before=None, token=None, last=False):
    blocks = len(pieces) // 2
    _, rows, width = left.shape
    left_spec = pl.BlockSpec((3, rows, width), lambda i, order: (order[i], 0, 0))
    left = pltpu.with_memory_space_constraint(left, pltpu.HBM)
    arrays = [array for array, _ in pieces]
    scratch = [VMEM((3, 256, 512), BF)]
    flops = blocks * 2 * rows * 768 * 512
    moved = blocks * 3 * 2 * (rows * 256 + 256 * 512) + rows * 512 * 4
    starts = [] if before is None else [before, token]
    out = jax.ShapeDtypeStruct((rows, 512), F32)
    kernel = first_products_kernel if before is None else next_products_kernel
    if last:
        out = [jax.ShapeDtypeStruct((16, 128, 128), BF)] * 2
        kernel = last_products_kernel
        scratch = [VMEM((rows, 512), F32), *scratch]
    return pl.pallas_call(
        kernel,
        grid_spec=pltpu.PrefetchScalarGridSpec(
            num_scalar_prefetch=1,
            grid=(blocks,),
            in_specs=[left_spec, *map(whole, starts), *piece_specs(pieces)],
            out_specs=jax.tree.map(whole, out),
            scratch_shapes=scratch,
        ),
        out_shape=out,
        cost_estimate=cost(flops, moved),
        compiler_params=ROOMY,
    )(order, left, *starts, *arrays)


RELATIVE = (0, -1, 1, 2)


def stage_kernel(order, own, one, two, three, weights, out, held):
    for i, source in enumerate((own, one, two, three)):
        for k in range(2):
            line = order[2 * i + k]
            held[line] = source[k, :64, :]
            held[8 + line] = source[k, 64:, :]
    values = held[...].reshape(1024, 128).astype(F32)
    values = jnp.transpose(values).astype(BF)
    factor = weights[...].reshape(1024, 512)
    total = jnp.dot(values, factor, preferred_element_type=F32)
    total = jnp.transpose(total).astype(BF)
    for q in range(4):
        for a in range(2):
            top = 256 * a + 64 * q
            out[q, 64 * a : 64 * (a + 1), :] = total[top : top + 64, :]


def over_cores(values):
    return jnp.stack([values, other_core(values)])


def over_chips(pair):
    return [pair, x_shift(pair, 1), x_shift(pair, -1), x_shift(pair, 2)]


SCALARS = pl.BlockSpec(memory_space=pltpu.SMEM)


def stage(order, values, panels, which):
    moved = over_chips(over_cores(values))
    out = jax.ShapeDtypeStruct((4, 128, 128), BF)
    partial = pl.pallas_call(
        stage_kernel,
        grid=(1,),
        in_specs=[
            SCALARS,
            *map(whole, moved),
            pl.BlockSpec((16, None, 64, 512), lambda i: (0, which, 0, 0)),
        ],
        out_specs=whole(out),
        scratch_shapes=[VMEM((16, 64, 128), BF)],
        out_shape=out,
        cost_estimate=cost(2 * 128 * 1024 * 512, 2 * 1024 * 512),
        compiler_params=ROOMY,
    )(order, *moved, panels)
    return partial


def over_z(partial):
    return z_exchange(partial).astype(F32).sum(axis=0)


def over_sites(partial):
    return lax.all_to_all(partial, "col", 0, 0, tiled=True).astype(F32).sum(axis=0)


def all_sites(values):
    sent = jnp.broadcast_to(values[None], (16, 128, 128))
    every = lax.all_to_all(sent, "col", 0, 0, tiled=True).reshape(4, 4, 2, 64, 128)
    return jnp.transpose(every, (2, 1, 3, 0, 4)).reshape(2, 256, 512)


def row_sum(values):
    values = values + other_core(values)
    return values + x_shift(values, 1) + x_shift(values, -1) + x_shift(values, 2)


def outer_part(every, col):
    own = lax.dynamic_slice_in_dim(every, 32 * col, 32, 2)
    return jnp.einsum("atm,atn->mn", own, every, preferred_element_type=F32)


def body(left_factor, prev_solution, cross, inverses, coupling, prior_cov):
    row, col = lax.axis_index("row"), lax.axis_index("col")
    x, k = row // 2, row % 2
    y, z = col // 4, col % 4
    order = jnp.stack([(x + d) % 4 * 2 + (k + e) % 2 for d in RELATIVE for e in range(2)])
    order = order.astype(jnp.int32)

    low, high, lines = prepare(prev_solution, inverses, coupling)
    before_low, after_high = x_shift(low, 1), x_shift(high, -1)
    before_high, after_low = x_shift(high, 1), x_shift(low, -1)
    sibling = in_hbm(other_core(prev_solution))
    left = split_tiles(in_hbm(left_factor))
    lines = z_exchange(lines)
    before_low, after_high, before_high, after_low, left, lines = lax.optimization_barrier(
        (before_low, after_high, before_high, after_low, left, lines)
    )
    panels = in_hbm(y_gather(lines))
    far_low, far_high = x_shift(before_low, 1), x_shift(after_high, -1)
    pieces = [(prev_solution, 0), (prev_solution, 1), (sibling, 0), (sibling, 1)]
    started = products(order[:2], left, pieces)
    token = started[:8, :128]
    pieces = []
    for pair in ((before_low, before_high), (after_low, after_high)):
        pieces += [(v, 0) for v in pair] + [(other_core(v), 0) for v in pair]
    started = products(order[2:6], left, pieces, started, token)
    far_low, far_high, token = lax.optimization_barrier(
        (far_low, far_high, started[:8, :128])
    )
    far = (far_low, far_high)
    pieces = [(v, 0) for v in far] + [(other_core(v), 0) for v in far]
    first, second = products(order[6:], left, pieces, started, token, last=True)

    known = lax.dynamic_slice(cross, (0, 64 * z, 128 * y), (4, 64, 128))
    known = known.astype(F32).reshape(2, 128, 128)
    first_rhs = (known[0] - over_sites(first)).astype(BF)
    first_rhs, second = lax.optimization_barrier((first_rhs, second))
    rest = known[1] - over_sites(second)
    solved_first = over_z(stage(order, first_rhs, panels, 0)).astype(BF)
    every_first = all_sites(solved_first)
    second_rhs = (rest - over_z(stage(order, solved_first, panels, 1))).astype(BF)
    partial = stage(order, second_rhs, panels, 2)
    partial, every_first = lax.optimization_barrier((partial, every_first))
    solved_second = over_z(partial).astype(BF)
    every_second = all_sites(solved_second)
    outer = outer_part(every_first, col) + outer_part(every_second, col)
    pred_cov = prior_cov - row_sum(outer) / S
    return jnp.concatenate([every_first, every_second]), pred_cov


def solution(mesh):
    placed = (
        P(None, "row", None, "col"),
        P("row", "col", None),
        P(None, "row", None),
        P(None, None, "row", None, "col"),
        P(None, "row", None, "col"),
        P("col", None),
    )
    return jax.shard_map(
        body,
        mesh=mesh,
        in_specs=placed,
        out_specs=(P(None, "row", None), P("col", None)),
        check_vma=False,
    )
```

```python
import jax
import jax.numpy as jnp
from jax import lax
from jax.experimental import pallas as pl
from jax.experimental.pallas import tpu as pltpu
from jax.sharding import PartitionSpec as P

S = 8192
BF = jnp.bfloat16
F32 = jnp.float32
VMEM = pltpu.VMEM
ROOMY = pltpu.CompilerParams(vmem_limit_bytes=20 << 20)


def x_shift(v, step):
    return lax.ppermute(v, "row", [(r, (r + 2 * step) % 8) for r in range(8)])


def other_core(v):
    return lax.ppermute(v, "row", [(r, r ^ 1) for r in range(8)])


def z_exchange(v):
    groups = [[4 * y + z for z in range(4)] for y in range(4)]
    return lax.all_to_all(v, "col", 0, 0, axis_index_groups=groups, tiled=True)


def y_gather(v):
    groups = [[4 * y + z for y in range(4)] for z in range(4)]
    sent = jnp.broadcast_to(v[None], (4, *v.shape))
    gathered = lax.all_to_all(sent, "col", 0, 0, axis_index_groups=groups, tiled=True)
    return gathered.reshape(16, *v.shape[1:])


def whole(array):
    rank = len(array.shape)
    return pl.BlockSpec(array.shape, lambda i, *_: (0,) * rank)


def cost(flops, moved):
    return pl.CostEstimate(flops=flops, bytes_accessed=moved, transcendentals=0)


def in_hbm(array):
    return pltpu.with_memory_space_constraint(array, pltpu.HBM)


def prepare_kernel(values, first, second, linking, low, high, lines):
    low[...] = values[:, :128, :]
    high[...] = values[:, 128:, :]
    for m, source in enumerate((first, linking, second)):
        turned = jnp.transpose(source[...].astype(F32)).astype(BF)
        for q in range(4):
            lines[q, m] = turned[64 * q : 64 * (q + 1), :]


def prepare(values, inverses, coupling):
    inverses = in_hbm(inverses.reshape(2, 512, 256))
    coupling = in_hbm(coupling.reshape(512, 256))
    half = jax.ShapeDtypeStruct((3, 128, 512), BF)
    out = [half, half, jax.ShapeDtypeStruct((4, 3, 64, 512), BF)]
    return pl.pallas_call(
        prepare_kernel,
        grid=(1,),
        in_specs=[
            whole(values),
            pl.BlockSpec((None, 512, 256), lambda i: (0, 0, 0)),
            pl.BlockSpec((None, 512, 256), lambda i: (1, 0, 0)),
            whole(coupling),
        ],
        out_specs=list(map(whole, out)),
        out_shape=out,
        compiler_params=ROOMY,
    )(in_hbm(values), inverses, inverses, coupling)


def split_tiles_kernel(src, dst):
    dst[:, 0] = pltpu.einshape("tbu->btu", src[0])


def split_tiles(left):
    rounds, tile, count, width = left.shape
    rows = 256
    out = pl.pallas_call(
        split_tiles_kernel,
        grid=(rounds, tile // rows),
        in_specs=[pl.BlockSpec((1, rows, count, width), lambda a, t: (a, t, 0, 0))],
        out_specs=pl.BlockSpec((count, 1, rows, width), lambda a, t: (0, a, t, 0)),
        out_shape=pltpu.HBM((count, rounds, tile, width), BF),
        cost_estimate=cost(0, 2 * left.size * 2),
        compiler_params=ROOMY,
    )(left)
    return out.reshape(count, rounds * tile, width)


def accumulate(acc, left, held, step):
    for base in (0, 512):
        here = slice(base, base + 512)
        total = jnp.dot(left[0, here, :], held[0], preferred_element_type=F32)
        for t in range(1, 3):
            total += jnp.dot(left[t, here, :], held[t], preferred_element_type=F32)

        @pl.when(step == 0)
        def _():
            acc[here, :] = total

        @pl.when(step > 0)
        def _():
            acc[here, :] += total


def take_pieces(step, pieces, held):
    half = held.shape[1] // 2
    for j in range(len(pieces) // 2):

        @pl.when(step == j)
        def _():
            held[:, :half, :] = pieces[2 * j][...]
            held[:, half:, :] = pieces[2 * j + 1][...]


def first_products_kernel(order, left, *refs):
    del order
    *pieces, acc, held = refs
    step = pl.program_id(0)
    take_pieces(step, pieces, held)
    accumulate(acc, left, held, step)


def next_products_kernel(order, left, before, token, *refs):
    del order, token
    *pieces, acc, held = refs
    step = pl.program_id(0)

    @pl.when(step == 0)
    def _():
        acc[...] = before[...]

    take_pieces(step, pieces, held)
    accumulate(acc, left, held, step + 1)


def last_products_kernel(order, left, before, token, *refs):
    *pieces, first, second, acc, held = refs
    next_products_kernel(order, left, before, token, *pieces, acc, held)

    @pl.when(pl.program_id(0) == pl.num_programs(0) - 1)
    def _():
        for out, base in ((first, 0), (second, 512)):
            for y in range(4):
                for z in range(4):
                    for a in range(2):
                        top = base + 256 * a + 64 * z
                        block = acc[top : top + 64, 128 * y : 128 * (y + 1)]
                        out[4 * y + z, 64 * a : 64 * (a + 1), :] = block.astype(BF)


def piece_specs(pieces):
    specs = []
    for array, place in pieces:
        specs.append(pl.BlockSpec((3, 128, 512), lambda i, *_, place=place: (0, place, 0)))
    return specs


def products(order, left, pieces, before=None, token=None, last=False):
    blocks = len(pieces) // 2
    _, rows, width = left.shape
    left_spec = pl.BlockSpec((3, rows, width), lambda i, order: (order[i], 0, 0))
    left = pltpu.with_memory_space_constraint(left, pltpu.HBM)
    arrays = [array for array, _ in pieces]
    scratch = [VMEM((3, 256, 512), BF)]
    flops = blocks * 2 * rows * 768 * 512
    moved = blocks * 3 * 2 * (rows * 256 + 256 * 512) + rows * 512 * 4
    starts = [] if before is None else [before, token]
    out = jax.ShapeDtypeStruct((rows, 512), F32)
    kernel = first_products_kernel if before is None else next_products_kernel
    if last:
        out = [jax.ShapeDtypeStruct((16, 128, 128), BF)] * 2
        kernel = last_products_kernel
        scratch = [VMEM((rows, 512), F32), *scratch]
    return pl.pallas_call(
        kernel,
        grid_spec=pltpu.PrefetchScalarGridSpec(
            num_scalar_prefetch=1,
            grid=(blocks,),
            in_specs=[left_spec, *map(whole, starts), *piece_specs(pieces)],
            out_specs=jax.tree.map(whole, out),
            scratch_shapes=scratch,
        ),
        out_shape=out,
        cost_estimate=cost(flops, moved),
        compiler_params=ROOMY,
    )(order, left, *starts, *arrays)


RELATIVE = (0, -1, 1, 2)


def stage_kernel(order, own, one, two, three, weights, out, held):
    for i, source in enumerate((own, one, two, three)):
        for k in range(2):
            line = order[2 * i + k]
            held[line] = source[k, :64, :]
            held[8 + line] = source[k, 64:, :]
    values = held[...].reshape(1024, 128).astype(F32)
    values = jnp.transpose(values).astype(BF)
    factor = weights[...].reshape(1024, 512)
    total = jnp.dot(values, factor, preferred_element_type=F32)
    total = jnp.transpose(total).astype(BF)
    for q in range(4):
        for a in range(2):
            top = 256 * a + 64 * q
            out[q, 64 * a : 64 * (a + 1), :] = total[top : top + 64, :]


def over_cores(values):
    return jnp.stack([values, other_core(values)])


def over_chips(pair):
    return [pair, x_shift(pair, 1), x_shift(pair, -1), x_shift(pair, 2)]


SCALARS = pl.BlockSpec(memory_space=pltpu.SMEM)


def stage(order, values, panels, which):
    moved = over_chips(over_cores(values))
    out = jax.ShapeDtypeStruct((4, 128, 128), BF)
    partial = pl.pallas_call(
        stage_kernel,
        grid=(1,),
        in_specs=[
            SCALARS,
            *map(whole, moved),
            pl.BlockSpec((16, None, 64, 512), lambda i: (0, which, 0, 0)),
        ],
        out_specs=whole(out),
        scratch_shapes=[VMEM((16, 64, 128), BF)],
        out_shape=out,
        cost_estimate=cost(2 * 128 * 1024 * 512, 2 * 1024 * 512),
        compiler_params=ROOMY,
    )(order, *moved, panels)
    return partial


def over_z(partial):
    return z_exchange(partial).astype(F32).sum(axis=0)


def over_sites(partial):
    return lax.all_to_all(partial, "col", 0, 0, tiled=True).astype(F32).sum(axis=0)


def all_sites(values):
    sent = jnp.broadcast_to(values[None], (16, 128, 128))
    every = lax.all_to_all(sent, "col", 0, 0, tiled=True).reshape(4, 4, 2, 64, 128)
    return jnp.transpose(every, (2, 1, 3, 0, 4)).reshape(2, 256, 512)


def row_sum(values):
    values = values + other_core(values)
    return values + x_shift(values, 1) + x_shift(values, -1) + x_shift(values, 2)


def outer_part(every, col):
    own = lax.dynamic_slice_in_dim(every, 32 * col, 32, 2)
    return jnp.einsum("atm,atn->mn", own, every, preferred_element_type=F32)


def body(left_factor, prev_solution, cross, inverses, coupling, prior_cov):
    row, col = lax.axis_index("row"), lax.axis_index("col")
    x, k = row // 2, row % 2
    y, z = col // 4, col % 4
    order = jnp.stack([(x + d) % 4 * 2 + (k + e) % 2 for d in RELATIVE for e in range(2)])
    order = order.astype(jnp.int32)

    low, high, lines = prepare(prev_solution, inverses, coupling)
    before_low, after_high = x_shift(low, 1), x_shift(high, -1)
    before_high, after_low = x_shift(high, 1), x_shift(low, -1)
    sibling = in_hbm(other_core(prev_solution))
    left = split_tiles(in_hbm(left_factor))
    lines = z_exchange(lines)
    before_low, after_high, before_high, after_low, sibling, left, lines = (
        lax.optimization_barrier(
            (before_low, after_high, before_high, after_low, sibling, left, lines)
        )
    )
    sibling = in_hbm(sibling)
    panels = in_hbm(y_gather(lines))
    far_low, far_high = x_shift(before_low, 1), x_shift(after_high, -1)
    pieces = [(prev_solution, 0), (prev_solution, 1), (sibling, 0), (sibling, 1)]
    started = products(order[:2], left, pieces)
    token = started[:8, :128]
    pieces = []
    for pair in ((before_low, before_high), (after_low, after_high)):
        pieces += [(in_hbm(v), 0) for v in pair]
        pieces += [(in_hbm(other_core(v)), 0) for v in pair]
    started = products(order[2:6], left, pieces, started, token)
    far_low, far_high, token = lax.optimization_barrier(
        (far_low, far_high, started[:8, :128])
    )
    far = (far_low, far_high)
    pieces = [(v, 0) for v in far] + [(other_core(v), 0) for v in far]
    first, second = products(order[6:], left, pieces, started, token, last=True)

    first, second, panels = lax.optimization_barrier((first, second, panels))
    panels = in_hbm(panels)
    known = lax.dynamic_slice(cross, (0, 64 * z, 128 * y), (4, 64, 128))
    known = known.astype(F32).reshape(2, 128, 128)
    first_rhs = (known[0] - over_sites(first)).astype(BF)
    first_rhs, second = lax.optimization_barrier((first_rhs, second))
    rest = known[1] - over_sites(second)
    solved_first = over_z(stage(order, first_rhs, panels, 0)).astype(BF)
    every_first = all_sites(solved_first)
    partial = stage(order, solved_first, panels, 1)
    partial, rest = lax.optimization_barrier((partial, rest))
    second_rhs = (rest - over_z(partial)).astype(BF)
    partial = stage(order, second_rhs, panels, 2)
    partial, every_first = lax.optimization_barrier((partial, every_first))
    solved_second = over_z(partial).astype(BF)
    every_second = all_sites(solved_second)
    outer = outer_part(every_first, col) + outer_part(every_second, col)
    pred_cov = prior_cov - row_sum(outer) / S
    return jnp.concatenate([every_first, every_second]), pred_cov


def solution(mesh):
    placed = (
        P(None, "row", None, "col"),
        P("row", "col", None),
        P(None, "row", None),
        P(None, None, "row", None, "col"),
        P(None, "row", None, "col"),
        P("col", None),
    )
    return jax.shard_map(
        body,
        mesh=mesh,
        in_specs=placed,
        out_specs=(P(None, "row", None), P("col", None)),
        check_vma=False,
    )
```

```python
import jax
import jax.numpy as jnp
from jax import lax
from jax.experimental import pallas as pl
from jax.experimental.pallas import tpu as pltpu
from jax.sharding import PartitionSpec as P

S = 8192
BF = jnp.bfloat16
F32 = jnp.float32
VMEM = pltpu.VMEM
ROOMY = pltpu.CompilerParams(vmem_limit_bytes=20 << 20)


def x_shift(v, step):
    return lax.ppermute(v, "row", [(r, (r + 2 * step) % 8) for r in range(8)])


def other_core(v):
    return lax.ppermute(v, "row", [(r, r ^ 1) for r in range(8)])


def z_exchange(v):
    groups = [[4 * y + z for z in range(4)] for y in range(4)]
    return lax.all_to_all(v, "col", 0, 0, axis_index_groups=groups, tiled=True)


def y_shift(v, step):
    return lax.ppermute(v, "col", [(c, (c // 4 + step) % 4 * 4 + c % 4) for c in range(16)])


def y_gather(v):
    groups = [[4 * y + z for y in range(4)] for z in range(4)]
    sent = jnp.broadcast_to(v[None], (4, *v.shape))
    gathered = lax.all_to_all(sent, "col", 0, 0, axis_index_groups=groups, tiled=True)
    return gathered.reshape(16, *v.shape[1:])


def whole(array):
    rank = len(array.shape)
    return pl.BlockSpec(array.shape, lambda i, *_: (0,) * rank)


def cost(flops, moved):
    return pl.CostEstimate(flops=flops, bytes_accessed=moved, transcendentals=0)


def in_hbm(array):
    return pltpu.with_memory_space_constraint(array, pltpu.HBM)


def prepare_kernel(values, first, second, linking, low, high, lines):
    low[...] = values[:, :128, :]
    high[...] = values[:, 128:, :]
    for m, source in enumerate((first, linking, second)):
        turned = jnp.transpose(source[...].astype(F32)).astype(BF)
        for q in range(4):
            lines[q, m] = turned[64 * q : 64 * (q + 1), :]


def prepare(values, inverses, coupling):
    inverses = in_hbm(inverses.reshape(2, 512, 256))
    coupling = in_hbm(coupling.reshape(512, 256))
    half = jax.ShapeDtypeStruct((3, 128, 512), BF)
    out = [half, half, jax.ShapeDtypeStruct((4, 3, 64, 512), BF)]
    return pl.pallas_call(
        prepare_kernel,
        grid=(1,),
        in_specs=[
            whole(values),
            pl.BlockSpec((None, 512, 256), lambda i: (0, 0, 0)),
            pl.BlockSpec((None, 512, 256), lambda i: (1, 0, 0)),
            whole(coupling),
        ],
        out_specs=list(map(whole, out)),
        out_shape=out,
        compiler_params=ROOMY,
    )(in_hbm(values), inverses, inverses, coupling)


def split_tiles_kernel(src, dst):
    tiles = pltpu.einshape("tbu->btu", src[0])
    for b in range(tiles.shape[0]):
        dst[b // 3, :, 256 * (b % 3) : 256 * (b % 3 + 1)] = tiles[b]


def split_tiles(left):
    rounds, tile, count, width = left.shape
    return pl.pallas_call(
        split_tiles_kernel,
        grid=(rounds,),
        in_specs=[pl.BlockSpec((1, tile, count, width), lambda a: (a, 0, 0, 0))],
        out_specs=pl.BlockSpec((count // 3, tile, 3 * width), lambda a: (0, a, 0)),
        out_shape=pltpu.HBM((count // 3, rounds * tile, 3 * width), BF),
        cost_estimate=cost(0, 2 * left.size * 2),
        compiler_params=ROOMY,
    )(left)


def accumulate(acc, left, held, step):
    values = held[...].reshape(768, 512)
    for base in (0, 512):
        here = slice(base, base + 512)
        total = jnp.dot(left[here, :], values, preferred_element_type=F32)

        @pl.when(step == 0)
        def _():
            acc[here, :] = total

        @pl.when(step > 0)
        def _():
            acc[here, :] += total


def take_pieces(step, pieces, held):
    half = held.shape[1] // 2
    for j in range(len(pieces) // 2):

        @pl.when(step == j)
        def _():
            held[:, :half, :] = pieces[2 * j][...]
            held[:, half:, :] = pieces[2 * j + 1][...]


def first_products_kernel(order, left, *refs):
    del order
    *pieces, acc, held = refs
    step = pl.program_id(0)
    take_pieces(step, pieces, held)
    accumulate(acc, left, held, step)


def next_products_kernel(order, left, before, token, *refs):
    del order, token
    *pieces, acc, held = refs
    step = pl.program_id(0)

    @pl.when(step == 0)
    def _():
        acc[...] = before[...]

    take_pieces(step, pieces, held)
    accumulate(acc, left, held, step + 1)


def last_products_kernel(order, left, before, token, *refs):
    *pieces, first, second, acc, held = refs
    next_products_kernel(order, left, before, token, *pieces, acc, held)

    @pl.when(pl.program_id(0) == pl.num_programs(0) - 1)
    def _():
        for out, base in ((first, 0), (second, 512)):
            for y in range(4):
                for z in range(4):
                    for a in range(2):
                        top = base + 256 * a + 64 * z
                        block = acc[top : top + 64, 128 * y : 128 * (y + 1)]
                        out[4 * y + z, 64 * a : 64 * (a + 1), :] = block.astype(BF)


def piece_specs(pieces):
    specs = []
    for array, place in pieces:
        specs.append(pl.BlockSpec((3, 128, 512), lambda i, *_, place=place: (0, place, 0)))
    return specs


def products(order, left, pieces, before=None, token=None, last=False):
    blocks = len(pieces) // 2
    _, rows, width = left.shape
    left_spec = pl.BlockSpec((None, rows, width), lambda i, order: (order[i], 0, 0))
    left = pltpu.with_memory_space_constraint(left, pltpu.HBM)
    arrays = [array for array, _ in pieces]
    scratch = [VMEM((3, 256, 512), BF)]
    flops = blocks * 2 * rows * 768 * 512
    moved = blocks * 2 * 768 * (rows + 512) + rows * 512 * 4
    starts = [] if before is None else [before, token]
    out = jax.ShapeDtypeStruct((rows, 512), F32)
    kernel = first_products_kernel if before is None else next_products_kernel
    if last:
        out = [jax.ShapeDtypeStruct((16, 128, 128), BF)] * 2
        kernel = last_products_kernel
        scratch = [VMEM((rows, 512), F32), *scratch]
    return pl.pallas_call(
        kernel,
        grid_spec=pltpu.PrefetchScalarGridSpec(
            num_scalar_prefetch=1,
            grid=(blocks,),
            in_specs=[left_spec, *map(whole, starts), *piece_specs(pieces)],
            out_specs=jax.tree.map(whole, out),
            scratch_shapes=scratch,
        ),
        out_shape=out,
        cost_estimate=cost(flops, moved),
        compiler_params=ROOMY,
    )(order, left, *starts, *arrays)


RELATIVE = (0, -1, 1, 2)


def place_values(order, sources, held):
    for i, source in enumerate(sources):
        for k in range(2):
            line = order[2 * i + k]
            held[line] = source[k, :64, :]
            held[8 + line] = source[k, 64:, :]


def put_quarters(total, out):
    total = jnp.transpose(total).astype(BF)
    for q in range(4):
        for a in range(2):
            top = 256 * a + 64 * q
            out[q, 64 * a : 64 * (a + 1), :] = total[top : top + 64, :]


def stage_kernel(order, own, one, two, three, weights, out, held):
    place_values(order, (own, one, two, three), held)
    values = held[...].reshape(1024, 128).astype(F32)
    values = jnp.transpose(values).astype(BF)
    factor = weights[...].reshape(1024, 512)
    total = jnp.dot(values, factor, preferred_element_type=F32)
    put_quarters(total, out)


def late_stage_kernel(order, ys, own, one, two, three, *refs):
    *weights, out, held = refs
    place_values(order, (own, one, two, three), held)
    total = jnp.zeros((128, 512), F32)
    for j, ref in enumerate(weights):
        values = held[pl.ds(4 * ys[j], 4)].reshape(256, 128).astype(F32)
        values = jnp.transpose(values).astype(BF)
        total += jnp.dot(values, ref[...].reshape(256, 512), preferred_element_type=F32)
    put_quarters(total, out)


def over_cores(values):
    return jnp.stack([values, other_core(values)])


def over_chips(pair):
    return [pair, x_shift(pair, 1), x_shift(pair, -1), x_shift(pair, 2)]


SCALARS = pl.BlockSpec(memory_space=pltpu.SMEM)


def stage(order, values, panels, which):
    moved = over_chips(over_cores(values))
    out = jax.ShapeDtypeStruct((4, 128, 128), BF)
    partial = pl.pallas_call(
        stage_kernel,
        grid=(1,),
        in_specs=[
            SCALARS,
            *map(whole, moved),
            pl.BlockSpec((16, None, 64, 512), lambda i: (0, which, 0, 0)),
        ],
        out_specs=whole(out),
        scratch_shapes=[VMEM((16, 64, 128), BF)],
        out_shape=out,
        cost_estimate=cost(2 * 128 * 1024 * 512, 2 * 1024 * 512),
        compiler_params=ROOMY,
    )(order, *moved, panels)
    return partial


def late_stage(order, ys, values, panels):
    moved = over_chips(over_cores(values))
    out = jax.ShapeDtypeStruct((4, 128, 128), BF)
    return pl.pallas_call(
        late_stage_kernel,
        grid=(1,),
        in_specs=[SCALARS, SCALARS, *map(whole, moved), *map(whole, panels)],
        out_specs=whole(out),
        scratch_shapes=[VMEM((16, 64, 128), BF)],
        out_shape=out,
        cost_estimate=cost(2 * 128 * 1024 * 512, 2 * 1024 * 512),
        compiler_params=ROOMY,
    )(order, ys, *moved, *panels)


def over_z(partial):
    return z_exchange(partial).astype(F32).sum(axis=0)


def over_sites(partial):
    return lax.all_to_all(partial, "col", 0, 0, tiled=True).astype(F32).sum(axis=0)


def all_sites(values):
    sent = jnp.broadcast_to(values[None], (16, 128, 128))
    every = lax.all_to_all(sent, "col", 0, 0, tiled=True).reshape(4, 4, 2, 64, 128)
    return jnp.transpose(every, (2, 1, 3, 0, 4)).reshape(2, 256, 512)


def row_sum(values):
    values = values + other_core(values)
    return values + x_shift(values, 1) + x_shift(values, -1) + x_shift(values, 2)


def outer_part(every, col):
    own = lax.dynamic_slice_in_dim(every, 32 * col, 32, 2)
    return jnp.einsum("atm,atn->mn", own, every, preferred_element_type=F32)


def body(left_factor, prev_solution, cross, inverses, coupling, prior_cov):
    row, col = lax.axis_index("row"), lax.axis_index("col")
    x, k = row // 2, row % 2
    y, z = col // 4, col % 4
    order = jnp.stack([(x + d) % 4 * 2 + (k + e) % 2 for d in RELATIVE for e in range(2)])
    ys = jnp.stack([(y + d) % 4 for d in RELATIVE]).astype(jnp.int32)
    order = order.astype(jnp.int32)

    low, high, lines = prepare(prev_solution, inverses, coupling)
    before_low, after_high = x_shift(low, 1), x_shift(high, -1)
    before_high, after_low = x_shift(high, 1), x_shift(low, -1)
    sibling = in_hbm(other_core(prev_solution))
    left = split_tiles(in_hbm(left_factor))
    lines = z_exchange(lines)
    before_low, after_high, before_high, after_low, sibling, left, lines = (
        lax.optimization_barrier(
            (before_low, after_high, before_high, after_low, sibling, left, lines)
        )
    )
    sibling = in_hbm(sibling)
    panels, late = in_hbm(y_gather(lines[:, :2])), lines[:, 2]
    far_low, far_high = x_shift(before_low, 1), x_shift(after_high, -1)
    pieces = [(prev_solution, 0), (prev_solution, 1), (sibling, 0), (sibling, 1)]
    started = products(order[:2], left, pieces)
    token = started[:8, :128]
    pieces = []
    for pair in ((before_low, before_high), (after_low, after_high)):
        pieces += [(in_hbm(v), 0) for v in pair]
        pieces += [(in_hbm(other_core(v)), 0) for v in pair]
    started = products(order[2:6], left, pieces, started, token)
    far_low, far_high, token = lax.optimization_barrier(
        (far_low, far_high, started[:8, :128])
    )
    far = (far_low, far_high)
    pieces = [(v, 0) for v in far] + [(other_core(v), 0) for v in far]
    first, second = products(order[6:], left, pieces, started, token, last=True)

    first, second, panels, late = lax.optimization_barrier((first, second, panels, late))
    late_panels = [y_shift(late, -d) if d else late for d in RELATIVE]
    panels = in_hbm(panels)
    known = lax.dynamic_slice(cross, (0, 64 * z, 128 * y), (4, 64, 128))
    known = known.astype(F32).reshape(2, 128, 128)
    first_rhs = (known[0] - over_sites(first)).astype(BF)
    first_rhs, second, *late_panels = lax.optimization_barrier(
        (first_rhs, second, *late_panels)
    )
    rest = known[1] - over_sites(second)
    partial = stage(order, first_rhs, panels, 0)
    solved_first = over_z(partial).astype(BF)
    every_first = all_sites(solved_first)
    partial = stage(order, solved_first, panels, 1)
    partial, rest = lax.optimization_barrier((partial, rest))
    second_rhs = (rest - over_z(partial)).astype(BF)
    partial = late_stage(order, ys, second_rhs, late_panels)
    partial, every_first = lax.optimization_barrier((partial, every_first))
    solved_second = over_z(partial).astype(BF)
    every_second = all_sites(solved_second)
    outer = outer_part(every_first, col) + outer_part(every_second, col)
    pred_cov = prior_cov - row_sum(outer) / S
    return jnp.concatenate([every_first, every_second]), pred_cov


def solution(mesh):
    placed = (
        P(None, "row", None, "col"),
        P("row", "col", None),
        P(None, "row", None),
        P(None, None, "row", None, "col"),
        P(None, "row", None, "col"),
        P("col", None),
    )
    return jax.shard_map(
        body,
        mesh=mesh,
        in_specs=placed,
        out_specs=(P(None, "row", None), P("col", None)),
        check_vma=False,
    )
```

```python
import jax
import jax.numpy as jnp
from jax import lax
from jax.experimental import pallas as pl
from jax.experimental.pallas import tpu as pltpu
from jax.sharding import PartitionSpec as P

S = 8192
BF = jnp.bfloat16
F32 = jnp.float32
VMEM = pltpu.VMEM
ROOMY = pltpu.CompilerParams(vmem_limit_bytes=20 << 20)


def x_shift(v, step):
    return lax.ppermute(v, "row", [(r, (r + 2 * step) % 8) for r in range(8)])


def other_core(v):
    return lax.ppermute(v, "row", [(r, r ^ 1) for r in range(8)])


def z_exchange(v):
    groups = [[4 * y + z for z in range(4)] for y in range(4)]
    return lax.all_to_all(v, "col", 0, 0, axis_index_groups=groups, tiled=True)


def y_gather(v):
    groups = [[4 * y + z for y in range(4)] for z in range(4)]
    sent = jnp.broadcast_to(v[None], (4, *v.shape))
    gathered = lax.all_to_all(sent, "col", 0, 0, axis_index_groups=groups, tiled=True)
    return gathered.reshape(16, *v.shape[1:])


def z_shift(v, step):
    return lax.ppermute(v, "col", [(c, c // 4 * 4 + (c + step) % 4) for c in range(16)])


def whole(array):
    rank = len(array.shape)
    return pl.BlockSpec(array.shape, lambda i, *_: (0,) * rank)


def cost(flops, moved):
    return pl.CostEstimate(flops=flops, bytes_accessed=moved, transcendentals=0)


def in_hbm(array):
    return pltpu.with_memory_space_constraint(array, pltpu.HBM)


def prepare_kernel(first, second, linking, lines):
    for m, source in enumerate((first, linking, second)):
        turned = jnp.transpose(source[...].astype(F32)).astype(BF)
        for q in range(4):
            lines[q, m] = turned[64 * q : 64 * (q + 1), :]


def prepare(inverses, coupling):
    inverses = in_hbm(inverses.reshape(2, 512, 256))
    coupling = in_hbm(coupling.reshape(512, 256))
    out = jax.ShapeDtypeStruct((4, 3, 64, 512), BF)
    return pl.pallas_call(
        prepare_kernel,
        grid=(1,),
        in_specs=[
            pl.BlockSpec((None, 512, 256), lambda i: (0, 0, 0)),
            pl.BlockSpec((None, 512, 256), lambda i: (1, 0, 0)),
            whole(coupling),
        ],
        out_specs=whole(out),
        out_shape=out,
        compiler_params=ROOMY,
    )(inverses, inverses, coupling)


def split_tiles_kernel(src, dst):
    dst[:, 0] = pltpu.einshape("tbu->btu", src[0])


def split_tiles(left):
    rounds, tile, count, width = left.shape
    rows = 256
    out = pl.pallas_call(
        split_tiles_kernel,
        grid=(rounds, tile // rows),
        in_specs=[pl.BlockSpec((1, rows, count, width), lambda a, t: (a, t, 0, 0))],
        out_specs=pl.BlockSpec((count, 1, rows, width), lambda a, t: (0, a, t, 0)),
        out_shape=pltpu.HBM((count, rounds, tile, width), BF),
        cost_estimate=cost(0, 2 * left.size * 2),
        compiler_params=ROOMY,
    )(left)
    return out.reshape(count, rounds * tile, width)


def accumulate(acc, left, held, step):
    for base in (0, 512):
        here = slice(base, base + 512)
        total = jnp.dot(left[0, here, :], held[0], preferred_element_type=F32)
        for t in range(1, 3):
            total += jnp.dot(left[t, here, :], held[t], preferred_element_type=F32)

        @pl.when(step == 0)
        def _():
            acc[here, :] = total

        @pl.when(step > 0)
        def _():
            acc[here, :] += total


def take_pieces(step, pieces, held):
    half = held.shape[1] // 2
    for j in range(len(pieces) // 2):

        @pl.when(step == j)
        def _():
            held[:, :half, :] = pieces[2 * j][...]
            held[:, half:, :] = pieces[2 * j + 1][...]


def first_products_kernel(order, left, *refs):
    del order
    *pieces, acc, held = refs
    step = pl.program_id(0)
    take_pieces(step, pieces, held)
    accumulate(acc, left, held, step)


def next_products_kernel(order, left, before, token, *refs):
    del order, token
    *pieces, acc, held = refs
    step = pl.program_id(0)

    @pl.when(step == 0)
    def _():
        acc[...] = before[...]

    take_pieces(step, pieces, held)
    accumulate(acc, left, held, step + 1)


def last_products_kernel(order, left, before, token, *refs):
    *pieces, first, second, acc, held = refs
    next_products_kernel(order, left, before, token, *pieces, acc, held)

    @pl.when(pl.program_id(0) == pl.num_programs(0) - 1)
    def _():
        for out, base in ((first, 0), (second, 512)):
            for y in range(4):
                for z in range(4):
                    for a in range(2):
                        top = base + 256 * a + 64 * z
                        block = acc[top : top + 64, 128 * y : 128 * (y + 1)]
                        out[4 * y + z, 64 * a : 64 * (a + 1), :] = block.astype(BF)


def piece_specs(pieces):
    specs = []
    for array, place in pieces:
        specs.append(pl.BlockSpec((3, 128, 512), lambda i, *_, place=place: (0, place, 0)))
    return specs


def products(order, left, pieces, before=None, token=None, last=False):
    blocks = len(pieces) // 2
    _, rows, width = left.shape
    left_spec = pl.BlockSpec((3, rows, width), lambda i, order: (order[i], 0, 0))
    left = pltpu.with_memory_space_constraint(left, pltpu.HBM)
    arrays = [array for array, _ in pieces]
    scratch = [VMEM((3, 256, 512), BF)]
    flops = blocks * 2 * rows * 768 * 512
    moved = blocks * 3 * 2 * (rows * 256 + 256 * 512) + rows * 512 * 4
    starts = [] if before is None else [before, token]
    out = jax.ShapeDtypeStruct((rows, 512), F32)
    kernel = first_products_kernel if before is None else next_products_kernel
    if last:
        out = [jax.ShapeDtypeStruct((16, 128, 128), BF)] * 2
        kernel = last_products_kernel
        scratch = [VMEM((rows, 512), F32), *scratch]
    return pl.pallas_call(
        kernel,
        grid_spec=pltpu.PrefetchScalarGridSpec(
            num_scalar_prefetch=1,
            grid=(blocks,),
            in_specs=[left_spec, *map(whole, starts), *piece_specs(pieces)],
            out_specs=jax.tree.map(whole, out),
            scratch_shapes=scratch,
        ),
        out_shape=out,
        cost_estimate=cost(flops, moved),
        compiler_params=ROOMY,
    )(order, left, *starts, *arrays)


RELATIVE = (0, -1, 1, 2)


def stage_kernel(order, targets, own, one, two, three, weights, *refs):
    *parts, held, result = refs
    for i, source in enumerate((own, one, two, three)):
        for k in range(2):
            line = order[2 * i + k]
            held[line] = source[k, :64, :]
            held[8 + line] = source[k, 64:, :]
    values = held[...].reshape(1024, 128).astype(F32)
    values = jnp.transpose(values).astype(BF)
    factor = weights[...].reshape(1024, 512)
    total = jnp.dot(values, factor, preferred_element_type=F32)
    result[...] = jnp.transpose(total)
    for d, part in enumerate(parts):
        for a in range(2):
            top = pl.multiple_of(256 * a + 64 * targets[d], 64)
            part[64 * a : 64 * (a + 1), :] = result[pl.ds(top, 64), :].astype(BF)


def over_cores(values):
    return jnp.stack([values, other_core(values)])


def over_chips(pair):
    return [pair, x_shift(pair, 1), x_shift(pair, -1), x_shift(pair, 2)]


SCALARS = pl.BlockSpec(memory_space=pltpu.SMEM)


def stage(order, targets, values, panels, which):
    moved = over_chips(over_cores(values))
    out = [jax.ShapeDtypeStruct((128, 128), BF)] * 4
    return pl.pallas_call(
        stage_kernel,
        grid=(1,),
        in_specs=[
            SCALARS,
            SCALARS,
            *map(whole, moved),
            pl.BlockSpec((16, None, 64, 512), lambda i: (0, which, 0, 0)),
        ],
        out_specs=list(map(whole, out)),
        scratch_shapes=[VMEM((16, 64, 128), BF), VMEM((512, 128), F32)],
        out_shape=out,
        cost_estimate=cost(2 * 128 * 1024 * 512, 2 * 1024 * 512),
        compiler_params=ROOMY,
    )(order, targets, *moved, panels)


def over_z(parts):
    moved = [z_shift(part, d) if d else part for d, part in enumerate(parts)]
    return sum(part.astype(F32) for part in moved)


def over_sites(partial):
    return lax.all_to_all(partial, "col", 0, 0, tiled=True).astype(F32).sum(axis=0)


def all_sites(values):
    sent = jnp.broadcast_to(values[None], (16, 128, 128))
    every = lax.all_to_all(sent, "col", 0, 0, tiled=True).reshape(4, 4, 2, 64, 128)
    return jnp.transpose(every, (2, 1, 3, 0, 4)).reshape(2, 256, 512)


def row_sum(values):
    values = values + other_core(values)
    return values + x_shift(values, 1) + x_shift(values, -1) + x_shift(values, 2)


def outer_part(every, col):
    own = lax.dynamic_slice_in_dim(every, 32 * col, 32, 2)
    return jnp.einsum("atm,atn->mn", own, every, preferred_element_type=F32)


def body(left_factor, prev_solution, cross, inverses, coupling, prior_cov):
    row, col = lax.axis_index("row"), lax.axis_index("col")
    x, k = row // 2, row % 2
    y, z = col // 4, col % 4
    order = jnp.stack([(x + d) % 4 * 2 + (k + e) % 2 for d in RELATIVE for e in range(2)])
    order = order.astype(jnp.int32)
    targets = jnp.stack([(z + d) % 4 for d in range(4)]).astype(jnp.int32)

    lines = prepare(inverses, coupling)
    before, after = x_shift(prev_solution, 1), x_shift(prev_solution, -1)
    sibling = other_core(prev_solution)
    left = split_tiles(in_hbm(left_factor))
    lines = z_exchange(lines)
    before, after, sibling, left, lines = lax.optimization_barrier(
        (before, after, sibling, left, lines)
    )
    panels = in_hbm(y_gather(lines))
    far_low, far_high = x_shift(before[:, :128, :], 1), x_shift(after[:, 128:, :], -1)
    halves = lambda v: [(in_hbm(v), 0), (in_hbm(v), 1)]
    pieces = halves(prev_solution) + halves(sibling)
    started = products(order[:2], left, pieces)
    token = started[:8, :128]
    pieces = []
    for block in (before, after):
        pieces += halves(block) + halves(other_core(block))
    started = products(order[2:6], left, pieces, started, token)
    far_low, far_high, token = lax.optimization_barrier(
        (far_low, far_high, started[:8, :128])
    )
    far = (far_low, far_high)
    pieces = [(v, 0) for v in far] + [(other_core(v), 0) for v in far]
    first, second = products(order[6:], left, pieces, started, token, last=True)

    first, second, panels = lax.optimization_barrier((first, second, panels))
    panels = in_hbm(panels)
    known = lax.dynamic_slice(cross, (0, 64 * z, 128 * y), (4, 64, 128))
    known = known.astype(F32).reshape(2, 128, 128)
    first_rhs = (known[0] - over_sites(first)).astype(BF)
    first_rhs, second = lax.optimization_barrier((first_rhs, second))
    rest = known[1] - over_sites(second)
    solved_first = over_z(stage(order, targets, first_rhs, panels, 0)).astype(BF)
    every_first = all_sites(solved_first)
    *parts, rest = lax.optimization_barrier(
        (*stage(order, targets, solved_first, panels, 1), rest)
    )
    second_rhs = (rest - over_z(parts)).astype(BF)
    *parts, every_first = lax.optimization_barrier(
        (*stage(order, targets, second_rhs, panels, 2), every_first)
    )
    solved_second = over_z(parts).astype(BF)
    every_second = all_sites(solved_second)
    outer = outer_part(every_first, col) + outer_part(every_second, col)
    pred_cov = prior_cov - row_sum(outer) / S
    return jnp.concatenate([every_first, every_second]), pred_cov


def solution(mesh):
    placed = (
        P(None, "row", None, "col"),
        P("row", "col", None),
        P(None, "row", None),
        P(None, None, "row", None, "col"),
        P(None, "row", None, "col"),
        P("col", None),
    )
    return jax.shard_map(
        body,
        mesh=mesh,
        in_specs=placed,
        out_specs=(P(None, "row", None), P("col", None)),
        check_vma=False,
    )
```

```python
import jax
import jax.numpy as jnp
from jax import lax
from jax.experimental import pallas as pl
from jax.experimental.pallas import tpu as pltpu
from jax.sharding import PartitionSpec as P

S = 8192
BF = jnp.bfloat16
F32 = jnp.float32
VMEM = pltpu.VMEM
ROOMY = pltpu.CompilerParams(vmem_limit_bytes=20 << 20)


def x_shift(v, step):
    return lax.ppermute(v, "row", [(r, (r + 2 * step) % 8) for r in range(8)])


def other_core(v):
    return lax.ppermute(v, "row", [(r, r ^ 1) for r in range(8)])


def z_exchange(v):
    groups = [[4 * y + z for z in range(4)] for y in range(4)]
    return lax.all_to_all(v, "col", 0, 0, axis_index_groups=groups, tiled=True)


def y_gather(v):
    groups = [[4 * y + z for y in range(4)] for z in range(4)]
    sent = jnp.broadcast_to(v[None], (4, *v.shape))
    gathered = lax.all_to_all(sent, "col", 0, 0, axis_index_groups=groups, tiled=True)
    return gathered.reshape(16, *v.shape[1:])


def z_shift(v, step):
    return lax.ppermute(v, "col", [(c, c // 4 * 4 + (c + step) % 4) for c in range(16)])


def whole(array):
    rank = len(array.shape)
    return pl.BlockSpec(array.shape, lambda i, *_: (0,) * rank)


def cost(flops, moved):
    return pl.CostEstimate(flops=flops, bytes_accessed=moved, transcendentals=0)


def in_hbm(array):
    return pltpu.with_memory_space_constraint(array, pltpu.HBM)


def prepare_kernel(first, second, linking, lines):
    for m, source in enumerate((first, linking, second)):
        turned = jnp.transpose(source[...].astype(F32)).astype(BF)
        for q in range(4):
            lines[q, m] = turned[64 * q : 64 * (q + 1), :]


def prepare(inverses, coupling):
    inverses = in_hbm(inverses.reshape(2, 512, 256))
    coupling = in_hbm(coupling.reshape(512, 256))
    out = jax.ShapeDtypeStruct((4, 3, 64, 512), BF)
    return pl.pallas_call(
        prepare_kernel,
        grid=(1,),
        in_specs=[
            pl.BlockSpec((None, 512, 256), lambda i: (0, 0, 0)),
            pl.BlockSpec((None, 512, 256), lambda i: (1, 0, 0)),
            whole(coupling),
        ],
        out_specs=whole(out),
        out_shape=out,
        compiler_params=ROOMY,
    )(inverses, inverses, coupling)


def split_tiles_kernel(src, token, dst):
    del token
    tiles = pltpu.einshape("tbu->btu", src[0])
    for b in range(tiles.shape[0]):
        dst[b // 3, :, 256 * (b % 3) : 256 * (b % 3 + 1)] = tiles[b]


def split_tiles(left, half, token):
    _, tile, count, width = left.shape
    return pl.pallas_call(
        split_tiles_kernel,
        grid=(2,),
        in_specs=[
            pl.BlockSpec((1, tile, count, width), lambda a: (2 * half + a, 0, 0, 0)),
            whole(token),
        ],
        out_specs=pl.BlockSpec((count // 3, tile, 3 * width), lambda a: (0, a, 0)),
        out_shape=pltpu.HBM((count // 3, 2 * tile, 3 * width), BF),
        cost_estimate=cost(0, left.size * 2),
        compiler_params=ROOMY,
    )(left, token)


def accumulate(acc, halves, held, step):
    values = held[...].reshape(768, 512)
    for half, left in enumerate(halves):
        here = slice(512 * half, 512 * (half + 1))
        total = jnp.dot(left[...], values, preferred_element_type=F32)

        @pl.when(step == 0)
        def _():
            acc[here, :] = total

        @pl.when(step > 0)
        def _():
            acc[here, :] += total


def take_pieces(step, pieces, held):
    half = held.shape[1] // 2
    for j in range(len(pieces) // 2):

        @pl.when(step == j)
        def _():
            held[:, :half, :] = pieces[2 * j][...]
            held[:, half:, :] = pieces[2 * j + 1][...]


def first_products_kernel(order, upper, lower, *refs):
    del order
    *pieces, acc, held = refs
    step = pl.program_id(0)
    take_pieces(step, pieces, held)
    accumulate(acc, (upper, lower), held, step)


def next_products_kernel(order, upper, lower, before, token, *refs):
    del order, token
    *pieces, acc, held = refs
    step = pl.program_id(0)

    @pl.when(step == 0)
    def _():
        acc[...] = before[...]

    take_pieces(step, pieces, held)
    accumulate(acc, (upper, lower), held, step + 1)


def last_products_kernel(order, upper, lower, before, token, *refs):
    *pieces, first, second, acc, held = refs
    next_products_kernel(order, upper, lower, before, token, *pieces, acc, held)

    @pl.when(pl.program_id(0) == pl.num_programs(0) - 1)
    def _():
        for out, base in ((first, 0), (second, 512)):
            for y in range(4):
                for z in range(4):
                    for a in range(2):
                        top = base + 256 * a + 64 * z
                        block = acc[top : top + 64, 128 * y : 128 * (y + 1)]
                        out[4 * y + z, 64 * a : 64 * (a + 1), :] = block.astype(BF)


def piece_specs(pieces):
    specs = []
    for array, place in pieces:
        specs.append(pl.BlockSpec((3, 128, 512), lambda i, *_, place=place: (0, place, 0)))
    return specs


def products(order, left, pieces, before=None, token=None, last=False):
    blocks = len(pieces) // 2
    rows = 1024
    left_spec = pl.BlockSpec((None, 512, 768), lambda i, order: (order[i], 0, 0))
    left = [in_hbm(half) for half in left]
    arrays = [array for array, _ in pieces]
    scratch = [VMEM((3, 256, 512), BF)]
    flops = blocks * 2 * rows * 768 * 512
    moved = blocks * 2 * 768 * (rows + 512) + rows * 512 * 4
    starts = [] if before is None else [before, token]
    out = jax.ShapeDtypeStruct((rows, 512), F32)
    kernel = first_products_kernel if before is None else next_products_kernel
    if last:
        out = [jax.ShapeDtypeStruct((16, 128, 128), BF)] * 2
        kernel = last_products_kernel
        scratch = [VMEM((rows, 512), F32), *scratch]
    return pl.pallas_call(
        kernel,
        grid_spec=pltpu.PrefetchScalarGridSpec(
            num_scalar_prefetch=1,
            grid=(blocks,),
            in_specs=[left_spec, left_spec, *map(whole, starts), *piece_specs(pieces)],
            out_specs=jax.tree.map(whole, out),
            scratch_shapes=scratch,
        ),
        out_shape=out,
        cost_estimate=cost(flops, moved),
        compiler_params=ROOMY,
    )(order, *left, *starts, *arrays)


RELATIVE = (0, -1, 1, 2)


def stage_kernel(order, targets, own, one, two, three, weights, *refs):
    *parts, held, result = refs
    for i, source in enumerate((own, one, two, three)):
        for k in range(2):
            line = order[2 * i + k]
            held[line] = source[k, :64, :]
            held[8 + line] = source[k, 64:, :]
    values = held[...].reshape(1024, 128).astype(F32)
    values = jnp.transpose(values).astype(BF)
    factor = weights[...].reshape(1024, 512)
    total = jnp.dot(values, factor, preferred_element_type=F32)
    result[...] = jnp.transpose(total)
    for d, part in enumerate(parts):
        for a in range(2):
            top = pl.multiple_of(256 * a + 64 * targets[d], 64)
            part[64 * a : 64 * (a + 1), :] = result[pl.ds(top, 64), :].astype(BF)


def over_cores(values):
    return jnp.stack([values, other_core(values)])


def over_chips(pair):
    return [pair, x_shift(pair, 1), x_shift(pair, -1), x_shift(pair, 2)]


SCALARS = pl.BlockSpec(memory_space=pltpu.SMEM)


def stage(order, targets, values, panels, which):
    moved = over_chips(over_cores(values))
    out = [jax.ShapeDtypeStruct((128, 128), BF)] * 4
    return pl.pallas_call(
        stage_kernel,
        grid=(1,),
        in_specs=[
            SCALARS,
            SCALARS,
            *map(whole, moved),
            pl.BlockSpec((16, None, 64, 512), lambda i: (0, which, 0, 0)),
        ],
        out_specs=list(map(whole, out)),
        scratch_shapes=[VMEM((16, 64, 128), BF), VMEM((512, 128), F32)],
        out_shape=out,
        cost_estimate=cost(2 * 128 * 1024 * 512, 2 * 1024 * 512),
        compiler_params=ROOMY,
    )(order, targets, *moved, panels)


def over_z(parts):
    moved = [z_shift(part, d) if d else part for d, part in enumerate(parts)]
    return sum(part.astype(F32) for part in moved)


def over_sites(partial):
    return lax.all_to_all(partial, "col", 0, 0, tiled=True).astype(F32).sum(axis=0)


def all_sites(values):
    sent = jnp.broadcast_to(values[None], (16, 128, 128))
    every = lax.all_to_all(sent, "col", 0, 0, tiled=True).reshape(4, 4, 2, 64, 128)
    return jnp.transpose(every, (2, 1, 3, 0, 4)).reshape(2, 256, 512)


def row_sum(values):
    values = values + other_core(values)
    return values + x_shift(values, 1) + x_shift(values, -1) + x_shift(values, 2)


def outer_part(every, col):
    own = lax.dynamic_slice_in_dim(every, 32 * col, 32, 2)
    return jnp.einsum("atm,atn->mn", own, every, preferred_element_type=F32)


def body(left_factor, prev_solution, cross, inverses, coupling, prior_cov):
    row, col = lax.axis_index("row"), lax.axis_index("col")
    x, k = row // 2, row % 2
    y, z = col // 4, col % 4
    order = jnp.stack([(x + d) % 4 * 2 + (k + e) % 2 for d in RELATIVE for e in range(2)])
    order = order.astype(jnp.int32)
    targets = jnp.stack([(z + d) % 4 for d in range(4)]).astype(jnp.int32)

    lines = prepare(inverses, coupling)
    before, after = x_shift(prev_solution, 1), x_shift(prev_solution, -1)
    sibling = other_core(prev_solution)
    tiles = in_hbm(left_factor)
    upper = split_tiles(tiles, 0, lines[0, 0, :16, :128])
    lines, token = lax.optimization_barrier((z_exchange(lines), upper[0, :16, :128]))
    lower = split_tiles(tiles, 1, token)
    before, after, sibling, upper, lower = lax.optimization_barrier(
        (before, after, sibling, upper, lower)
    )
    left = (upper, lower)
    panels = in_hbm(y_gather(lines))
    far_low, far_high = x_shift(before[:, :128, :], 1), x_shift(after[:, 128:, :], -1)
    halves = lambda v: [(in_hbm(v), 0), (in_hbm(v), 1)]
    pieces = halves(prev_solution) + halves(sibling)
    started = products(order[:2], left, pieces)
    token = started[:8, :128]
    pieces = []
    for block in (before, after):
        pieces += halves(block) + halves(other_core(block))
    started = products(order[2:6], left, pieces, started, token)
    far_low, far_high, token = lax.optimization_barrier(
        (far_low, far_high, started[:8, :128])
    )
    far = (far_low, far_high)
    pieces = [(v, 0) for v in far] + [(other_core(v), 0) for v in far]
    first, second = products(order[6:], left, pieces, started, token, last=True)

    first, second, panels = lax.optimization_barrier((first, second, panels))
    panels = in_hbm(panels)
    known = lax.dynamic_slice(cross, (0, 64 * z, 128 * y), (4, 64, 128))
    known = known.astype(F32).reshape(2, 128, 128)
    first_rhs = (known[0] - over_sites(first)).astype(BF)
    first_rhs, second = lax.optimization_barrier((first_rhs, second))
    rest = known[1] - over_sites(second)
    solved_first = over_z(stage(order, targets, first_rhs, panels, 0)).astype(BF)
    every_first = all_sites(solved_first)
    *parts, rest = lax.optimization_barrier(
        (*stage(order, targets, solved_first, panels, 1), rest)
    )
    second_rhs = (rest - over_z(parts)).astype(BF)
    *parts, every_first = lax.optimization_barrier(
        (*stage(order, targets, second_rhs, panels, 2), every_first)
    )
    solved_second = over_z(parts).astype(BF)
    every_second = all_sites(solved_second)
    outer = outer_part(every_first, col) + outer_part(every_second, col)
    pred_cov = prior_cov - row_sum(outer) / S
    return jnp.concatenate([every_first, every_second]), pred_cov


def solution(mesh):
    placed = (
        P(None, "row", None, "col"),
        P("row", "col", None),
        P(None, "row", None),
        P(None, None, "row", None, "col"),
        P(None, "row", None, "col"),
        P("col", None),
    )
    return jax.shard_map(
        body,
        mesh=mesh,
        in_specs=placed,
        out_specs=(P(None, "row", None), P("col", None)),
        check_vma=False,
    )
```

```python
import jax
import jax.numpy as jnp
from jax import lax
from jax.experimental import pallas as pl
from jax.experimental.pallas import tpu as pltpu
from jax.sharding import PartitionSpec as P

S = 8192
BF = jnp.bfloat16
F32 = jnp.float32
VMEM = pltpu.VMEM
ROOMY = pltpu.CompilerParams(vmem_limit_bytes=20 << 20)


def x_shift(v, step):
    return lax.ppermute(v, "row", [(r, (r + 2 * step) % 8) for r in range(8)])


def other_core(v):
    return lax.ppermute(v, "row", [(r, r ^ 1) for r in range(8)])


def z_exchange(v):
    groups = [[4 * y + z for z in range(4)] for y in range(4)]
    return lax.all_to_all(v, "col", 0, 0, axis_index_groups=groups, tiled=True)


def y_gather(v):
    groups = [[4 * y + z for y in range(4)] for z in range(4)]
    sent = jnp.broadcast_to(v[None], (4, *v.shape))
    gathered = lax.all_to_all(sent, "col", 0, 0, axis_index_groups=groups, tiled=True)
    return gathered.reshape(16, *v.shape[1:])


def z_shift(v, step):
    return lax.ppermute(v, "col", [(c, c // 4 * 4 + (c + step) % 4) for c in range(16)])


def whole(array):
    rank = len(array.shape)
    return pl.BlockSpec(array.shape, lambda i, *_: (0,) * rank)


def cost(flops, moved):
    return pl.CostEstimate(flops=flops, bytes_accessed=moved, transcendentals=0)


def in_hbm(array):
    return pltpu.with_memory_space_constraint(array, pltpu.HBM)


def prepare_kernel(first, second, linking, lines):
    for m, source in enumerate((first, linking, second)):
        turned = jnp.transpose(source[...].astype(F32)).astype(BF)
        for q in range(4):
            lines[q, m] = turned[64 * q : 64 * (q + 1), :]


def prepare(inverses, coupling):
    inverses = in_hbm(inverses.reshape(2, 512, 256))
    coupling = in_hbm(coupling.reshape(512, 256))
    out = jax.ShapeDtypeStruct((4, 3, 64, 512), BF)
    return pl.pallas_call(
        prepare_kernel,
        grid=(1,),
        in_specs=[
            pl.BlockSpec((None, 512, 256), lambda i: (0, 0, 0)),
            pl.BlockSpec((None, 512, 256), lambda i: (1, 0, 0)),
            whole(coupling),
        ],
        out_specs=whole(out),
        out_shape=out,
        compiler_params=ROOMY,
    )(inverses, inverses, coupling)


def split_tiles_kernel(src, token, dst):
    del token
    tiles = pltpu.einshape("tbu->btu", src[0])
    for b in range(tiles.shape[0]):
        dst[b // 3, :, 256 * (b % 3) : 256 * (b % 3 + 1)] = tiles[b]


def split_tiles(left, half, token):
    _, tile, count, width = left.shape
    return pl.pallas_call(
        split_tiles_kernel,
        grid=(2,),
        in_specs=[
            pl.BlockSpec((1, tile, count, width), lambda a: (2 * half + a, 0, 0, 0)),
            whole(token),
        ],
        out_specs=pl.BlockSpec((count // 3, tile, 3 * width), lambda a: (0, a, 0)),
        out_shape=pltpu.HBM((count // 3, 2 * tile, 3 * width), BF),
        cost_estimate=cost(0, left.size * 2),
        compiler_params=ROOMY,
    )(left, token)


def accumulate(acc, halves, held, step):
    values = held[...].reshape(768, 512)
    for half, left in enumerate(halves):
        here = slice(512 * half, 512 * (half + 1))
        total = jnp.dot(left[...], values, preferred_element_type=F32)

        @pl.when(step == 0)
        def _():
            acc[here, :] = total

        @pl.when(step > 0)
        def _():
            acc[here, :] += total


def take_pieces(step, pieces, held):
    half = held.shape[1] // 2
    for j in range(len(pieces) // 2):

        @pl.when(step == j)
        def _():
            held[:, :half, :] = pieces[2 * j][...]
            held[:, half:, :] = pieces[2 * j + 1][...]


def first_products_kernel(order, upper, lower, *refs):
    del order
    *pieces, acc, held = refs
    step = pl.program_id(0)
    take_pieces(step, pieces, held)
    accumulate(acc, (upper, lower), held, step)


def next_products_kernel(order, upper, lower, before, token, *refs):
    del order, token
    *pieces, acc, held = refs
    step = pl.program_id(0)

    @pl.when(step == 0)
    def _():
        acc[...] = before[...]

    take_pieces(step, pieces, held)
    accumulate(acc, (upper, lower), held, step + 1)


def last_products_kernel(order, upper, lower, before, token, *refs):
    *pieces, first, second, acc, held = refs
    next_products_kernel(order, upper, lower, before, token, *pieces, acc, held)

    @pl.when(pl.program_id(0) == pl.num_programs(0) - 1)
    def _():
        for out, base in ((first, 0), (second, 512)):
            for y in range(4):
                for z in range(4):
                    for a in range(2):
                        top = base + 256 * a + 64 * z
                        block = acc[top : top + 64, 128 * y : 128 * (y + 1)]
                        out[4 * y + z, 64 * a : 64 * (a + 1), :] = block.astype(BF)


def piece_specs(pieces):
    specs = []
    for array, place in pieces:
        specs.append(pl.BlockSpec((3, 128, 512), lambda i, *_, place=place: (0, place, 0)))
    return specs


def products(order, left, pieces, before=None, token=None, last=False):
    blocks = len(pieces) // 2
    rows = 1024
    left_spec = pl.BlockSpec((None, 512, 768), lambda i, order: (order[i], 0, 0))
    left = [in_hbm(half) for half in left]
    arrays = [array for array, _ in pieces]
    scratch = [VMEM((3, 256, 512), BF)]
    flops = blocks * 2 * rows * 768 * 512
    moved = blocks * 2 * 768 * (rows + 512) + rows * 512 * 4
    starts = [] if before is None else [before, token]
    out = jax.ShapeDtypeStruct((rows, 512), F32)
    kernel = first_products_kernel if before is None else next_products_kernel
    if last:
        out = [jax.ShapeDtypeStruct((16, 128, 128), BF)] * 2
        kernel = last_products_kernel
        scratch = [VMEM((rows, 512), F32), *scratch]
    return pl.pallas_call(
        kernel,
        grid_spec=pltpu.PrefetchScalarGridSpec(
            num_scalar_prefetch=1,
            grid=(blocks,),
            in_specs=[left_spec, left_spec, *map(whole, starts), *piece_specs(pieces)],
            out_specs=jax.tree.map(whole, out),
            scratch_shapes=scratch,
        ),
        out_shape=out,
        cost_estimate=cost(flops, moved),
        compiler_params=ROOMY,
    )(order, *left, *starts, *arrays)


RELATIVE = (0, -1, 1, 2)


def stage_kernel(order, targets, own, one, two, three, weights, *refs):
    *parts, held, result = refs
    for i, source in enumerate((own, one, two, three)):
        for k in range(2):
            line = order[2 * i + k]
            held[line] = source[k, :64, :]
            held[8 + line] = source[k, 64:, :]
    values = held[...].reshape(1024, 128).astype(F32)
    values = jnp.transpose(values).astype(BF)
    factor = weights[...].reshape(1024, 512)
    total = jnp.dot(values, factor, preferred_element_type=F32)
    result[...] = jnp.transpose(total)
    for d, part in enumerate(parts):
        for a in range(2):
            top = pl.multiple_of(256 * a + 64 * targets[d], 64)
            part[64 * a : 64 * (a + 1), :] = result[pl.ds(top, 64), :].astype(BF)


def over_cores(values):
    return jnp.stack([values, other_core(values)])


def over_chips(pair):
    return [pair, x_shift(pair, 1), x_shift(pair, -1), x_shift(pair, 2)]


SCALARS = pl.BlockSpec(memory_space=pltpu.SMEM)


def stage(order, targets, pair, panels, which):
    moved = over_chips(pair)
    out = [jax.ShapeDtypeStruct((128, 128), BF)] * 4
    return pl.pallas_call(
        stage_kernel,
        grid=(1,),
        in_specs=[
            SCALARS,
            SCALARS,
            *map(whole, moved),
            pl.BlockSpec((16, None, 64, 512), lambda i: (0, which, 0, 0)),
        ],
        out_specs=list(map(whole, out)),
        scratch_shapes=[VMEM((16, 64, 128), BF), VMEM((512, 128), F32)],
        out_shape=out,
        cost_estimate=cost(2 * 128 * 1024 * 512, 2 * 1024 * 512),
        compiler_params=ROOMY,
    )(order, targets, *moved, panels)


def over_z(parts):
    moved = [z_shift(part, d) if d else part for d, part in enumerate(parts)]
    return sum(part.astype(F32) for part in moved)


def over_sites(partial):
    return lax.all_to_all(partial, "col", 0, 0, tiled=True).astype(F32).sum(axis=0)


def all_sites(values):
    sent = jnp.broadcast_to(values[None], (16, 128, 128))
    every = lax.all_to_all(sent, "col", 0, 0, tiled=True).reshape(4, 4, 2, 64, 128)
    return jnp.transpose(every, (2, 1, 3, 0, 4)).reshape(2, 256, 512)


def row_sum(values):
    values = values + other_core(values)
    return values + x_shift(values, 1) + x_shift(values, -1) + x_shift(values, 2)


def outer_part(every, col):
    own = lax.dynamic_slice_in_dim(every, 32 * col, 32, 2)
    return jnp.einsum("atm,atn->mn", own, every, preferred_element_type=F32)


def body(left_factor, prev_solution, cross, inverses, coupling, prior_cov):
    row, col = lax.axis_index("row"), lax.axis_index("col")
    x, k = row // 2, row % 2
    y, z = col // 4, col % 4
    order = jnp.stack([(x + d) % 4 * 2 + (k + e) % 2 for d in RELATIVE for e in range(2)])
    order = order.astype(jnp.int32)
    targets = jnp.stack([(z + d) % 4 for d in range(4)]).astype(jnp.int32)

    lines = prepare(inverses, coupling)
    before, after = x_shift(prev_solution, 1), x_shift(prev_solution, -1)
    sibling = other_core(prev_solution)
    tiles = in_hbm(left_factor)
    upper = split_tiles(tiles, 0, lines[0, 0, :16, :128])
    lines, token = lax.optimization_barrier((z_exchange(lines), upper[0, :16, :128]))
    lower = split_tiles(tiles, 1, token)
    before, after, sibling, upper, lower = lax.optimization_barrier(
        (before, after, sibling, upper, lower)
    )
    left = (upper, lower)
    panels = in_hbm(y_gather(lines))
    far_low, far_high = x_shift(before[:, :128, :], 1), x_shift(after[:, 128:, :], -1)
    halves = lambda v: [(in_hbm(v), 0), (in_hbm(v), 1)]
    pieces = halves(prev_solution) + halves(sibling)
    for block in (before, after):
        pieces += halves(block) + halves(other_core(block))
    started = products(order[:6], left, pieces)
    far_low, far_high, token = lax.optimization_barrier(
        (far_low, far_high, started[:8, :128])
    )
    far = (far_low, far_high)
    pieces = [(v, 0) for v in far] + [(other_core(v), 0) for v in far]
    first, second = products(order[6:], left, pieces, started, token, last=True)

    first, second, panels = lax.optimization_barrier((first, second, panels))
    panels = in_hbm(panels)
    known = lax.dynamic_slice(cross, (0, 64 * z, 128 * y), (4, 64, 128))
    known = known.astype(F32).reshape(2, 128, 128)
    first_rhs = (known[0] - over_sites(first)).astype(BF)
    first_rhs, second = lax.optimization_barrier((first_rhs, second))
    rest = known[1] - over_sites(second)
    solved_first = over_z(stage(order, targets, over_cores(first_rhs), panels, 0)).astype(BF)
    pair, rest = lax.optimization_barrier((over_cores(solved_first), rest))
    every_first = all_sites(solved_first)
    parts = stage(order, targets, pair, panels, 1)
    second_rhs = (rest - over_z(parts)).astype(BF)
    *parts, every_first = lax.optimization_barrier(
        (*stage(order, targets, over_cores(second_rhs), panels, 2), every_first)
    )
    solved_second = over_z(parts).astype(BF)
    every_second = all_sites(solved_second)
    outer = outer_part(every_first, col) + outer_part(every_second, col)
    pred_cov = prior_cov - row_sum(outer) / S
    return jnp.concatenate([every_first, every_second]), pred_cov


def solution(mesh):
    placed = (
        P(None, "row", None, "col"),
        P("row", "col", None),
        P(None, "row", None),
        P(None, None, "row", None, "col"),
        P(None, "row", None, "col"),
        P("col", None),
    )
    return jax.shard_map(
        body,
        mesh=mesh,
        in_specs=placed,
        out_specs=(P(None, "row", None), P("col", None)),
        check_vma=False,
    )
```

```python
import jax
import jax.numpy as jnp
from jax import lax
from jax.experimental import pallas as pl
from jax.experimental.pallas import tpu as pltpu
from jax.sharding import PartitionSpec as P

S = 8192
BF = jnp.bfloat16
F32 = jnp.float32
VMEM = pltpu.VMEM
ROOMY = pltpu.CompilerParams(vmem_limit_bytes=20 << 20)


def x_shift(v, step):
    return lax.ppermute(v, "row", [(r, (r + 2 * step) % 8) for r in range(8)])


def other_core(v):
    return lax.ppermute(v, "row", [(r, r ^ 1) for r in range(8)])


def z_exchange(v):
    groups = [[4 * y + z for z in range(4)] for y in range(4)]
    return lax.all_to_all(v, "col", 0, 0, axis_index_groups=groups, tiled=True)


def y_gather(v):
    groups = [[4 * y + z for y in range(4)] for z in range(4)]
    sent = jnp.broadcast_to(v[None], (4, *v.shape))
    gathered = lax.all_to_all(sent, "col", 0, 0, axis_index_groups=groups, tiled=True)
    return gathered.reshape(16, *v.shape[1:])


def z_shift(v, step):
    return lax.ppermute(v, "col", [(c, c // 4 * 4 + (c + step) % 4) for c in range(16)])


def whole(array):
    rank = len(array.shape)
    return pl.BlockSpec(array.shape, lambda i, *_: (0,) * rank)


def cost(flops, moved):
    return pl.CostEstimate(flops=flops, bytes_accessed=moved, transcendentals=0)


def in_hbm(array):
    return pltpu.with_memory_space_constraint(array, pltpu.HBM)


def prepare_kernel(first, second, linking, lines):
    for m, source in enumerate((first, linking, second)):
        turned = jnp.transpose(source[...].astype(F32)).astype(BF)
        for q in range(4):
            lines[q, m] = turned[64 * q : 64 * (q + 1), :]


def prepare(inverses, coupling):
    inverses = in_hbm(inverses.reshape(2, 512, 256))
    coupling = in_hbm(coupling.reshape(512, 256))
    out = jax.ShapeDtypeStruct((4, 3, 64, 512), BF)
    return pl.pallas_call(
        prepare_kernel,
        grid=(1,),
        in_specs=[
            pl.BlockSpec((None, 512, 256), lambda i: (0, 0, 0)),
            pl.BlockSpec((None, 512, 256), lambda i: (1, 0, 0)),
            whole(coupling),
        ],
        out_specs=whole(out),
        out_shape=out,
        compiler_params=ROOMY,
    )(inverses, inverses, coupling)


def split_tiles_kernel(src, token, dst):
    del token
    tiles = pltpu.einshape("tbu->btu", src[0])
    for b in range(tiles.shape[0]):
        dst[b // 3, :, 256 * (b % 3) : 256 * (b % 3 + 1)] = tiles[b]


def split_tiles(left, half, token):
    _, tile, count, width = left.shape
    return pl.pallas_call(
        split_tiles_kernel,
        grid=(2,),
        in_specs=[
            pl.BlockSpec((1, tile, count, width), lambda a: (2 * half + a, 0, 0, 0)),
            pl.BlockSpec(memory_space=pltpu.HBM),
        ],
        out_specs=pl.BlockSpec((count // 3, tile, 3 * width), lambda a: (0, a, 0)),
        out_shape=pltpu.HBM((count // 3, 2 * tile, 3 * width), BF),
        cost_estimate=cost(0, left.size * 2),
        compiler_params=ROOMY,
    )(left, token)


def accumulate(acc, halves, held, step):
    values = held[...].reshape(768, 512)
    for half, left in enumerate(halves):
        here = slice(512 * half, 512 * (half + 1))
        total = jnp.dot(left[...], values, preferred_element_type=F32)

        @pl.when(step == 0)
        def _():
            acc[here, :] = total

        @pl.when(step > 0)
        def _():
            acc[here, :] += total


def take_pieces(step, pieces, held):
    half = held.shape[1] // 2
    for j in range(len(pieces) // 2):

        @pl.when(step == j)
        def _():
            held[:, :half, :] = pieces[2 * j][...]
            held[:, half:, :] = pieces[2 * j + 1][...]


def first_products_kernel(order, upper, lower, *refs):
    del order
    *pieces, acc, held = refs
    step = pl.program_id(0)
    take_pieces(step, pieces, held)
    accumulate(acc, (upper, lower), held, step)


def next_products_kernel(order, upper, lower, before, token, *refs):
    del order, token
    *pieces, acc, held = refs
    step = pl.program_id(0)

    @pl.when(step == 0)
    def _():
        acc[...] = before[...]

    take_pieces(step, pieces, held)
    accumulate(acc, (upper, lower), held, step + 1)


def last_products_kernel(order, upper, lower, before, token, *refs):
    *pieces, first, second, acc, held = refs
    next_products_kernel(order, upper, lower, before, token, *pieces, acc, held)

    @pl.when(pl.program_id(0) == pl.num_programs(0) - 1)
    def _():
        for out, base in ((first, 0), (second, 512)):
            for y in range(4):
                for z in range(4):
                    for a in range(2):
                        top = base + 256 * a + 64 * z
                        block = acc[top : top + 64, 128 * y : 128 * (y + 1)]
                        out[4 * y + z, 64 * a : 64 * (a + 1), :] = block.astype(BF)


def piece_specs(pieces):
    specs = []
    for array, place in pieces:
        specs.append(pl.BlockSpec((3, 128, 512), lambda i, *_, place=place: (0, place, 0)))
    return specs


def products(order, left, pieces, before=None, token=None, last=False):
    blocks = len(pieces) // 2
    rows = 1024
    left_spec = pl.BlockSpec((None, 512, 768), lambda i, order: (order[i], 0, 0))
    left = [in_hbm(half) for half in left]
    arrays = [array for array, _ in pieces]
    scratch = [VMEM((3, 256, 512), BF)]
    flops = blocks * 2 * rows * 768 * 512
    moved = blocks * 2 * 768 * (rows + 512) + rows * 512 * 4
    starts = [] if before is None else [before, token]
    out = jax.ShapeDtypeStruct((rows, 512), F32)
    kernel = first_products_kernel if before is None else next_products_kernel
    if last:
        out = [jax.ShapeDtypeStruct((16, 128, 128), BF)] * 2
        kernel = last_products_kernel
        scratch = [VMEM((rows, 512), F32), *scratch]
    return pl.pallas_call(
        kernel,
        grid_spec=pltpu.PrefetchScalarGridSpec(
            num_scalar_prefetch=1,
            grid=(blocks,),
            in_specs=[left_spec, left_spec, *map(whole, starts), *piece_specs(pieces)],
            out_specs=jax.tree.map(whole, out),
            scratch_shapes=scratch,
        ),
        out_shape=out,
        cost_estimate=cost(flops, moved),
        compiler_params=ROOMY,
    )(order, *left, *starts, *arrays)


RELATIVE = (0, -1, 1, 2)


def stage_kernel(order, targets, own, one, two, three, weights, *refs):
    *parts, held, result = refs
    for i, source in enumerate((own, one, two, three)):
        for k in range(2):
            line = order[2 * i + k]
            held[line] = source[k, :64, :]
            held[8 + line] = source[k, 64:, :]
    values = held[...].reshape(1024, 128).astype(F32)
    values = jnp.transpose(values).astype(BF)
    factor = weights[...].reshape(1024, 512)
    total = jnp.dot(values, factor, preferred_element_type=F32)
    result[...] = jnp.transpose(total)
    for d, part in enumerate(parts):
        for a in range(2):
            top = pl.multiple_of(256 * a + 64 * targets[d], 64)
            part[64 * a : 64 * (a + 1), :] = result[pl.ds(top, 64), :].astype(BF)


def over_cores(values):
    return jnp.stack([values, other_core(values)])


def over_chips(pair):
    return [pair, x_shift(pair, 1), x_shift(pair, -1), x_shift(pair, 2)]


SCALARS = pl.BlockSpec(memory_space=pltpu.SMEM)


def stage(order, targets, pair, panels, which):
    moved = over_chips(pair)
    out = [jax.ShapeDtypeStruct((128, 128), BF)] * 4
    return pl.pallas_call(
        stage_kernel,
        grid=(1,),
        in_specs=[
            SCALARS,
            SCALARS,
            *map(whole, moved),
            pl.BlockSpec((16, None, 64, 512), lambda i: (0, which, 0, 0)),
        ],
        out_specs=list(map(whole, out)),
        scratch_shapes=[VMEM((16, 64, 128), BF), VMEM((512, 128), F32)],
        out_shape=out,
        cost_estimate=cost(2 * 128 * 1024 * 512, 2 * 1024 * 512),
        compiler_params=ROOMY,
    )(order, targets, *moved, panels)


def over_z(parts):
    moved = [z_shift(part, d) if d else part for d, part in enumerate(parts)]
    return sum(part.astype(F32) for part in moved)


def over_sites(partial):
    return lax.all_to_all(partial, "col", 0, 0, tiled=True).astype(F32).sum(axis=0)


def all_sites(values):
    sent = jnp.broadcast_to(values[None], (16, 128, 128))
    every = lax.all_to_all(sent, "col", 0, 0, tiled=True).reshape(4, 4, 2, 64, 128)
    return jnp.transpose(every, (2, 1, 3, 0, 4)).reshape(2, 256, 512)


def row_sum(values):
    values = values + other_core(values)
    return values + x_shift(values, 1) + x_shift(values, -1) + x_shift(values, 2)


def outer_part(every, col):
    own = lax.dynamic_slice_in_dim(every, 32 * col, 32, 2)
    return jnp.einsum("atm,atn->mn", own, every, preferred_element_type=F32)


def body(left_factor, prev_solution, cross, inverses, coupling, prior_cov):
    row, col = lax.axis_index("row"), lax.axis_index("col")
    x, k = row // 2, row % 2
    y, z = col // 4, col % 4
    order = jnp.stack([(x + d) % 4 * 2 + (k + e) % 2 for d in RELATIVE for e in range(2)])
    order = order.astype(jnp.int32)
    targets = jnp.stack([(z + d) % 4 for d in range(4)]).astype(jnp.int32)

    lines = prepare(inverses, coupling)
    before, after = x_shift(prev_solution, 1), x_shift(prev_solution, -1)
    sibling = other_core(prev_solution)
    tiles = in_hbm(left_factor)
    upper = split_tiles(tiles, 0, in_hbm(lines))
    lines, upper = lax.optimization_barrier((z_exchange(lines), upper))
    lower = split_tiles(tiles, 1, in_hbm(upper))
    before, after, sibling, upper, lower = lax.optimization_barrier(
        (before, after, sibling, upper, lower)
    )
    left = (upper, lower)
    panels = in_hbm(y_gather(lines))
    far_low, far_high = x_shift(before[:, :128, :], 1), x_shift(after[:, 128:, :], -1)
    halves = lambda v: [(in_hbm(v), 0), (in_hbm(v), 1)]
    pieces = halves(prev_solution) + halves(sibling)
    for block in (before, after):
        pieces += halves(block) + halves(other_core(block))
    started = products(order[:6], left, pieces)
    far_low, far_high, token = lax.optimization_barrier(
        (far_low, far_high, started[:8, :128])
    )
    far = (far_low, far_high)
    pieces = [(v, 0) for v in far] + [(other_core(v), 0) for v in far]
    first, second = products(order[6:], left, pieces, started, token, last=True)

    first, second, panels = lax.optimization_barrier((first, second, panels))
    panels = in_hbm(panels)
    known = lax.dynamic_slice(cross, (0, 64 * z, 128 * y), (4, 64, 128))
    known = known.astype(F32).reshape(2, 128, 128)
    first_rhs = (known[0] - over_sites(first)).astype(BF)
    first_rhs, second = lax.optimization_barrier((first_rhs, second))
    rest = known[1] - over_sites(second)
    solved_first = over_z(stage(order, targets, over_cores(first_rhs), panels, 0)).astype(BF)
    pair, rest = lax.optimization_barrier((over_cores(solved_first), rest))
    every_first = all_sites(solved_first)
    parts = stage(order, targets, pair, panels, 1)
    second_rhs = (rest - over_z(parts)).astype(BF)
    *parts, every_first = lax.optimization_barrier(
        (*stage(order, targets, over_cores(second_rhs), panels, 2), every_first)
    )
    solved_second = over_z(parts).astype(BF)
    every_second = all_sites(solved_second)
    outer = outer_part(every_first, col) + outer_part(every_second, col)
    pred_cov = prior_cov - row_sum(outer) / S
    return jnp.concatenate([every_first, every_second]), pred_cov


def solution(mesh):
    placed = (
        P(None, "row", None, "col"),
        P("row", "col", None),
        P(None, "row", None),
        P(None, None, "row", None, "col"),
        P(None, "row", None, "col"),
        P("col", None),
    )
    return jax.shard_map(
        body,
        mesh=mesh,
        in_specs=placed,
        out_specs=(P(None, "row", None), P("col", None)),
        check_vma=False,
    )
```

```python
import jax
import jax.numpy as jnp
from jax import lax
from jax.experimental import pallas as pl
from jax.experimental.pallas import tpu as pltpu
from jax.sharding import PartitionSpec as P

S = 8192
BF = jnp.bfloat16
F32 = jnp.float32
VMEM = pltpu.VMEM
ROOMY = pltpu.CompilerParams(vmem_limit_bytes=20 << 20)


def x_shift(v, step):
    return lax.ppermute(v, "row", [(r, (r + 2 * step) % 8) for r in range(8)])


def other_core(v):
    return lax.ppermute(v, "row", [(r, r ^ 1) for r in range(8)])


def z_exchange(v):
    groups = [[4 * y + z for z in range(4)] for y in range(4)]
    return lax.all_to_all(v, "col", 0, 0, axis_index_groups=groups, tiled=True)


def y_gather(v):
    groups = [[4 * y + z for y in range(4)] for z in range(4)]
    sent = jnp.broadcast_to(v[None], (4, *v.shape))
    gathered = lax.all_to_all(sent, "col", 0, 0, axis_index_groups=groups, tiled=True)
    return gathered.reshape(16, *v.shape[1:])


def z_shift(v, step):
    return lax.ppermute(v, "col", [(c, c // 4 * 4 + (c + step) % 4) for c in range(16)])


def whole(array):
    rank = len(array.shape)
    return pl.BlockSpec(array.shape, lambda i, *_: (0,) * rank)


def cost(flops, moved):
    return pl.CostEstimate(flops=flops, bytes_accessed=moved, transcendentals=0)


def in_hbm(array):
    return pltpu.with_memory_space_constraint(array, pltpu.HBM)


def prepare_kernel(first, second, linking, lines):
    for m, source in enumerate((first, linking, second)):
        turned = jnp.transpose(source[...].astype(F32)).astype(BF)
        for q in range(4):
            lines[q, m] = turned[64 * q : 64 * (q + 1), :]


def prepare(inverses, coupling):
    inverses = in_hbm(inverses.reshape(2, 512, 256))
    coupling = in_hbm(coupling.reshape(512, 256))
    out = jax.ShapeDtypeStruct((4, 3, 64, 512), BF)
    return pl.pallas_call(
        prepare_kernel,
        grid=(1,),
        in_specs=[
            pl.BlockSpec((None, 512, 256), lambda i: (0, 0, 0)),
            pl.BlockSpec((None, 512, 256), lambda i: (1, 0, 0)),
            whole(coupling),
        ],
        out_specs=whole(out),
        out_shape=out,
        compiler_params=ROOMY,
    )(inverses, inverses, coupling)


def split_tiles_kernel(src, token, dst):
    del token
    tiles = pltpu.einshape("tbu->btu", src[0])
    for b in range(tiles.shape[0]):
        dst[b // 3, :, 256 * (b % 3) : 256 * (b % 3 + 1)] = tiles[b]


def split_tiles(left, half, token):
    _, tile, count, width = left.shape
    return pl.pallas_call(
        split_tiles_kernel,
        grid=(2,),
        in_specs=[
            pl.BlockSpec((1, tile, count, width), lambda a: (2 * half + a, 0, 0, 0)),
            pl.BlockSpec(memory_space=pltpu.HBM),
        ],
        out_specs=pl.BlockSpec((count // 3, tile, 3 * width), lambda a: (0, a, 0)),
        out_shape=pltpu.HBM((count // 3, 2 * tile, 3 * width), BF),
        cost_estimate=cost(0, left.size * 2),
        compiler_params=ROOMY,
    )(left, token)


def accumulate(acc, halves, held, step):
    values = held[...].reshape(768, 512)
    for half, left in enumerate(halves):
        here = slice(512 * half, 512 * (half + 1))
        total = jnp.dot(left[...], values, preferred_element_type=F32)

        @pl.when(step == 0)
        def _():
            acc[here, :] = total

        @pl.when(step > 0)
        def _():
            acc[here, :] += total


def take_pieces(step, pieces, held):
    half = held.shape[1] // 2
    for j in range(len(pieces) // 2):

        @pl.when(step == j)
        def _():
            held[:, :half, :] = pieces[2 * j][...]
            held[:, half:, :] = pieces[2 * j + 1][...]


def first_products_kernel(order, upper, lower, *refs):
    del order
    *pieces, acc, held = refs
    step = pl.program_id(0)
    take_pieces(step, pieces, held)
    accumulate(acc, (upper, lower), held, step)


def next_products_kernel(order, upper, lower, before, token, *refs):
    del order, token
    *pieces, acc, held = refs
    step = pl.program_id(0)

    @pl.when(step == 0)
    def _():
        acc[...] = before[...]

    take_pieces(step, pieces, held)
    accumulate(acc, (upper, lower), held, step + 1)


def last_products_kernel(order, upper, lower, before, token, *refs):
    *pieces, first, second, acc, held = refs
    next_products_kernel(order, upper, lower, before, token, *pieces, acc, held)

    @pl.when(pl.program_id(0) == pl.num_programs(0) - 1)
    def _():
        for out, base in ((first, 0), (second, 512)):
            for y in range(4):
                for z in range(4):
                    for a in range(2):
                        top = base + 256 * a + 64 * z
                        block = acc[top : top + 64, 128 * y : 128 * (y + 1)]
                        out[4 * y + z, 64 * a : 64 * (a + 1), :] = block.astype(BF)


def piece_specs(pieces):
    specs = []
    for array, place in pieces:
        specs.append(pl.BlockSpec((3, 128, 512), lambda i, *_, place=place: (0, place, 0)))
    return specs


def products(order, left, pieces, before=None, token=None, last=False):
    blocks = len(pieces) // 2
    rows = 1024
    left_spec = pl.BlockSpec((None, 512, 768), lambda i, order: (order[i], 0, 0))
    left = [in_hbm(half) for half in left]
    arrays = [array for array, _ in pieces]
    scratch = [VMEM((3, 256, 512), BF)]
    flops = blocks * 2 * rows * 768 * 512
    moved = blocks * 2 * 768 * (rows + 512) + rows * 512 * 4
    starts = [] if before is None else [before, token]
    out = jax.ShapeDtypeStruct((rows, 512), F32)
    kernel = first_products_kernel if before is None else next_products_kernel
    if last:
        out = [jax.ShapeDtypeStruct((16, 128, 128), BF)] * 2
        kernel = last_products_kernel
        scratch = [VMEM((rows, 512), F32), *scratch]
    return pl.pallas_call(
        kernel,
        grid_spec=pltpu.PrefetchScalarGridSpec(
            num_scalar_prefetch=1,
            grid=(blocks,),
            in_specs=[left_spec, left_spec, *map(whole, starts), *piece_specs(pieces)],
            out_specs=jax.tree.map(whole, out),
            scratch_shapes=scratch,
        ),
        out_shape=out,
        cost_estimate=cost(flops, moved),
        compiler_params=ROOMY,
    )(order, *left, *starts, *arrays)


RELATIVE = (0, -1, 1, 2)


def stage_kernel(order, targets, own, one, two, three, weights, *refs):
    *parts, held, result = refs
    for i, source in enumerate((own, one, two, three)):
        for k in range(2):
            line = order[2 * i + k]
            held[line] = source[k, :64, :]
            held[8 + line] = source[k, 64:, :]
    values = held[...].reshape(1024, 128).astype(F32)
    values = jnp.transpose(values).astype(BF)
    factor = weights[...].reshape(1024, 512)
    total = jnp.dot(values, factor, preferred_element_type=F32)
    result[...] = jnp.transpose(total)
    for d, part in enumerate(parts):
        for a in range(2):
            top = pl.multiple_of(256 * a + 64 * targets[d], 64)
            part[64 * a : 64 * (a + 1), :] = result[pl.ds(top, 64), :].astype(BF)


def over_cores(values):
    return jnp.stack([values, other_core(values)])


def over_chips(pair):
    return [pair, x_shift(pair, 1), x_shift(pair, -1), x_shift(pair, 2)]


SCALARS = pl.BlockSpec(memory_space=pltpu.SMEM)


def stage(order, targets, pair, panels, which):
    moved = over_chips(pair)
    out = [jax.ShapeDtypeStruct((128, 128), BF)] * 4
    return pl.pallas_call(
        stage_kernel,
        grid=(1,),
        in_specs=[
            SCALARS,
            SCALARS,
            *map(whole, moved),
            pl.BlockSpec((16, None, 64, 512), lambda i: (0, which, 0, 0)),
        ],
        out_specs=list(map(whole, out)),
        scratch_shapes=[VMEM((16, 64, 128), BF), VMEM((512, 128), F32)],
        out_shape=out,
        cost_estimate=cost(2 * 128 * 1024 * 512, 2 * 1024 * 512),
        compiler_params=ROOMY,
    )(order, targets, *moved, panels)


def over_z(parts):
    moved = [z_shift(part, d) if d else part for d, part in enumerate(parts)]
    return sum(part.astype(F32) for part in moved)


def over_sites(partial):
    return lax.all_to_all(partial, "col", 0, 0, tiled=True).astype(F32).sum(axis=0)


def all_sites(values):
    sent = jnp.broadcast_to(values[None], (16, 128, 128))
    every = lax.all_to_all(sent, "col", 0, 0, tiled=True).reshape(4, 4, 2, 64, 128)
    return jnp.transpose(every, (2, 1, 3, 0, 4)).reshape(2, 256, 512)


def row_sum(values):
    values = values + other_core(values)
    return values + x_shift(values, 1) + x_shift(values, -1) + x_shift(values, 2)


def outer_part(every, col):
    own = lax.dynamic_slice_in_dim(every, 32 * col, 32, 2)
    return jnp.einsum("atm,atn->mn", own, every, preferred_element_type=F32)


def body(left_factor, prev_solution, cross, inverses, coupling, prior_cov):
    row, col = lax.axis_index("row"), lax.axis_index("col")
    x, k = row // 2, row % 2
    y, z = col // 4, col % 4
    order = jnp.stack([(x + d) % 4 * 2 + (k + e) % 2 for d in RELATIVE for e in range(2)])
    order = order.astype(jnp.int32)
    targets = jnp.stack([(z + d) % 4 for d in range(4)]).astype(jnp.int32)

    lines = prepare(inverses, coupling)
    before, after = x_shift(prev_solution, 1), x_shift(prev_solution, -1)
    sibling = other_core(prev_solution)
    tiles = in_hbm(left_factor)
    upper = split_tiles(tiles, 0, in_hbm(lines))
    lines, upper = lax.optimization_barrier((z_exchange(lines), upper))
    lower = split_tiles(tiles, 1, in_hbm(upper))
    before, after, sibling, upper, lower = lax.optimization_barrier(
        (before, after, sibling, upper, lower)
    )
    left = (upper, lower)
    panels, late = in_hbm(y_gather(lines[:, :2])), lines[:, 2:]
    far_low, far_high = x_shift(before[:, :128, :], 1), x_shift(after[:, 128:, :], -1)
    halves = lambda v: [(in_hbm(v), 0), (in_hbm(v), 1)]
    pieces = halves(prev_solution) + halves(sibling)
    for block in (before, after):
        pieces += halves(block) + halves(other_core(block))
    started = products(order[:6], left, pieces)
    far_low, far_high, token, panels = lax.optimization_barrier(
        (far_low, far_high, started[:8, :128], panels)
    )
    far = (far_low, far_high)
    pieces = [(v, 0) for v in far] + [(other_core(v), 0) for v in far]
    first, second = products(order[6:], left, pieces, started, token, last=True)

    first, second, late = lax.optimization_barrier((first, second, late))
    panels = in_hbm(panels)
    known = lax.dynamic_slice(cross, (0, 64 * z, 128 * y), (4, 64, 128))
    known = known.astype(F32).reshape(2, 128, 128)
    first_rhs = (known[0] - over_sites(first)).astype(BF)
    first_rhs, second = lax.optimization_barrier((first_rhs, second))
    rest = known[1] - over_sites(second)
    solved_first = over_z(stage(order, targets, over_cores(first_rhs), panels, 0)).astype(BF)
    pair, rest = lax.optimization_barrier((over_cores(solved_first), rest))
    sent, late = lax.optimization_barrier((solved_first, late))
    late = in_hbm(y_gather(late))
    parts = stage(order, targets, pair, panels, 1)
    second_rhs = (rest - over_z(parts)).astype(BF)
    pair, late = lax.optimization_barrier((over_cores(second_rhs), late))
    every_first = all_sites(sent)
    parts = stage(order, targets, pair, in_hbm(late), 0)
    solved_second = over_z(parts).astype(BF)
    solved_second, every_first = lax.optimization_barrier((solved_second, every_first))
    every_second = all_sites(solved_second)
    outer = outer_part(every_first, col) + outer_part(every_second, col)
    pred_cov = prior_cov - row_sum(outer) / S
    return jnp.concatenate([every_first, every_second]), pred_cov


def solution(mesh):
    placed = (
        P(None, "row", None, "col"),
        P("row", "col", None),
        P(None, "row", None),
        P(None, None, "row", None, "col"),
        P(None, "row", None, "col"),
        P("col", None),
    )
    return jax.shard_map(
        body,
        mesh=mesh,
        in_specs=placed,
        out_specs=(P(None, "row", None), P("col", None)),
        check_vma=False,
    )
```

```python
import jax
import jax.numpy as jnp
from jax import lax
from jax.experimental import pallas as pl
from jax.experimental.pallas import tpu as pltpu
from jax.sharding import PartitionSpec as P

S = 8192
BF = jnp.bfloat16
F32 = jnp.float32
VMEM = pltpu.VMEM
ROOMY = pltpu.CompilerParams(vmem_limit_bytes=20 << 20)


def x_shift(v, step):
    return lax.ppermute(v, "row", [(r, (r + 2 * step) % 8) for r in range(8)])


def other_core(v):
    return lax.ppermute(v, "row", [(r, r ^ 1) for r in range(8)])


def z_exchange(v):
    groups = [[4 * y + z for z in range(4)] for y in range(4)]
    return lax.all_to_all(v, "col", 0, 0, axis_index_groups=groups, tiled=True)


def y_gather(v):
    groups = [[4 * y + z for y in range(4)] for z in range(4)]
    sent = jnp.broadcast_to(v[None], (4, *v.shape))
    gathered = lax.all_to_all(sent, "col", 0, 0, axis_index_groups=groups, tiled=True)
    return gathered.reshape(16, *v.shape[1:])


def z_shift(v, step):
    return lax.ppermute(v, "col", [(c, c // 4 * 4 + (c + step) % 4) for c in range(16)])


def whole(array):
    rank = len(array.shape)
    return pl.BlockSpec(array.shape, lambda i, *_: (0,) * rank)


def cost(flops, moved):
    return pl.CostEstimate(flops=flops, bytes_accessed=moved, transcendentals=0)


def in_hbm(array):
    return pltpu.with_memory_space_constraint(array, pltpu.HBM)


def prepare_kernel(first, second, linking, lines):
    for m, source in enumerate((first, linking, second)):
        turned = jnp.transpose(source[...].astype(F32)).astype(BF)
        for q in range(4):
            lines[q, m] = turned[64 * q : 64 * (q + 1), :]


def prepare(inverses, coupling):
    inverses = in_hbm(inverses.reshape(2, 512, 256))
    coupling = in_hbm(coupling.reshape(512, 256))
    out = jax.ShapeDtypeStruct((4, 3, 64, 512), BF)
    return pl.pallas_call(
        prepare_kernel,
        grid=(1,),
        in_specs=[
            pl.BlockSpec((None, 512, 256), lambda i: (0, 0, 0)),
            pl.BlockSpec((None, 512, 256), lambda i: (1, 0, 0)),
            whole(coupling),
        ],
        out_specs=whole(out),
        out_shape=out,
        compiler_params=ROOMY,
    )(inverses, inverses, coupling)


def split_tiles_kernel(src, token, dst):
    del token
    tiles = pltpu.einshape("tbu->btu", src[0])
    for b in range(tiles.shape[0]):
        dst[b // 3, :, 256 * (b % 3) : 256 * (b % 3 + 1)] = tiles[b]


def split_tiles(left, half, token):
    _, tile, count, width = left.shape
    return pl.pallas_call(
        split_tiles_kernel,
        grid=(2,),
        in_specs=[
            pl.BlockSpec((1, tile, count, width), lambda a: (2 * half + a, 0, 0, 0)),
            pl.BlockSpec(memory_space=pltpu.HBM),
        ],
        out_specs=pl.BlockSpec((count // 3, tile, 3 * width), lambda a: (0, a, 0)),
        out_shape=pltpu.HBM((count // 3, 2 * tile, 3 * width), BF),
        cost_estimate=cost(0, left.size * 2),
        compiler_params=ROOMY,
    )(left, token)


def accumulate(acc, halves, held, step):
    values = held[...].reshape(768, 512)
    for half, left in enumerate(halves):
        here = slice(512 * half, 512 * (half + 1))
        total = jnp.dot(left[...], values, preferred_element_type=F32)

        @pl.when(step == 0)
        def _():
            acc[here, :] = total

        @pl.when(step > 0)
        def _():
            acc[here, :] += total


def take_pieces(step, pieces, held):
    half = held.shape[1] // 2
    for j in range(len(pieces) // 2):

        @pl.when(step == j)
        def _():
            held[:, :half, :] = pieces[2 * j][...]
            held[:, half:, :] = pieces[2 * j + 1][...]


def first_products_kernel(order, upper, lower, *refs):
    del order
    *pieces, acc, held = refs
    step = pl.program_id(0)
    take_pieces(step, pieces, held)
    accumulate(acc, (upper, lower), held, step)


def next_products_kernel(order, upper, lower, before, token, *refs):
    del order, token
    *pieces, acc, held = refs
    step = pl.program_id(0)

    @pl.when(step == 0)
    def _():
        acc[...] = before[...]

    take_pieces(step, pieces, held)
    accumulate(acc, (upper, lower), held, step + 1)


def last_products_kernel(order, upper, lower, before, token, *refs):
    *pieces, first, second, acc, held = refs
    next_products_kernel(order, upper, lower, before, token, *pieces, acc, held)

    @pl.when(pl.program_id(0) == pl.num_programs(0) - 1)
    def _():
        for out, base in ((first, 0), (second, 512)):
            for y in range(4):
                for z in range(4):
                    for a in range(2):
                        top = base + 256 * a + 64 * z
                        block = acc[top : top + 64, 128 * y : 128 * (y + 1)]
                        out[4 * y + z, 64 * a : 64 * (a + 1), :] = block.astype(BF)


def piece_specs(pieces):
    specs = []
    for array, place in pieces:
        specs.append(pl.BlockSpec((3, 128, 512), lambda i, *_, place=place: (0, place, 0)))
    return specs


def products(order, left, pieces, before=None, token=None, last=False):
    blocks = len(pieces) // 2
    rows = 1024
    left_spec = pl.BlockSpec((None, 512, 768), lambda i, order: (order[i], 0, 0))
    left = [in_hbm(half) for half in left]
    arrays = [array for array, _ in pieces]
    scratch = [VMEM((3, 256, 512), BF)]
    flops = blocks * 2 * rows * 768 * 512
    moved = blocks * 2 * 768 * (rows + 512) + rows * 512 * 4
    starts = [] if before is None else [before, token]
    out = jax.ShapeDtypeStruct((rows, 512), F32)
    kernel = first_products_kernel if before is None else next_products_kernel
    if last:
        out = [jax.ShapeDtypeStruct((16, 128, 128), BF)] * 2
        kernel = last_products_kernel
        scratch = [VMEM((rows, 512), F32), *scratch]
    return pl.pallas_call(
        kernel,
        grid_spec=pltpu.PrefetchScalarGridSpec(
            num_scalar_prefetch=1,
            grid=(blocks,),
            in_specs=[left_spec, left_spec, *map(whole, starts), *piece_specs(pieces)],
            out_specs=jax.tree.map(whole, out),
            scratch_shapes=scratch,
        ),
        out_shape=out,
        cost_estimate=cost(flops, moved),
        compiler_params=ROOMY,
    )(order, *left, *starts, *arrays)


RELATIVE = (0, -1, 1, 2)


def stage_kernel(order, targets, own, one, two, three, weights, *refs):
    *parts, held, result = refs
    for i, source in enumerate((own, one, two, three)):
        for k in range(2):
            line = order[2 * i + k]
            held[line] = source[k, :64, :]
            held[8 + line] = source[k, 64:, :]
    values = held[...].reshape(1024, 128).astype(F32)
    values = jnp.transpose(values).astype(BF)
    factor = weights[...].reshape(1024, 512)
    total = jnp.dot(values, factor, preferred_element_type=F32)
    result[...] = jnp.transpose(total)
    for d, part in enumerate(parts):
        for a in range(2):
            top = pl.multiple_of(256 * a + 64 * targets[d], 64)
            part[64 * a : 64 * (a + 1), :] = result[pl.ds(top, 64), :].astype(BF)


def over_cores(values):
    return jnp.stack([values, other_core(values)])


def over_chips(pair):
    return [pair, x_shift(pair, 1), x_shift(pair, -1), x_shift(pair, 2)]


SCALARS = pl.BlockSpec(memory_space=pltpu.SMEM)


def stage(order, targets, pair, panels, which):
    moved = over_chips(pair)
    out = [jax.ShapeDtypeStruct((128, 128), BF)] * 4
    return pl.pallas_call(
        stage_kernel,
        grid=(1,),
        in_specs=[
            SCALARS,
            SCALARS,
            *map(whole, moved),
            pl.BlockSpec((16, None, 64, 512), lambda i: (0, which, 0, 0)),
        ],
        out_specs=list(map(whole, out)),
        scratch_shapes=[VMEM((16, 64, 128), BF), VMEM((512, 128), F32)],
        out_shape=out,
        cost_estimate=cost(2 * 128 * 1024 * 512, 2 * 1024 * 512),
        compiler_params=ROOMY,
    )(order, targets, *moved, panels)


def over_z(parts):
    moved = [z_shift(part, d) if d else part for d, part in enumerate(parts)]
    return sum(part.astype(F32) for part in moved)


def over_sites(partial):
    return lax.all_to_all(partial, "col", 0, 0, tiled=True).astype(F32).sum(axis=0)


def all_sites(values):
    sent = jnp.broadcast_to(values[None], (16, 128, 128))
    every = lax.all_to_all(sent, "col", 0, 0, tiled=True).reshape(4, 4, 2, 64, 128)
    return jnp.transpose(every, (2, 1, 3, 0, 4)).reshape(2, 256, 512)


def row_sum(values):
    values = values + other_core(values)
    return values + x_shift(values, 1) + x_shift(values, -1) + x_shift(values, 2)


def outer_part(every, col):
    own = lax.dynamic_slice_in_dim(every, 32 * col, 32, 2)
    return jnp.einsum("atm,atn->mn", own, every, preferred_element_type=F32)


def body(left_factor, prev_solution, cross, inverses, coupling, prior_cov):
    row, col = lax.axis_index("row"), lax.axis_index("col")
    x, k = row // 2, row % 2
    y, z = col // 4, col % 4
    order = jnp.stack([(x + d) % 4 * 2 + (k + e) % 2 for d in RELATIVE for e in range(2)])
    order = order.astype(jnp.int32)
    targets = jnp.stack([(z + d) % 4 for d in range(4)]).astype(jnp.int32)

    lines = prepare(inverses, coupling)
    before, after = x_shift(prev_solution, 1), x_shift(prev_solution, -1)
    sibling = other_core(prev_solution)
    tiles = in_hbm(left_factor)
    upper = split_tiles(tiles, 0, in_hbm(lines))
    lines, upper = lax.optimization_barrier((z_exchange(lines), upper))
    lower = split_tiles(tiles, 1, in_hbm(upper))
    before, after, sibling, upper, lower = lax.optimization_barrier(
        (before, after, sibling, upper, lower)
    )
    left = (upper, lower)
    panels = in_hbm(y_gather(lines))
    far_low, far_high = x_shift(before[:, :128, :], 1), x_shift(after[:, 128:, :], -1)
    halves = lambda v: [(in_hbm(v), 0), (in_hbm(v), 1)]
    pieces = halves(prev_solution) + halves(sibling)
    for block in (before, after):
        pieces += halves(block) + halves(other_core(block))
    started = products(order[:6], left, pieces)
    far_low, far_high, token = lax.optimization_barrier(
        (far_low, far_high, started[:8, :128])
    )
    far = (far_low, far_high)
    pieces = [(v, 0) for v in far] + [(other_core(v), 0) for v in far]
    first, second = products(order[6:], left, pieces, started, token, last=True)

    first, second, panels = lax.optimization_barrier((first, second, panels))
    panels = in_hbm(panels)
    known = lax.dynamic_slice(cross, (0, 64 * z, 128 * y), (4, 64, 128))
    known = known.astype(F32).reshape(2, 128, 128)
    first_rhs = (known[0] - over_sites(first)).astype(BF)
    first_rhs, second = lax.optimization_barrier((first_rhs, second))
    rest = known[1] - over_sites(second)
    solved_first = over_z(stage(order, targets, over_cores(first_rhs), panels, 0)).astype(BF)
    pair = over_cores(solved_first)
    every_first = all_sites(solved_first)
    parts = stage(order, targets, pair, panels, 1)
    second_rhs = (rest - over_z(parts)).astype(BF)
    *parts, every_first = lax.optimization_barrier(
        (*stage(order, targets, over_cores(second_rhs), panels, 2), every_first)
    )
    solved_second = over_z(parts).astype(BF)
    every_second = all_sites(solved_second)
    outer = outer_part(every_first, col) + outer_part(every_second, col)
    pred_cov = prior_cov - row_sum(outer) / S
    return jnp.concatenate([every_first, every_second]), pred_cov


def solution(mesh):
    placed = (
        P(None, "row", None, "col"),
        P("row", "col", None),
        P(None, "row", None),
        P(None, None, "row", None, "col"),
        P(None, "row", None, "col"),
        P("col", None),
    )
    return jax.shard_map(
        body,
        mesh=mesh,
        in_specs=placed,
        out_specs=(P(None, "row", None), P("col", None)),
        check_vma=False,
    )
```

```python
import jax
import jax.numpy as jnp
from jax import lax
from jax.experimental import pallas as pl
from jax.experimental.pallas import tpu as pltpu
from jax.sharding import PartitionSpec as P

S = 8192
BF = jnp.bfloat16
F32 = jnp.float32
VMEM = pltpu.VMEM
ROOMY = pltpu.CompilerParams(vmem_limit_bytes=20 << 20)


def x_shift(v, step):
    return lax.ppermute(v, "row", [(r, (r + 2 * step) % 8) for r in range(8)])


def other_core(v):
    return lax.ppermute(v, "row", [(r, r ^ 1) for r in range(8)])


def z_exchange(v):
    groups = [[4 * y + z for z in range(4)] for y in range(4)]
    return lax.all_to_all(v, "col", 0, 0, axis_index_groups=groups, tiled=True)


def y_gather(v):
    groups = [[4 * y + z for y in range(4)] for z in range(4)]
    sent = jnp.broadcast_to(v[None], (4, *v.shape))
    gathered = lax.all_to_all(sent, "col", 0, 0, axis_index_groups=groups, tiled=True)
    return gathered.reshape(16, *v.shape[1:])


def z_shift(v, step):
    return lax.ppermute(v, "col", [(c, c // 4 * 4 + (c + step) % 4) for c in range(16)])


def whole(array):
    rank = len(array.shape)
    return pl.BlockSpec(array.shape, lambda i, *_: (0,) * rank)


def cost(flops, moved):
    return pl.CostEstimate(flops=flops, bytes_accessed=moved, transcendentals=0)


def in_hbm(array):
    return pltpu.with_memory_space_constraint(array, pltpu.HBM)


def prepare_kernel(first, second, linking, lines):
    for m, source in enumerate((first, linking, second)):
        turned = jnp.transpose(source[...].astype(F32)).astype(BF)
        for q in range(4):
            lines[q, m] = turned[64 * q : 64 * (q + 1), :]


def prepare(inverses, coupling):
    inverses = in_hbm(inverses.reshape(2, 512, 256))
    coupling = in_hbm(coupling.reshape(512, 256))
    out = jax.ShapeDtypeStruct((4, 3, 64, 512), BF)
    return pl.pallas_call(
        prepare_kernel,
        grid=(1,),
        in_specs=[
            pl.BlockSpec((None, 512, 256), lambda i: (0, 0, 0)),
            pl.BlockSpec((None, 512, 256), lambda i: (1, 0, 0)),
            whole(coupling),
        ],
        out_specs=whole(out),
        out_shape=out,
        compiler_params=ROOMY,
    )(inverses, inverses, coupling)


def split_tiles_kernel(src, token, dst):
    del token
    tiles = pltpu.einshape("tbu->btu", src[0])
    for b in range(tiles.shape[0]):
        dst[b // 3, :, 256 * (b % 3) : 256 * (b % 3 + 1)] = tiles[b]


def split_tiles(left, half, token):
    _, tile, count, width = left.shape
    return pl.pallas_call(
        split_tiles_kernel,
        grid=(2,),
        in_specs=[
            pl.BlockSpec((1, tile, count, width), lambda a: (2 * half + a, 0, 0, 0)),
            pl.BlockSpec(memory_space=pltpu.HBM),
        ],
        out_specs=pl.BlockSpec((count // 3, tile, 3 * width), lambda a: (0, a, 0)),
        out_shape=pltpu.HBM((count // 3, 2 * tile, 3 * width), BF),
        cost_estimate=cost(0, left.size * 2),
        compiler_params=ROOMY,
    )(left, token)


def accumulate(acc, halves, held, step):
    values = held[...].reshape(768, 512)
    for half, left in enumerate(halves):
        here = slice(512 * half, 512 * (half + 1))
        total = jnp.dot(left[...], values, preferred_element_type=F32)

        @pl.when(step == 0)
        def _():
            acc[here, :] = total

        @pl.when(step > 0)
        def _():
            acc[here, :] += total


def take_pieces(step, pieces, held):
    half = held.shape[1] // 2
    for j in range(len(pieces) // 2):

        @pl.when(step == j)
        def _():
            held[:, :half, :] = pieces[2 * j][...]
            held[:, half:, :] = pieces[2 * j + 1][...]


def first_products_kernel(order, upper, lower, *refs):
    del order
    *pieces, acc, held = refs
    step = pl.program_id(0)
    take_pieces(step, pieces, held)
    accumulate(acc, (upper, lower), held, step)


def next_products_kernel(order, upper, lower, before, token, *refs):
    del order, token
    *pieces, acc, held = refs
    step = pl.program_id(0)

    @pl.when(step == 0)
    def _():
        acc[...] = before[...]

    take_pieces(step, pieces, held)
    accumulate(acc, (upper, lower), held, step + 1)


def last_products_kernel(order, upper, lower, before, token, *refs):
    *pieces, first, second, acc, held = refs
    next_products_kernel(order, upper, lower, before, token, *pieces, acc, held)

    @pl.when(pl.program_id(0) == pl.num_programs(0) - 1)
    def _():
        for out, base in ((first, 0), (second, 512)):
            for y in range(4):
                for z in range(4):
                    for a in range(2):
                        top = base + 256 * a + 64 * z
                        block = acc[top : top + 64, 128 * y : 128 * (y + 1)]
                        out[4 * y + z, 64 * a : 64 * (a + 1), :] = block.astype(BF)


def piece_specs(pieces):
    specs = []
    for array, place in pieces:
        specs.append(pl.BlockSpec((3, 128, 512), lambda i, *_, place=place: (0, place, 0)))
    return specs


def products(order, left, pieces, before=None, token=None, last=False):
    blocks = len(pieces) // 2
    rows = 1024
    left_spec = pl.BlockSpec((None, 512, 768), lambda i, order: (order[i], 0, 0))
    left = [in_hbm(half) for half in left]
    arrays = [array for array, _ in pieces]
    scratch = [VMEM((3, 256, 512), BF)]
    flops = blocks * 2 * rows * 768 * 512
    moved = blocks * 2 * 768 * (rows + 512) + rows * 512 * 4
    starts = [] if before is None else [before, token]
    out = jax.ShapeDtypeStruct((rows, 512), F32)
    kernel = first_products_kernel if before is None else next_products_kernel
    if last:
        out = [jax.ShapeDtypeStruct((16, 128, 128), BF)] * 2
        kernel = last_products_kernel
        scratch = [VMEM((rows, 512), F32), *scratch]
    return pl.pallas_call(
        kernel,
        grid_spec=pltpu.PrefetchScalarGridSpec(
            num_scalar_prefetch=1,
            grid=(blocks,),
            in_specs=[left_spec, left_spec, *map(whole, starts), *piece_specs(pieces)],
            out_specs=jax.tree.map(whole, out),
            scratch_shapes=scratch,
        ),
        out_shape=out,
        cost_estimate=cost(flops, moved),
        compiler_params=ROOMY,
    )(order, *left, *starts, *arrays)


RELATIVE = (0, -1, 1, 2)


def stage_kernel(order, targets, own, one, two, three, weights, *refs):
    *parts, held, result = refs
    for i, source in enumerate((own, one, two, three)):
        for k in range(2):
            line = order[2 * i + k]
            held[line] = source[k, :64, :]
            held[8 + line] = source[k, 64:, :]
    values = held[...].reshape(1024, 128).astype(F32)
    values = jnp.transpose(values).astype(BF)
    factor = weights[...].reshape(1024, 512)
    total = jnp.dot(values, factor, preferred_element_type=F32)
    result[...] = jnp.transpose(total)
    for d, part in enumerate(parts):
        for a in range(2):
            top = pl.multiple_of(256 * a + 64 * targets[d], 64)
            part[64 * a : 64 * (a + 1), :] = result[pl.ds(top, 64), :].astype(BF)


def over_cores(values):
    return jnp.stack([values, other_core(values)])


def over_chips(pair):
    return [pair, x_shift(pair, 1), x_shift(pair, -1), x_shift(pair, 2)]


SCALARS = pl.BlockSpec(memory_space=pltpu.SMEM)


def stage(order, targets, pair, panels, which):
    moved = over_chips(pair)
    out = [jax.ShapeDtypeStruct((128, 128), BF)] * 4
    return pl.pallas_call(
        stage_kernel,
        grid=(1,),
        in_specs=[
            SCALARS,
            SCALARS,
            *map(whole, moved),
            pl.BlockSpec((16, None, 64, 512), lambda i: (0, which, 0, 0)),
        ],
        out_specs=list(map(whole, out)),
        scratch_shapes=[VMEM((16, 64, 128), BF), VMEM((512, 128), F32)],
        out_shape=out,
        cost_estimate=cost(2 * 128 * 1024 * 512, 2 * 1024 * 512),
        compiler_params=ROOMY,
    )(order, targets, *moved, panels)


def over_z(parts):
    moved = [z_shift(part, d) if d else part for d, part in enumerate(parts)]
    return sum(part.astype(F32) for part in moved)


def over_sites(partial):
    return lax.all_to_all(partial, "col", 0, 0, tiled=True).astype(F32).sum(axis=0)


def all_sites(values):
    sent = jnp.broadcast_to(values[None], (16, 128, 128))
    every = lax.all_to_all(sent, "col", 0, 0, tiled=True).reshape(4, 4, 2, 64, 128)
    return jnp.transpose(every, (2, 1, 3, 0, 4)).reshape(2, 256, 512)


def row_sum(values):
    values = values + other_core(values)
    sent = values.astype(BF)
    return values + sum(x_shift(sent, d).astype(F32) for d in (1, -1, 2))


def outer_part(every, col):
    own = lax.dynamic_slice_in_dim(every, 32 * col, 32, 2)
    return jnp.einsum("atm,atn->mn", own, every, preferred_element_type=F32)


def body(left_factor, prev_solution, cross, inverses, coupling, prior_cov):
    row, col = lax.axis_index("row"), lax.axis_index("col")
    x, k = row // 2, row % 2
    y, z = col // 4, col % 4
    order = jnp.stack([(x + d) % 4 * 2 + (k + e) % 2 for d in RELATIVE for e in range(2)])
    order = order.astype(jnp.int32)
    targets = jnp.stack([(z + d) % 4 for d in range(4)]).astype(jnp.int32)

    lines = prepare(inverses, coupling)
    before, after = x_shift(prev_solution, 1), x_shift(prev_solution, -1)
    sibling = other_core(prev_solution)
    tiles = in_hbm(left_factor)
    upper = split_tiles(tiles, 0, in_hbm(lines))
    lines, upper = lax.optimization_barrier((z_exchange(lines), upper))
    lower = split_tiles(tiles, 1, in_hbm(upper))
    before, after, sibling, upper, lower = lax.optimization_barrier(
        (before, after, sibling, upper, lower)
    )
    left = (upper, lower)
    panels = in_hbm(y_gather(lines))
    far_low, far_high = x_shift(before[:, :128, :], 1), x_shift(after[:, 128:, :], -1)
    halves = lambda v: [(in_hbm(v), 0), (in_hbm(v), 1)]
    pieces = halves(prev_solution) + halves(sibling)
    for block in (before, after):
        pieces += halves(block) + halves(other_core(block))
    started = products(order[:6], left, pieces)
    far_low, far_high, token = lax.optimization_barrier(
        (far_low, far_high, started[:8, :128])
    )
    far = (far_low, far_high)
    pieces = [(v, 0) for v in far] + [(other_core(v), 0) for v in far]
    first, second = products(order[6:], left, pieces, started, token, last=True)

    first, second, panels = lax.optimization_barrier((first, second, panels))
    panels = in_hbm(panels)
    known = lax.dynamic_slice(cross, (0, 64 * z, 128 * y), (4, 64, 128))
    known = known.astype(F32).reshape(2, 128, 128)
    first_rhs = (known[0] - over_sites(first)).astype(BF)
    first_rhs, second = lax.optimization_barrier((first_rhs, second))
    rest = known[1] - over_sites(second)
    solved_first = over_z(stage(order, targets, over_cores(first_rhs), panels, 0)).astype(BF)
    pair = over_cores(solved_first)
    every_first = all_sites(solved_first)
    parts = stage(order, targets, pair, panels, 1)
    second_rhs = (rest - over_z(parts)).astype(BF)
    *parts, every_first = lax.optimization_barrier(
        (*stage(order, targets, over_cores(second_rhs), panels, 2), every_first)
    )
    solved_second = over_z(parts).astype(BF)
    every_second = all_sites(solved_second)
    outer = outer_part(every_first, col) + outer_part(every_second, col)
    pred_cov = prior_cov - row_sum(outer) / S
    return jnp.concatenate([every_first, every_second]), pred_cov


def solution(mesh):
    placed = (
        P(None, "row", None, "col"),
        P("row", "col", None),
        P(None, "row", None),
        P(None, None, "row", None, "col"),
        P(None, "row", None, "col"),
        P("col", None),
    )
    return jax.shard_map(
        body,
        mesh=mesh,
        in_specs=placed,
        out_specs=(P(None, "row", None), P("col", None)),
        check_vma=False,
    )
```
